32 devices in a mesh: seq: 8 (over z, core), state: 4 (over y, x).
Axes of the slice: x: 2, y: 2, z: 4, core: 2. Of those that a mesh axis runs over, the one named last changes fastest.
Arguments:
- tokens: bfloat16 [16384, 1024], P(('seq', 'state')), may hold values from -6 to 6
- lengths: int32 [8], P('seq'), may hold values from 1024 to 2048, as said below
- grad_out: bfloat16 [16384, 1024], P(('seq', 'state')), may hold values from -6 to 6
- norm_gain: float32 [1024], replicated, may hold values from 0.5 to 1.5
- in_weight: bfloat16 [1024, 4096], replicated, may hold values from -0.1875 to 0.1875
- conv_weight: float32 [4, 2048], replicated, may hold values from -2 to 2
- conv_bias: float32 [2048], replicated, may hold values from -0.5 to 0.5
- xproj_weight: bfloat16 [2048, 96], replicated, may hold values from -0.125 to 0.125
- dtproj_weight: bfloat16 [2048, 64], replicated, may hold values from -0.75 to 0.75
- dt_bias: float32 [2048], replicated, may hold values from -5 to -2
- a_log: float32 [16, 2048], P('state'), may hold values from -3 to 2.5
- d_skip: float32 [2048], replicated, may hold values from 0.5 to 1.5
- out_weight: bfloat16 [2048, 1024], replicated, may hold values from -0.25 to 0.25
Outputs:
- output: bfloat16 [16384, 1024], P(('seq', 'state'))
- grad_tokens: float32 [16384, 1024], P(('seq', 'state'))
- grad_norm_gain: float32 [1024], replicated
- grad_in_weight: float32 [1024, 4096], P('seq')
- grad_conv_weight: float32 [4, 2048], replicated
- grad_conv_bias: float32 [2048], replicated
- grad_xproj_weight: float32 [2048, 96], P('seq')
- grad_dtproj_weight: float32 [2048, 64], P('seq')
- grad_dt_bias: float32 [2048], replicated
- grad_a_log: float32 [16, 2048], P('state')
- grad_d_skip: float32 [2048], replicated
- grad_out_weight: float32 [2048, 1024], P('seq')
- dt_mean: float32 [2048], replicated
- dt_spread: float32 [2048], replicated
The draws below stay inside these ranges and needn't reach their ends.
Inputs may be any that keep to these rules, and one draw needn't show every extreme that they name: `lengths`: each slot of 2048 rows holds one sequence from its first row on, padding after it; in every draw one slot is full and one holds exactly half of 2048 tokens.
All inputs are finite; a program needn't handle non-finite values.
Results may differ from the reference program's by a relative error of at most 0.0034.
The reference program's roundings to bfloat16 on the way count: a program that leaves them out, or rounds other values in their place, can miss the bound.
Values may be sent and summed in bfloat16 or wider, within the bound.
No kernel may reach another device: no remote copies, remote signals or barrier semaphores. Data moves between devices by JAX's collectives and lax.ppermute only.
A program may use at most 832 MiB of HBM per device.

```python
import math
import jax
import jax.numpy as jnp
from jax import lax

D = 1024
E = 2048
DSTATE = 16
RANK = 64
CONV = 4
SLOT = 2048
TOKENS = 16384
SLOTS = 8
NPROJ = 96


def draw_lengths(key, part):
    first_key, second_key = jax.random.split(key)
    values = jax.random.randint(first_key, (SLOTS,), SLOT // 2, SLOT + 1)
    chosen = jax.random.permutation(second_key, SLOTS)
    values = values.at[chosen[0]].set(SLOT)
    values = values.at[chosen[1]].set(SLOT // 2)
    return values.astype(jnp.int32)


def shard_levels(key, extent, cuts, smallest, top_value):
    def one(dim, shards_of):
        heights = jax.random.uniform(jax.random.fold_in(jax.random.fold_in(key, 6), dim), (shards_of,), jnp.float32, smallest / len(cuts), top_value / len(cuts))
        return jnp.repeat(jnp.exp(heights), extent[dim] // shards_of).reshape((-1,) + (1,) * (len(extent) - dim - 1))

    level = one(*cuts[0])
    for cut in cuts[1:]:
        level = level * one(*cut)
    return level


def bell_draw(rng, dims, scale, reach, cuts=(), held_as=jnp.bfloat16):
    values = scale * jax.random.normal(rng, dims, jnp.float32)
    if cuts:
        values = values * shard_levels(rng, dims, cuts, -0.22, 0.18)
    return jnp.clip(values, -reach, reach).astype(held_as)


def setup_inputs(seed: int = 0) -> dict:
    streams_of = jax.random.split(jax.random.key(seed), 14)
    return {
        "tokens": bell_draw(streams_of[0], (TOKENS, D), 1.0, 6.0, ((0, 32),)),
        "lengths": draw_lengths(jax.random.fold_in(streams_of[13], 71), 0),
        "grad_out": bell_draw(streams_of[2], (TOKENS, D), 1.0, 6.0, ((0, 32),)),
        "norm_gain": jnp.clip(1.0 + 0.1 * jax.random.normal(streams_of[3], (D,), jnp.float32), 0.5, 1.5),
        "in_weight": bell_draw(streams_of[4], (D, 2 * E), D ** -0.5, 0.1875),
        "conv_weight": bell_draw(streams_of[5], (CONV, E), 0.5, 2.0, (), jnp.float32),
        "conv_bias": jnp.clip(jax.random.uniform(streams_of[6], (E,), jnp.float32, -0.5, 0.5), -0.5, 0.5),
        "xproj_weight": bell_draw(streams_of[7], (E, NPROJ), E ** -0.5, 0.125),
        "dtproj_weight": bell_draw(streams_of[8], (E, RANK), RANK ** -0.5, 0.75),
        "dt_bias": jnp.clip(jax.random.uniform(streams_of[9], (E,), jnp.float32, -5.0, -2.0), -5.0, -2.0),
        "a_log": jnp.clip(-3.0 + 5.5 * jax.random.uniform(streams_of[10], (DSTATE, E), jnp.float32) ** shard_levels(streams_of[10], (DSTATE, E), ((0, 4),), -0.2, 0.2), -3.0, 2.5),
        "d_skip": jnp.clip(jax.random.uniform(streams_of[11], (E,), jnp.float32, 0.5, 1.5), 0.5, 1.5),
        "out_weight": bell_draw(streams_of[12], (E, D), (E // 4) ** -0.5, 0.25),
    }


@jax.custom_vjp
def low(v):
    return lax.optimization_barrier(v.astype(jnp.bfloat16)).astype(jnp.float32)

@jax.custom_vjp
def low_back(v):
    return v

def low_keep(v):
    return (low(v), None)

def low_pass(kept, grad):
    return (grad,)

def back_keep(v):
    return (v, None)

def back_low(kept, grad):
    return (low(grad),)
low.defvjp(low_keep, low_pass)
low_back.defvjp(back_keep, back_low)
EPSILON = 1e-05
HIGHEST = lax.Precision.HIGHEST

def combine(earlier, later_pair):
    return (earlier[0] * later_pair[0], later_pair[0] * earlier[1] + later_pair[1])

def product(left_side, right_side):
    return jnp.dot(left_side, right_side, precision=HIGHEST, preferred_element_type=jnp.float32)

def slot_forward(params, inputs, alive_rows):
    norm_gain, in_weight, conv_weight, conv_bias, xproj_weight, dtproj_weight, dt_bias, a_log, d_skip, out_weight = params
    normed = inputs * lax.rsqrt(lax.optimization_barrier(jnp.mean(inputs * inputs, axis=1, keepdims=True)) + EPSILON)
    normed_low = low(normed * norm_gain)
    joined = low_back(product(normed_low, in_weight))
    inner = low(joined[:, :E])
    gate_in = joined[:, E:]
    padded = jnp.concatenate([jnp.zeros((CONV - 1, E), jnp.float32), inner], axis=0)
    conv_pre = conv_bias + jnp.zeros((SLOT, E), jnp.float32)
    for tap_index in range(CONV):
        conv_pre = conv_pre + conv_weight[tap_index] * padded[tap_index:tap_index + SLOT]
    mixed = jax.nn.silu(conv_pre)
    projected = low_back(product(low(mixed), xproj_weight))
    rank_low = low(projected[:, :RANK])
    b_in = projected[:, RANK:RANK + DSTATE]
    c_in = projected[:, RANK + DSTATE:]
    raised = low_back(product(rank_low, dtproj_weight.T)) + dt_bias
    step_size = jax.nn.softplus(raised)
    decay_rate = -jnp.exp(a_log)

    def scan_block(carry_state, block_items):
        step_block, mixed_block, b_block, c_block = block_items
        factor = jnp.exp(step_block[:, None, :] * decay_rate[None])
        drive_term = (step_block * mixed_block)[:, None, :] * b_block[:, :, None]
        cum_factor, cum_drive = lax.associative_scan(combine, (factor, drive_term), axis=0)
        states = cum_factor * carry_state[None] + cum_drive
        return (states[-1], lax.optimization_barrier(jnp.sum(c_block[:, :, None] * states, axis=1)))
    block_span = math.gcd(SLOT, 256)
    block_count = SLOT // block_span
    block_items = (step_size.reshape(block_count, block_span, E), mixed.reshape(block_count, block_span, E), b_in.reshape(block_count, block_span, DSTATE), c_in.reshape(block_count, block_span, DSTATE))
    unused, summed = lax.scan(jax.checkpoint(scan_block), jnp.zeros((DSTATE, E), jnp.float32), block_items)
    summed_y = low_back(summed.reshape(SLOT, E))
    full_y = summed_y + d_skip * mixed
    gated_low = low(full_y * jax.nn.silu(gate_in))
    result = inputs + alive_rows[:, None] * product(gated_low, out_weight)
    weighted = alive_rows[:, None] * step_size
    return (result, (lax.optimization_barrier(jnp.sum(weighted, axis=0)), lax.optimization_barrier(jnp.sum(weighted * step_size, axis=0))))

def reference(tokens, lengths, grad_out, norm_gain, in_weight, conv_weight, conv_bias, xproj_weight, dtproj_weight, dt_bias, a_log, d_skip, out_weight):
    params = tuple((weight.astype(jnp.float32) for weight in (norm_gain, in_weight, conv_weight, conv_bias, xproj_weight, dtproj_weight, dt_bias, a_log, d_skip, out_weight)))
    inputs = tokens.astype(jnp.float32).reshape(SLOTS, SLOT, D)
    alive_rows = (jnp.arange(SLOT, dtype=jnp.int32)[None, :] < lengths[:, None]).astype(jnp.float32)

    def forward_all(params_in, inputs_in):

        def one_slot(pair_items):
            return slot_forward(params_in, pair_items[0], pair_items[1])
        return lax.map(jax.checkpoint(one_slot), (inputs_in, alive_rows))
    outputs, pullback, dt_sums = jax.vjp(forward_all, params, inputs, has_aux=True)
    weight_grads, grad_inputs = pullback(grad_out.astype(jnp.float32).reshape(SLOTS, SLOT, D))
    live_count = jnp.sum(lengths).astype(jnp.float32)
    dt_mean = lax.optimization_barrier(jnp.sum(dt_sums[0], axis=0)) / live_count
    dt_spread = jnp.sqrt(lax.optimization_barrier(jnp.sum(dt_sums[1], axis=0)) / live_count - dt_mean * dt_mean + 1e-06)
    return (outputs.reshape(TOKENS, D).astype(jnp.bfloat16), grad_inputs.reshape(TOKENS, D), weight_grads[0], weight_grads[1], weight_grads[2], weight_grads[3], weight_grads[4], weight_grads[5], weight_grads[6], weight_grads[7], weight_grads[8], weight_grads[9], dt_mean, dt_spread)
```

```python
import functools

import jax
import jax.numpy as jnp
from jax import lax
from jax.experimental import pallas as pl
from jax.experimental.pallas import tpu as pltpu
from jax.sharding import PartitionSpec as P

EPSILON = 1e-05
LOG2E = 1.4426950408889634
LN2 = 0.6931471805599453
F32 = jnp.float32
BF16 = jnp.bfloat16


def swapped(value, distance):
    count = lax.axis_size("state")
    return lax.ppermute(value, "state", [(i, i ^ distance) for i in range(count)])


def shifted(value, axis, steps):
    count = lax.axis_size(axis)
    leading, last = (max(0, -steps), min(count, count - steps))
    return lax.ppermute(value, axis, [(source, source + steps) for source in range(leading, last)])


def rotated(value, axis, steps):
    count = lax.axis_size(axis)
    return lax.ppermute(value, axis, [(i, (i + steps) % count) for i in range(count)])


def gathered(value):
    count = lax.axis_size("state")
    return [value] + [swapped(value, d) for d in range(1, count)]


def column_exchange(value):
    count = lax.axis_size("state")
    me = lax.axis_index("state")
    width = value.shape[1] // count
    pieces = []
    for d in range(count):
        part = lax.dynamic_slice_in_dim(value, (me ^ d) * width, width, 1)
        pieces.append(part if d == 0 else swapped(part, d))
    return pieces


def row_reduce(value):
    count = lax.axis_size("state")
    me = lax.axis_index("state")
    height = value.shape[0] // count
    total = None
    for d in range(count):
        part = lax.dynamic_slice_in_dim(value, (me ^ d) * height, height, 0)
        part = part if d == 0 else swapped(part, d)
        total = part if total is None else total + part
    return total


def seq_rows_reduce(value, send_type):
    count = lax.axis_size("seq")
    me = lax.axis_index("seq")
    height = value.shape[0] // count
    total = lax.dynamic_slice_in_dim(value, me * height, height, 0)
    for r in range(1, count):
        part = lax.dynamic_slice_in_dim(value, lax.rem(me + r, count) * height, height, 0)
        total = total + rotated(part.astype(send_type), "seq", r).astype(F32)
    return total


def seq_sum(value):
    count = lax.axis_size("seq")
    total = value
    for r in range(1, count):
        total = total + rotated(value, "seq", r)
    return total


def channel_rows_reduce(value, send_type):
    seqs = lax.axis_size("seq")
    states = lax.axis_size("state")
    seq = lax.axis_index("seq")
    height = value.shape[0] // seqs
    total = None
    for r in range(seqs):
        pairs = []
        for s in range(seqs):
            for t in range(states):
                chunk = t * seqs + (r + s) % seqs
                pairs.append((s * states + t, (chunk // states) * states + chunk % states))
        part = lax.dynamic_slice_in_dim(value, lax.rem(seq + r, seqs) * height, height, 0)
        got = lax.ppermute(part.astype(send_type), ("seq", "state"), pairs).astype(F32)
        total = got if total is None else total + got
    return total


def placed_rows(value):
    count = lax.axis_size("state")
    me = lax.axis_index("state")
    out = jnp.zeros((count * value.shape[0],) + value.shape[1:], value.dtype)
    for d, piece in enumerate(gathered(value)):
        out = lax.dynamic_update_slice_in_dim(out, piece, (me ^ d) * value.shape[0], 0)
    return out


def placed_columns(value):
    count = lax.axis_size("state")
    me = lax.axis_index("state")
    out = jnp.zeros((value.shape[0], count * value.shape[1]), value.dtype)
    for d, piece in enumerate(gathered(value)):
        out = lax.dynamic_update_slice_in_dim(out, piece, (me ^ d) * value.shape[1], 1)
    return out


def fill_lanes(out_ref, cols_ref, rows):
    groups = 8
    states = cols_ref.shape[0]
    lanes = min(128, rows)

    def step(i, unused):
        tiles = []
        for u in range(groups):
            first = (i * groups + u) * 8
            base = pl.multiple_of((first // lanes) * lanes, lanes)
            tile = cols_ref[:, pl.ds(base, lanes)]
            tiles.append(pltpu.roll(tile, lax.rem(lanes - (first - base), lanes), axis=1))
        for u in range(groups):
            for r in range(8):
                out_ref[(i * groups + u) * 8 + r] = jnp.broadcast_to(
                    tiles[u][:, r : r + 1], (states, 128)
                )
        return 0

    lax.fori_loop(0, rows // (8 * groups), step, 0)


def sums_to_rows(values, sublane):
    step = 1
    while len(values) > 1:
        low = (sublane & step) == 0
        values = [
            jnp.where(low, a, b) + pltpu.roll(jnp.where(low, b, a), step, axis=0)
            for a, b in zip(values[::2], values[1::2])
        ]
        step *= 2
    return values[0]


def spread(ref, row, count):
    return jnp.broadcast_to(ref[pl.ds(row, 1), :], (count, ref.shape[1]))


def widened(value, times):
    return jnp.concatenate([value] * times, axis=1)


def ends_kernel(cols, rate, step, drive, grad_y, state_out, grad_out, lanes):
    rows, width = step.shape
    states = rate.shape[0]
    reps = width // 128

    @pl.when(pl.program_id(0) == 0)
    def _():
        fill_lanes(lanes, cols, rows)

    rates = rate[...]
    groups = rows // 8

    def body(i, carry):
        state, grad = carry
        for r in range(8):
            p = i * 8 + r
            factor = jnp.exp2(rates * spread(step, p, states))
            b_wide = widened(lanes[p, 0:states], reps)
            state = factor * state + spread(drive, p, states) * b_wide
        for r in range(7, -1, -1):
            p = (groups - 1 - i) * 8 + r
            factor = jnp.exp2(rates * spread(step, p, states))
            c_wide = widened(lanes[p, states : 2 * states], reps)
            grad = factor * (grad + spread(grad_y, p, states) * c_wide)
        return state, grad

    zero = jnp.zeros((states, width), F32)
    state, grad = lax.fori_loop(0, groups, body, (zero, zero))
    state_out[...] = state
    grad_out[...] = grad


def scan_kernel(
    cols, rate, step, drive, grad_y, state_in, grad_in,
    y_out, decay_out, source_out, rate_out, b_out, c_out, lanes, held
):
    rows, width = step.shape
    states = rate.shape[0]
    half = states // 2
    reps = width // 128

    @pl.when(pl.program_id(0) == 0)
    def _():
        fill_lanes(lanes, cols, rows)
        b_out[...] = jnp.zeros_like(b_out)
        c_out[...] = jnp.zeros_like(c_out)

    rates = rate[...]
    groups = rows // 8
    sublane = lax.broadcasted_iota(jnp.int32, (8, width), 0)
    held[0] = state_in[...]

    def forward(i, state):
        parts = []
        for r in range(8):
            p = i * 8 + r
            factor = jnp.exp2(rates * spread(step, p, states))
            b_wide = widened(lanes[p, 0:states], reps)
            c_wide = widened(lanes[p, states : 2 * states], reps)
            state = factor * state + spread(drive, p, states) * b_wide
            held[p + 1] = state
            seen = state * c_wide
            parts.append(seen[:half] + seen[half:])
        y_out[pl.ds(pl.multiple_of(i * 8, 8), 8), :] = sums_to_rows(parts, sublane)
        return state

    lax.fori_loop(0, groups, forward, state_in[...])

    def over_tiles(value):
        total = value[:, 0:128]
        for t in range(1, reps):
            total = total + value[:, 128 * t : 128 * t + 128]
        return total

    def backward(k, carry):
        grad_next, rate_sum = carry
        i = groups - 1 - k
        decay_parts = [None] * 8
        source_parts = [None] * 8
        here = held[i * 8 + 8]
        for r in range(7, -1, -1):
            p = i * 8 + r
            step_wide = spread(step, p, states)
            y_wide = spread(grad_y, p, states)
            factor = jnp.exp2(rates * step_wide)
            b_wide = widened(lanes[p, 0:states], reps)
            c_wide = widened(lanes[p, states : 2 * states], reps)
            grad = grad_next + y_wide * c_wide
            before = held[p]
            grad_next = factor * grad
            c_out[p] += over_tiles(here * y_wide)
            b_out[p] += over_tiles(grad * spread(drive, p, states))
            through = grad_next * before
            decay = through * rates
            rate_sum = rate_sum + through * step_wide
            source = grad * b_wide
            decay_parts[r] = decay[:half] + decay[half:]
            source_parts[r] = source[:half] + source[half:]
            here = before
        row = pl.ds(pl.multiple_of(i * 8, 8), 8)
        decay_out[row, :] = sums_to_rows(decay_parts, sublane)
        source_out[row, :] = sums_to_rows(source_parts, sublane)
        return grad_next, rate_sum

    zero = jnp.zeros((states, width), F32)
    unused, rate_sum = lax.fori_loop(0, groups, backward, (grad_in[...], zero))
    rate_out[...] = rate_sum


def block_width(channels):
    return min(512, channels)


def local_ends(cols, rate, step, drive, grad_y):
    rows, channels = step.shape
    states = rate.shape[0]
    width = block_width(channels)
    by_rows = pl.BlockSpec((rows, width), lambda q: (0, q))
    by_state = pl.BlockSpec((states, width), lambda q: (0, q))
    return pl.pallas_call(
        ends_kernel,
        grid=(channels // width,),
        in_specs=[pl.BlockSpec(cols.shape, lambda q: (0, 0)), by_state, by_rows, by_rows, by_rows],
        out_specs=[by_state, by_state],
        out_shape=[jax.ShapeDtypeStruct((states, channels), F32)] * 2,
        scratch_shapes=[pltpu.VMEM((rows, 2 * states, 128), F32)],
        compiler_params=pltpu.CompilerParams(vmem_limit_bytes=60 << 20),
        name="ends",
    )(cols, rate, step, drive, grad_y)


def full_scan(cols, rate, step, drive, grad_y, state_in, grad_in):
    rows, channels = step.shape
    states = rate.shape[0]
    width = block_width(channels)
    by_rows = pl.BlockSpec((rows, width), lambda q: (0, q))
    by_state = pl.BlockSpec((states, width), lambda q: (0, q))
    kept = pl.BlockSpec((rows, states, 128), lambda q: (0, 0, 0))
    return pl.pallas_call(
        scan_kernel,
        grid=(channels // width,),
        in_specs=[
            pl.BlockSpec(cols.shape, lambda q: (0, 0)),
            by_state,
            by_rows,
            by_rows,
            by_rows,
            by_state,
            by_state,
        ],
        out_specs=[by_rows, by_rows, by_rows, by_state, kept, kept],
        out_shape=[jax.ShapeDtypeStruct((rows, channels), F32)] * 3
        + [jax.ShapeDtypeStruct((states, channels), F32)]
        + [jax.ShapeDtypeStruct((rows, states, 128), F32)] * 2,
        scratch_shapes=[
            pltpu.VMEM((rows, 2 * states, 128), F32),
            pltpu.VMEM((rows + 1, states, width), F32),
        ],
        compiler_params=pltpu.CompilerParams(vmem_limit_bytes=63 << 20),
        name="scan",
    )(cols, rate, step, drive, grad_y, state_in, grad_in)


def dot(a, b, dims):
    return lax.dot_general(a, b, ((dims[0], dims[1]), ((), ())), preferred_element_type=F32)


def body(
    tokens,
    lengths,
    grad_out,
    norm_gain,
    in_weight,
    conv_weight,
    conv_bias,
    xproj_weight,
    dtproj_weight,
    dt_bias,
    a_log,
    d_skip,
    out_weight,
):
    rows, width = tokens.shape
    channels = out_weight.shape[0]
    rank = dtproj_weight.shape[1]
    states = (xproj_weight.shape[1] - rank) // 2
    taps = conv_weight.shape[0]
    group = lax.axis_size("state")
    member = lax.axis_index("state")
    position = member * rows + jnp.arange(rows, dtype=jnp.int32)
    alive = (position < lengths[0]).astype(F32)[:, None]

    cotangent = grad_out.astype(F32)
    masked_low = (cotangent * alive).astype(BF16)
    masked_all = gathered(masked_low)
    a_full = placed_rows(a_log)
    inputs = tokens.astype(F32)
    inv_scale = lax.rsqrt(jnp.mean(inputs * inputs, axis=1, keepdims=True) + EPSILON)
    normed = inputs * inv_scale
    normed_low = (normed * norm_gain).astype(BF16)
    normed_all = gathered(normed_low)
    inner = jnp.dot(normed_low, in_weight[:, :channels], preferred_element_type=F32).astype(BF16)
    inner_before = shifted(inner[rows - (taps - 1) :], "state", 1)
    inner_ext = jnp.concatenate([inner_before, inner], axis=0)
    gate_in = jnp.dot(normed_low, in_weight[:, channels:], preferred_element_type=F32)
    gate_sigmoid = jax.nn.sigmoid(gate_in)
    gate_act = gate_in * gate_sigmoid
    grad_gated = dot(masked_low, out_weight, ((1,), (1,)))
    grad_y = grad_gated * gate_act
    grad_y_low = grad_y.astype(BF16)

    conv_pre = conv_bias + conv_weight[taps - 1] * inner
    for s in range(1, taps):
        conv_pre = conv_pre + conv_weight[taps - 1 - s] * inner_ext[taps - 1 - s : taps - 1 - s + rows]
    mixed = jax.nn.silu(conv_pre)
    mixed_low = mixed.astype(BF16)
    projected = jnp.dot(mixed_low, xproj_weight, preferred_element_type=F32)
    rank_low = projected[:, :rank].astype(BF16)
    raised = dot(rank_low, dtproj_weight, ((1,), (1,))) + dt_bias
    step = jax.nn.softplus(raised)
    drive = step * mixed
    cols = projected[:, rank:].T
    rate = -jnp.exp(a_full)
    rate2 = rate * LOG2E

    state_end, grad_end = local_ends(cols, rate2, step, drive, grad_y_low.astype(F32))
    step_sum = jnp.sum(step, axis=0, keepdims=True)
    packed = jnp.concatenate(
        [state_end, grad_end, jnp.broadcast_to(step_sum, (8, channels))], axis=0
    )
    pieces = jnp.stack(gathered(packed))
    state_in = jnp.zeros((states, channels), F32)
    grad_in = jnp.zeros((states, channels), F32)
    for k in range(group):
        one = lax.dynamic_index_in_dim(pieces, member ^ k, 0, keepdims=False)
        passed = one[:states] + jnp.exp2(rate2 * one[2 * states : 2 * states + 1]) * state_in
        state_in = jnp.where(k < member, passed, state_in)
    for k in range(group - 1, -1, -1):
        one = lax.dynamic_index_in_dim(pieces, member ^ k, 0, keepdims=False)
        passed = (
            one[states : 2 * states] + jnp.exp2(rate2 * one[2 * states : 2 * states + 1]) * grad_in
        )
        grad_in = jnp.where(k > member, passed, grad_in)

    summed_y, decay_sum, source_sum, rate_sum, grad_b, grad_c = full_scan(
        cols, rate2, step, drive, grad_y_low.astype(F32), state_in, grad_in
    )

    full_y = summed_y + d_skip * mixed
    gated_low = (full_y * gate_act).astype(BF16)
    branch = jnp.dot(gated_low, out_weight, preferred_element_type=F32)
    output = (inputs + alive * branch).astype(BF16)
    grad_gate_low = (
        grad_gated * full_y * gate_sigmoid * (1.0 + gate_in * (1.0 - gate_sigmoid))
    ).astype(BF16)
    gated_all = column_exchange(gated_low)
    gate_all = column_exchange(grad_gate_low)
    out_part = sum(dot(g, m, ((0,), (0,))) for g, m in zip(gated_all, masked_all))
    gate_part = sum(dot(n, g, ((0,), (0,))) for n, g in zip(normed_all, gate_all))
    grad_out_w = placed_rows(channel_rows_reduce(out_part, BF16))
    gate_w = seq_rows_reduce(gate_part, BF16)

    weighted = alive * step
    grad_step = LN2 * decay_sum + mixed * source_sum
    grad_raised = grad_step * jax.nn.sigmoid(raised)
    raised_low = grad_raised.astype(BF16)
    grad_dtproj = dot(raised_low, rank_low, ((0,), (0,)))
    grad_rank = jnp.dot(raised_low, dtproj_weight, preferred_element_type=F32)
    grad_proj_low = jnp.concatenate(
        [grad_rank, jnp.sum(grad_b, axis=2), jnp.sum(grad_c, axis=2)], axis=1
    ).astype(BF16)
    grad_xproj = dot(mixed_low, grad_proj_low, ((0,), (0,)))
    grad_mixed = (
        step * source_sum + grad_y * d_skip + dot(grad_proj_low, xproj_weight, ((1,), (1,)))
    )
    pre_sigmoid = jax.nn.sigmoid(conv_pre)
    grad_pre = grad_mixed * pre_sigmoid * (1.0 + conv_pre * (1.0 - pre_sigmoid))
    grad_ahead = shifted(grad_pre[: taps - 1], "state", -1)
    grad_ext = jnp.concatenate([grad_pre, grad_ahead], axis=0)
    grad_inner = conv_weight[taps - 1] * grad_pre
    for s in range(1, taps):
        grad_inner = grad_inner + conv_weight[taps - 1 - s] * grad_ext[s : s + rows]
    grad_inner_low = grad_inner.astype(BF16)
    inner_all = column_exchange(grad_inner_low)
    inner_part = sum(dot(n, g, ((0,), (0,))) for n, g in zip(normed_all, inner_all))
    inner_w = seq_rows_reduce(inner_part, BF16)
    grad_in_w = jnp.concatenate([placed_columns(inner_w), placed_columns(gate_w)], axis=1)

    narrow = jnp.concatenate([grad_xproj, grad_dtproj], axis=1)
    narrow = placed_rows(channel_rows_reduce(row_reduce(narrow), F32))
    proj_width = xproj_weight.shape[1]

    vectors = [jnp.sum(grad_pre * inner_ext[k : k + rows].astype(F32), axis=0) for k in range(taps)]
    vectors += [
        jnp.sum(grad_pre, axis=0),
        jnp.sum(grad_raised, axis=0),
        jnp.sum(grad_y * mixed, axis=0),
        jnp.sum(weighted, axis=0),
        jnp.sum(weighted * step, axis=0),
    ]
    small = jnp.concatenate([jnp.stack(vectors), rate_sum * rate], axis=0)
    small = row_reduce(small.reshape(small.shape[0], group, -1).transpose(1, 0, 2).reshape(group * small.shape[0], -1))
    small = placed_columns(seq_sum(small))

    grad_normed = dot(grad_inner_low, in_weight[:, :channels], ((1,), (1,))) + dot(
        grad_gate_low, in_weight[:, channels:], ((1,), (1,))
    )
    grad_gain = jnp.sum(grad_normed * normed, axis=0)
    grad_gain = sum(gathered(seq_sum(grad_gain)))
    scaled = grad_normed * norm_gain
    grad_tokens = cotangent + inv_scale * (
        scaled - normed * jnp.mean(scaled * normed, axis=1, keepdims=True)
    )
    live = seq_sum(lengths[0].astype(F32))
    dt_mean = small[taps + 3] / live
    dt_spread = jnp.sqrt(small[taps + 4] / live - dt_mean * dt_mean + 1e-06)
    grad_a_log = lax.dynamic_slice_in_dim(
        small[taps + 5 :], member * a_log.shape[0], a_log.shape[0], 0
    )
    return (
        output,
        grad_tokens,
        grad_gain,
        grad_in_w,
        small[:taps],
        small[taps],
        narrow[:, :proj_width],
        narrow[:, proj_width:],
        small[taps + 1],
        grad_a_log,
        small[taps + 2],
        grad_out_w,
        dt_mean,
        dt_spread,
    )


def solution(mesh):
    rows = P(("seq", "state"), None)
    return jax.shard_map(
        body,
        mesh=mesh,
        in_specs=(rows, P("seq"), rows) + (P(),) * 7 + (P("state", None), P(), P()),
        out_specs=(rows, rows, P(), P("seq", None), P(), P(), P("seq", None), P("seq", None), P())
        + (P("state", None), P(), P("seq", None), P(), P()),
        check_vma=False,
    )
```

```python
import functools

import jax
import jax.numpy as jnp
from jax import lax
from jax.experimental import pallas as pl
from jax.experimental.pallas import tpu as pltpu
from jax.sharding import PartitionSpec as P

EPSILON = 1e-05
LOG2E = 1.4426950408889634
LN2 = 0.6931471805599453
F32 = jnp.float32
BF16 = jnp.bfloat16


def swapped(value, distance):
    count = lax.axis_size("state")
    return lax.ppermute(value, "state", [(i, i ^ distance) for i in range(count)])


def shifted(value, axis, steps):
    count = lax.axis_size(axis)
    leading, last = (max(0, -steps), min(count, count - steps))
    return lax.ppermute(value, axis, [(source, source + steps) for source in range(leading, last)])


def rotated(value, axis, steps):
    count = lax.axis_size(axis)
    return lax.ppermute(value, axis, [(i, (i + steps) % count) for i in range(count)])


def gathered(value):
    count = lax.axis_size("state")
    return [value] + [swapped(value, d) for d in range(1, count)]


def half_of(value, axis, bit):
    return lax.dynamic_index_in_dim(value, bit, axis, keepdims=True)


def halved(value, axis, index_bit, name, distance, send_type):
    mine = half_of(value, axis, index_bit)
    other = half_of(value, axis, 1 - index_bit).astype(send_type)
    count = lax.axis_size(name)
    got = lax.ppermute(other, name, [(i, i ^ distance) for i in range(count)])
    return mine + got.astype(F32)


def seq_scatter(value, send_type):
    seqs = lax.axis_size("seq")
    seq = lax.axis_index("seq")
    bits = seqs.bit_length() - 1
    value = value.reshape((2,) * bits + value.shape[1:])
    for k in range(bits):
        axis = bits - 1 - k
        value = halved(value, axis, (seq >> k) & 1, "seq", 1 << k, F32 if k == 0 else send_type)
    return value.reshape(value.shape[bits:])


def total_scatter(value):
    seqs = lax.axis_size("seq")
    states = lax.axis_size("state")
    seq = lax.axis_index("seq")
    state = lax.axis_index("state")
    seq_bits = seqs.bit_length() - 1
    state_bits = states.bit_length() - 1
    bits = seq_bits + state_bits
    value = value.reshape((2,) * bits + value.shape[1:])
    for name, index, k in (
        [("seq", seq, 0)]
        + [("state", state, k) for k in range(state_bits)]
        + [("seq", seq, k) for k in range(1, seq_bits)]
    ):
        axis = (seq_bits if name == "seq" else bits) - 1 - k
        value = halved(value, axis, (index >> k) & 1, name, 1 << k, F32)
    return value.reshape(value.shape[bits:])


def total_sum(value):
    for name in ("seq", "state"):
        count = lax.axis_size(name)
        for k in range(count.bit_length() - 1):
            value = value + lax.ppermute(value, name, [(i, i ^ (1 << k)) for i in range(count)])
    return value


def to_owner(value):
    seqs = lax.axis_size("seq")
    states = lax.axis_size("state")
    pairs = [(s * states + t, t * seqs + s) for s in range(seqs) for t in range(states)]
    return lax.ppermute(value, ("seq", "state"), pairs)


def placed(pieces, axis):
    me = lax.axis_index("state")
    size = pieces[0].shape[axis]
    shape = list(pieces[0].shape)
    shape[axis] = size * len(pieces)
    out = jnp.zeros(shape, pieces[0].dtype)
    for d, piece in enumerate(pieces):
        out = lax.dynamic_update_slice_in_dim(out, piece, (me ^ d) * size, axis)
    return out


def fill_lanes(out_ref, cols_ref, rows):
    groups = 8
    states = cols_ref.shape[0]
    lanes = min(128, rows)

    def step(i, unused):
        tiles = []
        for u in range(groups):
            first = (i * groups + u) * 8
            base = pl.multiple_of((first // lanes) * lanes, lanes)
            tile = cols_ref[:, pl.ds(base, lanes)]
            tiles.append(pltpu.roll(tile, lax.rem(lanes - (first - base), lanes), axis=1))
        for u in range(groups):
            for r in range(8):
                out_ref[(i * groups + u) * 8 + r] = jnp.broadcast_to(
                    tiles[u][:, r : r + 1], (states, 128)
                )
        return 0

    lax.fori_loop(0, rows // (8 * groups), step, 0)


def sums_to_rows(values, sublane):
    step = 1
    while len(values) > 1:
        low = (sublane & step) == 0
        values = [
            jnp.where(low, a, b) + pltpu.roll(jnp.where(low, b, a), step, axis=0)
            for a, b in zip(values[::2], values[1::2])
        ]
        step *= 2
    return values[0]


def spread(ref, row, count):
    return jnp.broadcast_to(ref[pl.ds(row, 1), :], (count, ref.shape[1]))


def widened(value, times):
    return jnp.concatenate([value] * times, axis=1)


def conv_window(window, weight, bias, rows):
    taps = weight.shape[0]
    total = bias + weight[taps - 1 : taps] * window[8:]
    for s in range(1, taps):
        total = total + weight[taps - 1 - s : taps - s] * window[8 - s : 8 - s + rows]
    return total


def logistic(value):
    return 1.0 / (1.0 + jnp.exp(-value))


def by_eight(value):
    total = value[0:8]
    for k in range(8, value.shape[0], 8):
        total = total + value[k : k + 8]
    return total


def widen_rows(ext, before, inner):
    rows = inner.shape[0]
    ext[0:8] = before[...].astype(F32)

    def move(i, unused):
        at = pl.multiple_of(i * 32, 32)
        ext[pl.ds(at + 8, 32), :] = inner[pl.ds(at, 32), :].astype(F32)
        return 0

    lax.fori_loop(0, rows // 32, move, 0)


def front_kernel(inner, before, conv_w, conv_b, xproj, mixed_out, proj_out, ext, low):
    rows = inner.shape[0]

    @pl.when(pl.program_id(0) == 0)
    def _():
        proj_out[...] = jnp.zeros_like(proj_out)

    widen_rows(ext, before, inner)
    weight = conv_w[...]
    bias = conv_b[...]

    def chunk(i, unused):
        at = pl.multiple_of(i * 32, 32)
        pre = conv_window(ext[pl.ds(at, 40), :], weight, bias, 32)
        mixed = pre * logistic(pre)
        mixed_out[pl.ds(at, 32), :] = mixed
        low[pl.ds(at, 32), :] = mixed.astype(BF16)
        return 0

    lax.fori_loop(0, rows // 32, chunk, 0)
    proj_out[...] += jnp.dot(low[...], xproj[...], preferred_element_type=F32)


def ends_kernel(
    live, proj, dtproj, dt_b, mixed, gate, grad_gated, rate,
    step_out, gy_out, sig_out, stat_out, state_out, grad_out, cols_out, lanes, drive, rank_low,
):
    rows, width = mixed.shape
    states = rate.shape[0]
    rank = dtproj.shape[1]
    reps = width // 128

    @pl.when(pl.program_id(0) == 0)
    def _():
        cols_out[...] = jnp.transpose(proj[...])[rank : rank + 2 * states]
        rank_low[...] = proj[:, :rank].astype(BF16)
        fill_lanes(lanes, cols_out, rows)

    bias = dt_b[...]
    count = min(64, rows)
    zero8 = jnp.zeros((8, width), F32)

    def prepare(i, sums):
        at = pl.ds(pl.multiple_of(i * count, count), count)
        raised = bias + dot(rank_low[at, :], dtproj[...], ((1,), (1,)))
        small = jnp.exp(-jnp.abs(raised))
        step = jnp.maximum(raised, 0.0) + jnp.log1p(small)
        inverse = 1.0 / (1.0 + small)
        step_out[at, :] = step
        sig_out[at, :] = jnp.where(raised >= 0.0, inverse, small * inverse)
        drive[at, :] = step * mixed[at, :]
        value = gate[at, :]
        grad_y = grad_gated[at, :] * (value * logistic(value))
        gy_out[at, :] = grad_y.astype(BF16).astype(F32)
        row = i * count + lax.broadcasted_iota(jnp.int32, (count, width), 0)
        seen = jnp.where(row < live[0], step, 0.0)
        return sums[0] + by_eight(step), sums[1] + by_eight(seen), sums[2] + by_eight(seen * step)

    sums = lax.fori_loop(0, rows // count, prepare, (zero8, zero8, zero8))
    stat_out[...] = zero8
    for k in range(3):
        stat_out[k : k + 1, :] = jnp.sum(sums[k], axis=0, keepdims=True)

    rates = rate[...]
    groups = rows // 8

    def body(i, carry):
        state, grad = carry
        for r in range(8):
            p = i * 8 + r
            factor = jnp.exp2(rates * spread(step_out, p, states))
            b_wide = widened(lanes[p, 0:states], reps)
            state = factor * state + spread(drive, p, states) * b_wide
        for r in range(7, -1, -1):
            p = (groups - 1 - i) * 8 + r
            factor = jnp.exp2(rates * spread(step_out, p, states))
            c_wide = widened(lanes[p, states : 2 * states], reps)
            grad = factor * (grad + spread(gy_out, p, states) * c_wide)
        return state, grad

    zero = jnp.zeros((states, width), F32)
    state, grad = lax.fori_loop(0, groups, body, (zero, zero))
    state_out[...] = state
    grad_out[...] = grad


def scan_kernel(
    order, cols, proj, rate, step, mixed, grad_y, sig, gate, grad_gated, state_in, grad_in, skip, dtproj,
    *rest,
):
    (
        gated_out, gate_out, send_out, mix_out, rate_out, vec_out, dtproj_out, rank_out, bc_out,
        lanes, held, b_sum, c_sum, drive, y_sum, decay_sum, source_sum, raised_low, rank_low,
    ) = rest[-19:]
    rows, width = step.shape
    states = rate.shape[0]
    rank = dtproj.shape[1]
    half = states // 2
    reps = width // 128
    block = pl.program_id(0)

    @pl.when(block == 0)
    def _():
        fill_lanes(lanes, cols, rows)
        rank_low[...] = proj[:, :rank].astype(BF16)
        b_sum[...] = jnp.zeros_like(b_sum)
        c_sum[...] = jnp.zeros_like(c_sum)
        rank_out[...] = jnp.zeros_like(rank_out)

    rates = rate[...]
    groups = rows // 8
    sublane = lax.broadcasted_iota(jnp.int32, (8, width), 0)
    held[0] = state_in[...]

    def forward(i, state):
        parts = []
        row = pl.ds(pl.multiple_of(i * 8, 8), 8)
        drive[row, :] = step[row, :] * mixed[row, :]
        for r in range(8):
            p = i * 8 + r
            factor = jnp.exp2(rates * spread(step, p, states))
            b_wide = widened(lanes[p, 0:states], reps)
            c_wide = widened(lanes[p, states : 2 * states], reps)
            state = factor * state + spread(drive, p, states) * b_wide
            held[p + 1] = state
            seen = state * c_wide
            parts.append(seen[:half] + seen[half:])
        y_sum[row, :] = sums_to_rows(parts, sublane)
        return state

    lax.fori_loop(0, groups, forward, state_in[...])

    def over_tiles(value):
        total = value[:, 0:128]
        for t in range(1, reps):
            total = total + value[:, 128 * t : 128 * t + 128]
        return total

    def backward(k, carry):
        grad_next, rate_sum = carry
        i = groups - 1 - k
        decay_parts = [None] * 8
        source_parts = [None] * 8
        here = held[i * 8 + 8]
        for r in range(7, -1, -1):
            p = i * 8 + r
            step_wide = spread(step, p, states)
            y_wide = spread(grad_y, p, states)
            factor = jnp.exp2(rates * step_wide)
            b_wide = widened(lanes[p, 0:states], reps)
            c_wide = widened(lanes[p, states : 2 * states], reps)
            grad = grad_next + y_wide * c_wide
            before = held[p]
            grad_next = factor * grad
            c_sum[p] += over_tiles(here * y_wide)
            b_sum[p] += over_tiles(grad * spread(drive, p, states))
            through = grad_next * before
            decay = through * rates
            rate_sum = rate_sum + through * step_wide
            source = grad * b_wide
            decay_parts[r] = decay[:half] + decay[half:]
            source_parts[r] = source[:half] + source[half:]
            here = before
        row = pl.ds(pl.multiple_of(i * 8, 8), 8)
        decay_sum[row, :] = sums_to_rows(decay_parts, sublane)
        source_sum[row, :] = sums_to_rows(source_parts, sublane)
        return grad_next, rate_sum

    zero = jnp.zeros((states, width), F32)
    unused, rate_sum = lax.fori_loop(0, groups, backward, (grad_in[...], zero))
    rate_out[...] = rate_sum * (rates * LN2)

    gain = skip[...]
    count = min(32, rows)
    zero8 = jnp.zeros((8, width), F32)

    def finish(i, sums):
        at = pl.ds(pl.multiple_of(i * count, count), count)
        value = gate[at, :]
        mix = mixed[at, :]
        upstream = grad_gated[at, :]
        full_y = y_sum[at, :] + gain * mix
        squash = logistic(value)
        act = value * squash
        gated = (full_y * act).astype(BF16)
        grad_gate = (upstream * full_y * squash * (1.0 + value * (1.0 - squash))).astype(BF16)
        gated_out[at, :] = gated
        gate_out[at, :] = grad_gate
        send_out[0, at, 0:width] = gated
        send_out[0, at, width : 2 * width] = grad_gate
        grad_full = upstream * act
        source = source_sum[at, :]
        grad_raised = (LN2 * decay_sum[at, :] + mix * source) * sig[at, :]
        raised = grad_raised.astype(BF16)
        raised_low[at, :] = raised
        mix_out[at, :] = step[at, :] * source + grad_full * gain
        rank_out[at, :] += jnp.dot(raised, dtproj[...], preferred_element_type=F32)
        return sums[0] + by_eight(grad_raised), sums[1] + by_eight(grad_full * mix)

    sums = lax.fori_loop(0, rows // count, finish, (zero8, zero8))
    vec_out[...] = zero8
    for k in range(2):
        vec_out[k : k + 1, :] = jnp.sum(sums[k], axis=0, keepdims=True)
    dtproj_out[...] = dot(raised_low[...], rank_low[...], ((0,), (0,)))

    @pl.when(block == pl.num_programs(0) - 1)
    def _():
        lane = lax.broadcasted_iota(jnp.int32, (states, 128), 1)

        def tile(j, unused):
            def gather(i, carry):
                b_tile, c_tile = carry
                for r in range(16):
                    p = j * 128 + i * 16 + r
                    here = lane == i * 16 + r
                    b_tile = jnp.where(here, jnp.sum(b_sum[p], axis=1, keepdims=True), b_tile)
                    c_tile = jnp.where(here, jnp.sum(c_sum[p], axis=1, keepdims=True), c_tile)
                return b_tile, c_tile

            zero_tile = jnp.zeros((states, 128), F32)
            b_tile, c_tile = lax.fori_loop(0, 8, gather, (zero_tile, zero_tile))
            at = pl.ds(pl.multiple_of(j * 128, 128), 128)
            bc_out[0:states, at] = b_tile
            bc_out[states : 2 * states, at] = c_tile
            return 0

        lax.fori_loop(0, rows // 128, tile, 0)


def back_kernel(
    order, proj_grad, xproj, mix_grad, inner, before, ahead, conv_w, conv_b,
    inner_out, send_out, vec_out, xproj_out, ext, pre_ext, low,
):
    rows, width = mix_grad.shape
    taps = conv_w.shape[0]
    widen_rows(ext, before, inner)
    weight = conv_w[...]
    bias = conv_b[...]
    pre_ext[rows : rows + 8, :] = ahead[...]
    zero8 = jnp.zeros((8, width), F32)

    def chunk(i, sums):
        at = pl.multiple_of(i * 32, 32)
        window = ext[pl.ds(at, 40), :]
        pre = conv_window(window, weight, bias, 32)
        squash = logistic(pre)
        low[pl.ds(at, 32), :] = (pre * squash).astype(BF16)
        grad_mixed = mix_grad[pl.ds(at, 32), :] + dot(
            proj_grad[pl.ds(at, 32), :], xproj[...], ((1,), (1,))
        )
        grad_pre = grad_mixed * squash * (1.0 + pre * (1.0 - squash))
        pre_ext[pl.ds(at, 32), :] = grad_pre
        added = [sums[taps] + by_eight(grad_pre)]
        for k in range(taps - 1, -1, -1):
            shift = taps - 1 - k
            added.insert(0, sums[k] + by_eight(grad_pre * window[8 - shift : 40 - shift]))
        return tuple(added)

    sums = lax.fori_loop(0, rows // 32, chunk, (zero8,) * (taps + 1))
    vec_out[...] = zero8
    for k in range(taps + 1):
        vec_out[k : k + 1, :] = jnp.sum(sums[k], axis=0, keepdims=True)

    def spread_back(i, unused):
        at = pl.multiple_of(i * 32, 32)
        window = pre_ext[pl.ds(at, 40), :]
        total = weight[taps - 1 : taps] * window[0:32]
        for s in range(1, taps):
            total = total + weight[taps - 1 - s : taps - s] * window[s : s + 32]
        rounded = total.astype(BF16)
        inner_out[pl.ds(at, 32), :] = rounded
        send_out[0, pl.ds(at, 32), :] = rounded
        return 0

    lax.fori_loop(0, rows // 32, spread_back, 0)
    xproj_out[...] = dot(low[...], proj_grad[...], ((0,), (0,)))


def struct(*shape, dtype=F32):
    return jax.ShapeDtypeStruct(shape, dtype)


def whole(shape):
    return pl.BlockSpec(shape, lambda *unused: (0,) * len(shape))


LIMIT = pltpu.CompilerParams(vmem_limit_bytes=63 << 20)


def front(inner, before, conv_weight, conv_bias, xproj, width):
    rows, channels = inner.shape

    def part(height):
        return pl.BlockSpec((height, width), lambda q: (0, q))

    return pl.pallas_call(
        front_kernel,
        grid=(channels // width,),
        in_specs=[
            part(rows), part(8), part(conv_weight.shape[0]), part(1),
            pl.BlockSpec((width, xproj.shape[1]), lambda q: (q, 0)),
        ],
        out_specs=[part(rows), whole((rows, xproj.shape[1]))],
        out_shape=[struct(rows, channels), struct(rows, xproj.shape[1])],
        scratch_shapes=[pltpu.VMEM((rows + 8, width), F32), pltpu.VMEM((rows, width), BF16)],
        compiler_params=LIMIT,
        name="front",
    )(inner, before, conv_weight, conv_bias, xproj)


def local_ends(live, proj, dtproj, dt_bias, mixed, gate, grad_gated, rate, width):
    rows, channels = mixed.shape
    states = rate.shape[0]
    rank = dtproj.shape[1]

    def part(height):
        return pl.BlockSpec((height, width), lambda q: (0, q))

    return pl.pallas_call(
        ends_kernel,
        grid=(channels // width,),
        in_specs=[
            pl.BlockSpec(memory_space=pltpu.SMEM), whole(proj.shape),
            pl.BlockSpec((width, rank), lambda q: (q, 0)), part(1),
            part(rows), part(rows), part(rows), part(states),
        ],
        out_specs=[part(rows)] * 3 + [part(8), part(states), part(states), whole((2 * states, rows))],
        out_shape=[struct(rows, channels)] * 3
        + [struct(8, channels), struct(states, channels), struct(states, channels), struct(2 * states, rows)],
        scratch_shapes=[
            pltpu.VMEM((rows, 2 * states, 128), F32),
            pltpu.VMEM((rows, width), F32),
            pltpu.VMEM((rows, rank), BF16),
        ],
        compiler_params=LIMIT,
        name="ends",
    )(live, proj, dtproj, dt_bias, mixed, gate, grad_gated, rate)


def full_scan(
    order, cols, proj, rate, step, mixed, grad_y, sig, gate, grad_gated, state_in, grad_in, skip, dtproj,
    earlier,
):
    rows, channels = step.shape
    states = rate.shape[0]
    rank = dtproj.shape[1]
    width = channels // lax.axis_size("state")
    blocks = order.shape[0]

    def part(height):
        return pl.BlockSpec((height, width), lambda q, order: (0, order[q]))

    tall = pl.BlockSpec((width, rank), lambda q, order: (order[q], 0))
    rows_f32 = part(rows)
    in_specs = [
        whole(cols.shape), whole(proj.shape), part(states), rows_f32, rows_f32, rows_f32, rows_f32,
        rows_f32, rows_f32, part(states), part(states), part(1), tall,
    ]
    out_specs = [
        part(rows), part(rows), pl.BlockSpec((1, rows, 2 * width), lambda q, order: (q, 0, 0)),
        part(rows), part(states), part(8), tall, whole((rows, rank)), whole((2 * states, rows)),
    ]
    out_shape = [
        struct(rows, channels, dtype=BF16), struct(rows, channels, dtype=BF16),
        struct(blocks, rows, 2 * width, dtype=BF16), struct(rows, channels), struct(states, channels),
        struct(8, channels), struct(channels, rank), struct(rows, rank), struct(2 * states, rows),
    ]
    args = [
        order, cols, proj, rate, step, mixed, grad_y, sig, gate, grad_gated, state_in, grad_in, skip, dtproj,
    ]
    aliases = {}
    for out, value in earlier:
        aliases[len(args)] = out
        args.append(value)
        in_specs.append(pl.BlockSpec(memory_space=pl.ANY))
    block = pltpu.VMEM((rows, width), F32)
    return pl.pallas_call(
        scan_kernel,
        grid_spec=pltpu.PrefetchScalarGridSpec(
            num_scalar_prefetch=1,
            grid=(blocks,),
            in_specs=in_specs,
            out_specs=out_specs,
            scratch_shapes=[
                pltpu.VMEM((rows, 2 * states, 128), F32),
                pltpu.VMEM((rows + 1, states, width), F32),
                pltpu.VMEM((rows, states, 128), F32),
                pltpu.VMEM((rows, states, 128), F32),
                block, block, block, block,
                pltpu.VMEM((rows, width), BF16),
                pltpu.VMEM((rows, rank), BF16),
            ],
        ),
        out_shape=out_shape,
        input_output_aliases=aliases,
        compiler_params=LIMIT,
        name="scan",
    )(*args)


def back(order, proj_grad, xproj, mix_grad, inner, before, ahead, conv_weight, conv_bias):
    rows, channels = mix_grad.shape
    width = channels // lax.axis_size("state")
    blocks = order.shape[0]

    def part(height):
        return pl.BlockSpec((height, width), lambda q, order: (0, order[q]))

    tall = pl.BlockSpec((width, xproj.shape[1]), lambda q, order: (order[q], 0))
    return pl.pallas_call(
        back_kernel,
        grid_spec=pltpu.PrefetchScalarGridSpec(
            num_scalar_prefetch=1,
            grid=(blocks,),
            in_specs=[
                whole(proj_grad.shape), tall, part(rows), part(rows), part(8), part(8),
                part(conv_weight.shape[0]), part(1),
            ],
            out_specs=[
                part(rows), pl.BlockSpec((1, rows, width), lambda q, order: (q, 0, 0)), part(8), tall,
            ],
            scratch_shapes=[
                pltpu.VMEM((rows + 8, width), F32),
                pltpu.VMEM((rows + 8, width), F32),
                pltpu.VMEM((rows, width), BF16),
            ],
        ),
        out_shape=[
            struct(rows, channels, dtype=BF16), struct(blocks, rows, width, dtype=BF16),
            struct(8, channels), struct(channels, xproj.shape[1]),
        ],
        compiler_params=LIMIT,
        name="back",
    )(order, proj_grad, xproj, mix_grad, inner, before, ahead, conv_weight, conv_bias)


def dot(a, b, dims):
    return lax.dot_general(a, b, (dims, ((), ())), preferred_element_type=F32)


def body(
    tokens,
    lengths,
    grad_out,
    norm_gain,
    in_weight,
    conv_weight,
    conv_bias,
    xproj_weight,
    dtproj_weight,
    dt_bias,
    a_log,
    d_skip,
    out_weight,
):
    rows, features = tokens.shape
    channels = out_weight.shape[0]
    rank = dtproj_weight.shape[1]
    proj_width = xproj_weight.shape[1]
    states = (proj_width - rank) // 2
    taps = conv_weight.shape[0]
    group = lax.axis_size("state")
    seqs = lax.axis_size("seq")
    member = lax.axis_index("state")
    width = channels // group
    live_rows = jnp.clip(lengths - member * rows, 0, rows)
    alive = (jnp.arange(rows, dtype=jnp.int32) < live_rows[0]).astype(F32)[:, None]
    conv_row = conv_bias[None]
    xproj = jnp.pad(xproj_weight, ((0, 0), (0, 128 - proj_width)))

    a_full = lax.all_gather(a_log, "state", axis=0, tiled=True)
    rate2 = -jnp.exp(a_full) * LOG2E
    cotangent = grad_out.astype(F32)
    masked_low = (cotangent * alive).astype(BF16)
    masked_all = lax.all_gather(masked_low, "state", axis=0, tiled=True)
    inputs = tokens.astype(F32)
    inv_scale = lax.rsqrt(jnp.mean(inputs * inputs, axis=1, keepdims=True) + EPSILON)
    normed = inputs * inv_scale
    normed_low = (normed * norm_gain).astype(BF16)
    normed_all = lax.all_gather(normed_low, "state", axis=0, tiled=True)
    inner = jnp.dot(normed_low, in_weight[:, :channels], preferred_element_type=F32).astype(BF16)
    before = shifted(inner[rows - 8 :], "state", 1)
    gate_in = jnp.dot(normed_low, in_weight[:, channels:], preferred_element_type=F32)
    grad_gated = dot(masked_low, out_weight, ((1,), (1,)))
    mixed, proj = front(inner, before, conv_weight, conv_row, xproj, width)
    step, grad_y, sig, stats, state_end, grad_end, cols = local_ends(
        live_rows, proj, dtproj_weight, dt_bias[None], mixed, gate_in, grad_gated, rate2, width
    )

    sums_row = stats[0:8]
    pieces = [jnp.concatenate([state_end, sums_row], axis=0)]
    for d in range(1, group):
        chosen = jnp.where(member < (member ^ d), state_end, grad_end)
        pieces.append(swapped(jnp.concatenate([chosen, sums_row], axis=0), d))
    pieces = jnp.stack(pieces)
    state_in = jnp.zeros((states, channels), F32)
    grad_in = jnp.zeros((states, channels), F32)
    for k in range(group - 1):
        one = lax.dynamic_index_in_dim(pieces, member ^ k, 0, keepdims=False)
        passed = one[:states] + jnp.exp2(rate2 * one[states : states + 1]) * state_in
        state_in = jnp.where(k < member, passed, state_in)
    for k in range(group - 1, 0, -1):
        one = lax.dynamic_index_in_dim(pieces, member ^ k, 0, keepdims=False)
        passed = one[:states] + jnp.exp2(rate2 * one[states : states + 1]) * grad_in
        grad_in = jnp.where(k > member, passed, grad_in)

    first = list(range(1, group // 2 + 1))
    second = list(range(group // 2 + 1, group)) + [0]
    call = (cols, proj, rate2, step, mixed, grad_y, sig, gate_in, grad_gated, state_in, grad_in)
    call += (d_skip[None], dtproj_weight)
    one = full_scan(jnp.stack([member ^ d for d in first]), *call, [])
    gates = {d: swapped(one[2][q], d) for q, d in enumerate(first)}
    shared = [(k, one[k]) for k in (0, 1, 3, 4, 5, 6)]
    two = full_scan(jnp.stack([member ^ d for d in second]), *call, shared)
    gates.update({d: swapped(two[2][q], d) if d else two[2][q] for q, d in enumerate(second)})
    gated_low, grad_gate_low, _, mix_grad, grad_a, scan_sums, grad_dtproj, _, _ = two
    grad_rank = one[7] + two[7]
    grad_bc = (one[8] + two[8]).T

    grad_proj = jnp.concatenate(
        [grad_rank, grad_bc, jnp.zeros((rows, 128 - proj_width), F32)], axis=1
    ).astype(BF16)
    window = jnp.concatenate([before, inner[:8]], axis=0).astype(F32)
    head_pre = conv_window(window, conv_weight, conv_row, 8)
    head_squash = jax.nn.sigmoid(head_pre)
    head_mixed = mix_grad[:8] + dot(grad_proj[:8], xproj, ((1,), (1,)))
    head_grad = head_mixed * head_squash * (1.0 + head_pre * (1.0 - head_squash))
    ahead = shifted(head_grad, "state", -1)
    order = jnp.stack([member ^ d for d in range(group)])
    grad_inner_low, inner_sends, conv_sums, grad_xproj = back(
        order, grad_proj, xproj, mix_grad, inner, before, ahead, conv_weight, conv_row
    )
    inners = {d: swapped(inner_sends[d], d) if d else inner_sends[0] for d in range(group)}

    branch = jnp.dot(gated_low, out_weight, preferred_element_type=F32)
    output = (inputs + alive * branch).astype(BF16)

    def rows_of(values, d):
        return lax.dynamic_slice_in_dim(values, (member ^ d) * rows, rows, 0)

    out_part = sum(dot(gates[d][:, :width], rows_of(masked_all, d), ((0,), (0,))) for d in range(group))
    gate_part = sum(dot(rows_of(normed_all, d), gates[d][:, width:], ((0,), (0,))) for d in range(group))
    early = jnp.concatenate([out_part.reshape(seqs, -1), gate_part.reshape(seqs, -1)], axis=1)
    early = seq_scatter(early, BF16)
    half = early.shape[0] // 2
    early_out = to_owner(early[:half].reshape(width // seqs, features))
    grad_out_w = placed(gathered(early_out), 0)
    gate_w = early[half:].reshape(features // seqs, width)

    inner_part = sum(dot(rows_of(normed_all, d), inners[d], ((0,), (0,))) for d in range(group))
    inner_w = seq_scatter(inner_part.reshape(seqs, -1), BF16).reshape(features // seqs, width)
    grad_in_w = jnp.concatenate([placed(gathered(inner_w), 1), placed(gathered(gate_w), 1)], axis=1)

    narrow = jnp.concatenate([grad_xproj[:, :proj_width], grad_dtproj], axis=1)
    narrow = total_scatter(narrow.reshape(seqs * group, -1)).reshape(-1, proj_width + rank)
    narrow = placed(gathered(narrow), 0)

    small = total_sum(jnp.concatenate([grad_a, scan_sums, stats], axis=0))
    dtb, skip_sum = small[states], small[states + 1]
    sum_one, sum_two = small[states + 9], small[states + 10]

    grad_normed = dot(grad_inner_low, in_weight[:, :channels], ((1,), (1,))) + dot(
        grad_gate_low, in_weight[:, channels:], ((1,), (1,))
    )
    gain_part = jnp.sum(grad_normed * normed, axis=0)
    scaled = grad_normed * norm_gain
    grad_tokens = cotangent + inv_scale * (
        scaled - normed * jnp.mean(scaled * normed, axis=1, keepdims=True)
    )
    live_part = jnp.broadcast_to(live_rows.astype(F32), (channels - features,))
    late = jnp.concatenate([conv_sums[: taps + 1], jnp.concatenate([gain_part, live_part])[None]], axis=0)
    late = total_sum(late)
    live_count = late[taps + 1, features]
    dt_mean = sum_one / live_count
    dt_spread = jnp.sqrt(sum_two / live_count - dt_mean * dt_mean + 1e-06)
    grad_a_log = lax.dynamic_slice_in_dim(small, member * a_log.shape[0], a_log.shape[0], 0)
    return (
        output,
        grad_tokens,
        late[taps + 1, :features],
        grad_in_w,
        late[:taps],
        late[taps],
        narrow[:, :proj_width],
        narrow[:, proj_width:],
        dtb,
        grad_a_log,
        skip_sum,
        grad_out_w,
        dt_mean,
        dt_spread,
    )


def solution(mesh):
    rows = P(("seq", "state"), None)
    return jax.shard_map(
        body,
        mesh=mesh,
        in_specs=(rows, P("seq"), rows) + (P(),) * 7 + (P("state", None), P(), P()),
        out_specs=(rows, rows, P(), P("seq", None), P(), P(), P("seq", None), P("seq", None), P())
        + (P("state", None), P(), P("seq", None), P(), P()),
        check_vma=False,
    )
```

```python
import functools

import jax
import jax.numpy as jnp
from jax import lax
from jax.experimental import pallas as pl
from jax.experimental.pallas import tpu as pltpu
from jax.sharding import PartitionSpec as P

EPSILON = 1e-05
LOG2E = 1.4426950408889634
LN2 = 0.6931471805599453
F32 = jnp.float32
BF16 = jnp.bfloat16


def swapped(value, distance):
    count = lax.axis_size("state")
    return lax.ppermute(value, "state", [(i, i ^ distance) for i in range(count)])


def shifted(value, axis, steps):
    count = lax.axis_size(axis)
    leading, last = (max(0, -steps), min(count, count - steps))
    return lax.ppermute(value, axis, [(source, source + steps) for source in range(leading, last)])


def rotated(value, axis, steps):
    count = lax.axis_size(axis)
    return lax.ppermute(value, axis, [(i, (i + steps) % count) for i in range(count)])


def gathered(value):
    count = lax.axis_size("state")
    return [value] + [swapped(value, d) for d in range(1, count)]


def two_words(value):
    high = lax.reduce_precision(value, 8, 7)
    return jnp.concatenate([high.astype(BF16), (value - high).astype(BF16)], axis=0)


def one_word(value):
    count = value.shape[0] // 2
    return value[:count].astype(F32) + value[count:].astype(F32)


def seq_exchange(value, distance):
    count = lax.axis_size("seq")
    return lax.ppermute(value, "seq", [(i, i ^ distance) for i in range(count)])


def seq_scatter(mine, other, extra=0, hold=None, behind=None):
    seqs = lax.axis_size("seq")
    seq = lax.axis_index("seq")
    width = mine.shape[1]
    total = mine + seq_exchange(other, 1)
    if behind is not None:
        total, behind = lax.optimization_barrier((total, behind))
    chips = seqs // 2
    high = (total.shape[0] - extra) // chips
    total, sums = total[: chips * high], total[chips * high :]
    k = 1
    while chips > 1:
        chips //= 2
        total = total.reshape(chips, 2, high, width)
        bit = (seq >> k) & 1
        kept = lax.dynamic_index_in_dim(total, bit, 1, keepdims=False)
        away = lax.dynamic_index_in_dim(total, 1 - bit, 1, keepdims=False).astype(BF16)
        away = away.reshape(chips * high, width)
        if extra:
            away = jnp.concatenate([away, two_words(sums)], axis=0)
        got = seq_exchange(away, 1 << k)
        total = kept + got[: chips * high].astype(F32).reshape(kept.shape)
        if extra:
            sums = sums + one_word(got[chips * high :])
        k += 1
    total = total.reshape(high, width)
    if hold is not None:
        total, hold = lax.optimization_barrier((total, hold))
    return total, sums, hold, behind


def to_owner(value):
    seqs = lax.axis_size("seq")
    states = lax.axis_size("state")
    pairs = [(s * states + t, t * seqs + s) for s in range(seqs) for t in range(states)]
    return lax.ppermute(value, ("seq", "state"), pairs)


def placed(pieces, axis, out=None, start=0):
    me = lax.axis_index("state")
    size = pieces[0].shape[axis]
    if out is None:
        shape = list(pieces[0].shape)
        shape[axis] = size * len(pieces)
        out = jnp.zeros(shape, pieces[0].dtype)
    for d, piece in enumerate(pieces):
        out = lax.dynamic_update_slice_in_dim(out, piece, start + (me ^ d) * size, axis)
    return out


def fill_lanes(out_ref, cols_ref, rows):
    groups = 8
    states = cols_ref.shape[0]
    lanes = min(128, rows)

    def step(i, unused):
        tiles = []
        for u in range(groups):
            first = (i * groups + u) * 8
            base = pl.multiple_of((first // lanes) * lanes, lanes)
            tile = cols_ref[:, pl.ds(base, lanes)]
            tiles.append(pltpu.roll(tile, lax.rem(lanes - (first - base), lanes), axis=1))
        for u in range(groups):
            for r in range(8):
                out_ref[(i * groups + u) * 8 + r] = jnp.broadcast_to(
                    tiles[u][:, r : r + 1], (states, 128)
                )
        return 0

    lax.fori_loop(0, rows // (8 * groups), step, 0)


def sums_to_rows(values, sublane):
    step = 1
    while len(values) > 1:
        low = (sublane & step) == 0
        values = [
            jnp.where(low, a, b) + pltpu.roll(jnp.where(low, b, a), step, axis=0)
            for a, b in zip(values[::2], values[1::2])
        ]
        step *= 2
    return values[0]


def spread(ref, row, count):
    return jnp.broadcast_to(ref[pl.ds(row, 1), :], (count, ref.shape[1]))


def widened(value, times):
    return jnp.concatenate([value] * times, axis=1)


def conv_window(window, weight, bias, rows):
    taps = weight.shape[0]
    total = bias + weight[taps - 1 : taps] * window[8:]
    for s in range(1, taps):
        total = total + weight[taps - 1 - s : taps - s] * window[8 - s : 8 - s + rows]
    return total


def logistic(value):
    return 1.0 / (1.0 + jnp.exp(-value))


def by_eight(value):
    total = value[0:8]
    for k in range(8, value.shape[0], 8):
        total = total + value[k : k + 8]
    return total


def widen_rows(ext, before, inner):
    rows = inner.shape[0]
    ext[0:8] = before[...].astype(F32)

    def move(i, unused):
        at = pl.multiple_of(i * 32, 32)
        ext[pl.ds(at + 8, 32), :] = inner[pl.ds(at, 32), :].astype(F32)
        return 0

    lax.fori_loop(0, rows // 32, move, 0)


def front_kernel(inner, before, conv_w, conv_b, xproj, mixed_out, proj_out, ext, low):
    rows = inner.shape[0]

    @pl.when(pl.program_id(0) == 0)
    def _():
        proj_out[...] = jnp.zeros_like(proj_out)

    widen_rows(ext, before, inner)
    weight = conv_w[...]
    bias = conv_b[...]

    def chunk(i, unused):
        at = pl.multiple_of(i * 32, 32)
        pre = conv_window(ext[pl.ds(at, 40), :], weight, bias, 32)
        mixed = pre * logistic(pre)
        mixed_out[pl.ds(at, 32), :] = mixed
        low[pl.ds(at, 32), :] = mixed.astype(BF16)
        return 0

    lax.fori_loop(0, rows // 32, chunk, 0)
    proj_out[...] += jnp.dot(low[...], xproj[...], preferred_element_type=F32)


def ends_kernel(
    live, proj, dtproj, dt_b, mixed, gate, grad_gated, rate,
    step_out, gy_out, sig_out, stat_out, state_out, grad_out, cols_out, lanes, drive, rank_low,
):
    rows, width = mixed.shape
    states = rate.shape[0]
    rank = dtproj.shape[1]
    reps = width // 128

    @pl.when(pl.program_id(0) == 0)
    def _():
        cols_out[...] = jnp.transpose(proj[...])[rank : rank + 2 * states]
        rank_low[...] = proj[:, :rank].astype(BF16)
        fill_lanes(lanes, cols_out, rows)

    bias = dt_b[...]
    count = min(64, rows)
    zero8 = jnp.zeros((8, width), F32)

    def prepare(i, sums):
        at = pl.ds(pl.multiple_of(i * count, count), count)
        raised = bias + dot(rank_low[at, :], dtproj[...], ((1,), (1,)))
        small = jnp.exp(-jnp.abs(raised))
        step = jnp.maximum(raised, 0.0) + jnp.log1p(small)
        inverse = 1.0 / (1.0 + small)
        step_out[at, :] = step
        sig_out[at, :] = jnp.where(raised >= 0.0, inverse, small * inverse)
        drive[at, :] = step * mixed[at, :]
        value = gate[at, :]
        grad_y = grad_gated[at, :] * (value * logistic(value))
        gy_out[at, :] = grad_y.astype(BF16).astype(F32)
        row = i * count + lax.broadcasted_iota(jnp.int32, (count, width), 0)
        seen = jnp.where(row < live[0], step, 0.0)
        return sums[0] + by_eight(step), sums[1] + by_eight(seen), sums[2] + by_eight(seen * step)

    sums = lax.fori_loop(0, rows // count, prepare, (zero8, zero8, zero8))
    stat_out[...] = zero8
    for k in range(3):
        stat_out[k : k + 1, :] = jnp.sum(sums[k], axis=0, keepdims=True)

    rates = rate[...]
    groups = rows // 8

    def body(i, carry):
        state, grad = carry
        for r in range(8):
            p = i * 8 + r
            factor = jnp.exp2(rates * spread(step_out, p, states))
            b_wide = widened(lanes[p, 0:states], reps)
            state = factor * state + spread(drive, p, states) * b_wide
        for r in range(7, -1, -1):
            p = (groups - 1 - i) * 8 + r
            factor = jnp.exp2(rates * spread(step_out, p, states))
            c_wide = widened(lanes[p, states : 2 * states], reps)
            grad = factor * (grad + spread(gy_out, p, states) * c_wide)
        return state, grad

    zero = jnp.zeros((states, width), F32)
    state, grad = lax.fori_loop(0, groups, body, (zero, zero))
    state_out[...] = state
    grad_out[...] = grad


def scan_kernel(
    skipped, order, cols, proj, rate, step, mixed, grad_y, sig, gate, grad_gated, state_in, grad_in, skip, dtproj,
    *rest,
):
    rest = rest[skipped:]
    gated_out, gate_out, mix_out, rate_out, vec_out, dtproj_out, rank_out, bc_out = rest[:8]
    sends = rest[8:-10]
    (
        lanes, held, b_sum, c_sum, drive, y_sum, decay_sum, source_sum, raised_low, rank_low
    ) = rest[-10:]
    rows, width = step.shape
    states = rate.shape[0]
    rank = dtproj.shape[1]
    half = states // 2
    reps = width // 128
    block = pl.program_id(0)

    @pl.when(block == 0)
    def _():
        fill_lanes(lanes, cols, rows)
        rank_low[...] = proj[:, :rank].astype(BF16)
        b_sum[...] = jnp.zeros_like(b_sum)
        c_sum[...] = jnp.zeros_like(c_sum)
        rank_out[...] = jnp.zeros_like(rank_out)

    rates = rate[...]
    groups = rows // 8
    sublane = lax.broadcasted_iota(jnp.int32, (8, width), 0)
    held[0] = state_in[...]

    def forward(i, state):
        parts = []
        row = pl.ds(pl.multiple_of(i * 8, 8), 8)
        drive[row, :] = step[row, :] * mixed[row, :]
        for r in range(8):
            p = i * 8 + r
            factor = jnp.exp2(rates * spread(step, p, states))
            b_wide = widened(lanes[p, 0:states], reps)
            c_wide = widened(lanes[p, states : 2 * states], reps)
            state = factor * state + spread(drive, p, states) * b_wide
            held[p + 1] = state
            seen = state * c_wide
            parts.append(seen[:half] + seen[half:])
        y_sum[row, :] = sums_to_rows(parts, sublane)
        return state

    lax.fori_loop(0, groups, forward, state_in[...])

    def over_tiles(value):
        total = value[:, 0:128]
        for t in range(1, reps):
            total = total + value[:, 128 * t : 128 * t + 128]
        return total

    def backward(k, carry):
        grad_next, rate_sum = carry
        i = groups - 1 - k
        decay_parts = [None] * 8
        source_parts = [None] * 8
        here = held[i * 8 + 8]
        for r in range(7, -1, -1):
            p = i * 8 + r
            step_wide = spread(step, p, states)
            y_wide = spread(grad_y, p, states)
            factor = jnp.exp2(rates * step_wide)
            b_wide = widened(lanes[p, 0:states], reps)
            c_wide = widened(lanes[p, states : 2 * states], reps)
            grad = grad_next + y_wide * c_wide
            before = held[p]
            grad_next = factor * grad
            c_sum[p] += over_tiles(here * y_wide)
            b_sum[p] += over_tiles(grad * spread(drive, p, states))
            through = grad_next * before
            decay = through * rates
            rate_sum = rate_sum + through * step_wide
            source = grad * b_wide
            decay_parts[r] = decay[:half] + decay[half:]
            source_parts[r] = source[:half] + source[half:]
            here = before
        row = pl.ds(pl.multiple_of(i * 8, 8), 8)
        decay_sum[row, :] = sums_to_rows(decay_parts, sublane)
        source_sum[row, :] = sums_to_rows(source_parts, sublane)
        return grad_next, rate_sum

    zero = jnp.zeros((states, width), F32)
    unused, rate_sum = lax.fori_loop(0, groups, backward, (grad_in[...], zero))
    rate_out[...] = rate_sum * (rates * LN2)

    gain = skip[...]
    count = min(32, rows)
    zero8 = jnp.zeros((8, width), F32)

    def finish(i, sums):
        at = pl.ds(pl.multiple_of(i * count, count), count)
        value = gate[at, :]
        mix = mixed[at, :]
        upstream = grad_gated[at, :]
        full_y = y_sum[at, :] + gain * mix
        squash = logistic(value)
        act = value * squash
        gated = (full_y * act).astype(BF16)
        grad_gate = (upstream * full_y * squash * (1.0 + value * (1.0 - squash))).astype(BF16)
        gated_out[at, :] = gated
        gate_out[at, :] = grad_gate
        for d, send in enumerate(sends):

            @pl.when(block == d)
            def _(send=send):
                send[at, 0:width] = gated
                send[at, width : 2 * width] = grad_gate

        grad_full = upstream * act
        source = source_sum[at, :]
        grad_raised = (LN2 * decay_sum[at, :] + mix * source) * sig[at, :]
        raised = grad_raised.astype(BF16)
        raised_low[at, :] = raised
        mix_out[at, :] = step[at, :] * source + grad_full * gain
        rank_out[at, :] += jnp.dot(raised, dtproj[...], preferred_element_type=F32)
        return sums[0] + by_eight(grad_raised), sums[1] + by_eight(grad_full * mix)

    sums = lax.fori_loop(0, rows // count, finish, (zero8, zero8))
    vec_out[...] = zero8
    for k in range(2):
        vec_out[k : k + 1, :] = jnp.sum(sums[k], axis=0, keepdims=True)
    dtproj_out[...] = dot(raised_low[...], rank_low[...], ((0,), (0,)))

    @pl.when(block == pl.num_programs(0) - 1)
    def _():
        lane = lax.broadcasted_iota(jnp.int32, (states, 128), 1)

        def tile(j, unused):
            def gather(i, carry):
                b_tile, c_tile = carry
                for r in range(16):
                    p = j * 128 + i * 16 + r
                    here = lane == i * 16 + r
                    b_tile = jnp.where(here, jnp.sum(b_sum[p], axis=1, keepdims=True), b_tile)
                    c_tile = jnp.where(here, jnp.sum(c_sum[p], axis=1, keepdims=True), c_tile)
                return b_tile, c_tile

            zero_tile = jnp.zeros((states, 128), F32)
            b_tile, c_tile = lax.fori_loop(0, 8, gather, (zero_tile, zero_tile))
            at = pl.ds(pl.multiple_of(j * 128, 128), 128)
            bc_out[0:states, at] = b_tile
            bc_out[states : 2 * states, at] = c_tile
            return 0

        lax.fori_loop(0, rows // 128, tile, 0)


def back_kernel(
    order, proj_grad, xproj, mix_grad, inner, before, ahead, conv_w, conv_b, rate_sums, scan_sums, step_sums,
    dtproj_grad, inner_out, thin_out, *rest,
):
    sends, (ext, pre_ext, low) = rest[:-3], rest[-3:]
    rows, width = mix_grad.shape
    taps = conv_w.shape[0]
    states = rate_sums.shape[0]
    block = pl.program_id(0)
    widen_rows(ext, before, inner)
    weight = conv_w[...]
    bias = conv_b[...]
    pre_ext[rows : rows + 8, :] = ahead[...]
    zero8 = jnp.zeros((8, width), F32)

    def chunk(i, sums):
        at = pl.multiple_of(i * 32, 32)
        window = ext[pl.ds(at, 40), :]
        pre = conv_window(window, weight, bias, 32)
        squash = logistic(pre)
        low[pl.ds(at, 32), :] = (pre * squash).astype(BF16)
        grad_mixed = mix_grad[pl.ds(at, 32), :] + dot(
            proj_grad[pl.ds(at, 32), :], xproj[...], ((1,), (1,))
        )
        grad_pre = grad_mixed * squash * (1.0 + pre * (1.0 - squash))
        pre_ext[pl.ds(at, 32), :] = grad_pre
        added = [sums[taps] + by_eight(grad_pre)]
        for k in range(taps - 1, -1, -1):
            shift = taps - 1 - k
            added.insert(0, sums[k] + by_eight(grad_pre * window[8 - shift : 40 - shift]))
        return tuple(added)

    sums = lax.fori_loop(0, rows // 32, chunk, (zero8,) * (taps + 1))

    summed = jnp.concatenate(
        [rate_sums[...], scan_sums[0:2, :], step_sums[1:3, :]]
        + [jnp.sum(v, axis=0, keepdims=True) for v in sums]
        + [jnp.zeros((32 - states - 5 - taps, width), F32)],
        axis=0,
    )
    high = summed.astype(BF16)
    words = jnp.concatenate([high, (summed - high.astype(F32)).astype(BF16)], axis=0)

    xproj_grad = dot(low[...], proj_grad[...], ((0,), (0,)))
    xproj_grad = xproj_grad.astype(BF16)
    step_grad = dtproj_grad[...].astype(BF16)
    group, entries, thin, _ = thin_out.shape
    seqs = width // thin
    side = seqs // (entries - seqs)
    me = order[group - 1]
    for c in range(seqs):
        chunk_index = order[block] * seqs + c
        place = lax.rem(chunk_index, group) ^ me
        thin_out[place, chunk_index // group] = xproj_grad[c * thin : (c + 1) * thin]
    for c in range(0, seqs, side * group):
        for t in range(group):
            parts = [
                step_grad[(c + k * group + t) * thin : (c + k * group + t + 1) * thin] for k in range(side)
            ]
            parts += [jnp.zeros_like(parts[0])] * (2 - side)
            at = (order[block] * seqs + c) // (group * side)
            thin_out[t ^ me, seqs + at] = jnp.concatenate(parts, axis=1)

    def spread_back(i, unused):
        at = pl.multiple_of(i * 32, 32)
        window = pre_ext[pl.ds(at, 40), :]
        total = weight[taps - 1 : taps] * window[0:32]
        for s in range(1, taps):
            total = total + weight[taps - 1 - s : taps - s] * window[s : s + 32]
        rounded = total.astype(BF16)
        inner_out[pl.ds(at, 32), :] = rounded
        for d, send in enumerate(sends):

            @pl.when(block == d)
            def _(send=send):
                send[pl.ds(at, 32), :] = rounded

        return 0

    lax.fori_loop(0, rows // 32, spread_back, 0)
    for d, send in enumerate(sends):

        @pl.when(block == d)
        def _(send=send):
            send[rows : rows + 64, :] = words


def put_chunks(targets, total, core, step, entry, high, first_row, fold):
    width = targets[0].shape[1]
    rows = high // fold
    each = total.shape[0] // rows
    for c in range(each):
        first = pl.multiple_of((step * each + c) // 2 * entry, 8) + first_row
        for parity in range(2):

            @pl.when(lax.rem(core + c, 2) == parity)
            def _(parity=parity, first=first, c=c):
                for f in range(fold):
                    targets[parity][pl.ds(first + f * rows, rows), :] = total[
                        c * rows : (c + 1) * rows, f * width : (f + 1) * width
                    ]


def summed_products(lefts, rights):
    total = None
    for left, right in zip(lefts, rights):
        part = dot(left, right, ((0,), (0,)))
        total = part if total is None else total + part
    return total


def wide_kernel(high, at, *refs):
    count = (len(refs) - 2) // 4
    outs, gates, masked, normed = (refs[k * count : (k + 1) * count] for k in range(4))
    targets = refs[-2:]
    width = targets[0].shape[1]
    total = summed_products([r[...] for r in outs], [r[...] for r in masked])
    fold = masked[0].shape[1] // width
    step = pl.program_id(0)
    put_chunks(targets, total, at[0], step, 2 * high, high, 0, fold)
    total = summed_products([r[...] for r in normed], [r[...] for r in gates])
    put_chunks(targets, total, at[0], step, 2 * high, high, high, 1)


def inner_kernel(total_chunks, at, *refs):
    count = (len(refs) - 4) // 3
    normed, inners, thins = (refs[k * count : (k + 1) * count] for k in range(3))
    gain, live = refs[3 * count : 3 * count + 2]
    targets = refs[-2:]
    core = at[0]
    rows = normed[0].shape[0]
    width = inners[0].shape[1]
    entries, thin, _ = thins[0].shape
    columns = 256
    seqs = total_chunks
    side = seqs // (entries - seqs)
    chips = seqs // 2
    extra = 48 if gain.shape[0] <= 8 else 0
    entry = (targets[0].shape[0] - extra) // chips
    packed = thin * columns // width
    high = entry - packed
    step = pl.program_id(0)
    total = summed_products([r[...] for r in normed], [r[0:rows, :] for r in inners])
    each = total.shape[0] // high
    for c in range(each):
        first = pl.multiple_of((step * each + c) // 2 * entry, 8)
        for parity in range(2):

            @pl.when(lax.rem(core + c, 2) == parity)
            def _(parity=parity, first=first, c=c):
                targets[parity][pl.ds(first, high), :] = total[c * high : (c + 1) * high]

    @pl.when(step == 0)
    def _():
        for i in range(seqs):
            value = thins[0][i].astype(F32)
            near = thins[0][seqs + i // side].astype(F32)
            for r in thins[1:]:
                value = value + r[i].astype(F32)
                near = near + r[seqs + i // side].astype(F32)
            at_lane = (i % side) * 64
            near = near[:, at_lane : at_lane + 64]
            value = jnp.concatenate([value, near, jnp.zeros_like(near)], axis=1)
            first = i // 2 * entry + high
            for parity in range(2):

                @pl.when(lax.rem(core + i, 2) == parity)
                def _(parity=parity, first=first, value=value):
                    if columns >= width:
                        for f in range(columns // width):
                            targets[parity][first + f * thin : first + (f + 1) * thin, :] = value[
                                :, f * width : (f + 1) * width
                            ]
                    else:
                        for f in range(width // columns):
                            targets[parity][
                                first : first + packed, f * columns : (f + 1) * columns
                            ] = value[f * packed : (f + 1) * packed]

        sums = None
        for r in inners:
            words = r[rows : rows + 64, :]
            value = words[0:32].astype(F32) + words[32:64].astype(F32)
            sums = value if sums is None else sums + value
        tail = jnp.concatenate(
            [sums, gain[...], jnp.full((extra - 32 - gain.shape[0], width), live[0], F32)], axis=0
        )
        for target in targets:
            target[chips * entry : chips * entry + extra, :] = tail


def assemble_kernel(
    at, *refs
):
    in_out, out_out, xproj_out, dtproj_out, conv_out, bias_out, dtb_out, skip_out, mean_out, spread_out = refs[-13:-3]
    a_out, gain_out, narrow = refs[-3:]
    count = (len(refs) - 13) // 2
    wides, lasts = refs[:count], refs[count : 2 * count]
    high = in_out.shape[0]
    channels = in_out.shape[1] // 2
    width = wides[0].shape[1]
    fold = out_out.shape[1] // width
    strip = high // fold
    thin, columns = narrow.shape[0] // count, narrow.shape[1]
    packed = thin * columns // width
    taps = conv_out.shape[0]
    mine = a_out.shape[0]
    states = mine * count
    rest = None
    first = high + packed
    for d in range(count):
        them = at[d + 1]
        piece = lasts[d]
        lanes = pl.ds(pl.multiple_of(them * width, 128), width)
        in_out[:, lanes] = piece[0:high, :]
        in_out[:, pl.ds(pl.multiple_of(channels + them * width, 128), width)] = wides[d][high : 2 * high, :]
        for f in range(fold):
            rows = pl.ds(pl.multiple_of(them * strip, 8), strip)
            out_out[rows, f * width : (f + 1) * width] = wides[d][f * strip : (f + 1) * strip, :]
        if columns >= width:
            for f in range(columns // width):
                rows = pl.ds(pl.multiple_of(them * thin, 8), thin)
                narrow[rows, f * width : (f + 1) * width] = piece[high + f * thin : high + (f + 1) * thin, :]
        else:
            for f in range(width // columns):
                rows = pl.ds(pl.multiple_of(them * thin + f * packed, 8), packed)
                narrow[rows, :] = piece[high : high + packed, f * columns : (f + 1) * columns]
        for k in range(count):

            @pl.when(at[1] == k)
            def _(k=k, lanes=lanes, piece=piece):
                a_out[:, lanes] = piece[first + k * mine : first + (k + 1) * mine, :]

        after = first + states
        dtb_out[:, lanes] = piece[after : after + 1, :]
        skip_out[:, lanes] = piece[after + 1 : after + 2, :]
        mean_out[:, lanes] = piece[after + 2 : after + 3, :]
        spread_out[:, lanes] = piece[after + 3 : after + 4, :]
        conv_out[:, lanes] = piece[after + 4 : after + 4 + taps, :]
        bias_out[:, lanes] = piece[after + 4 + taps : after + 5 + taps, :]
        tail = piece[first + 32 : first + 48, :]
        rest = tail if rest is None else rest + tail
    xproj_out[...] = narrow[:, 0 : xproj_out.shape[1]]
    dtproj_out[...] = narrow[:, 128 : 128 + dtproj_out.shape[1]]
    gain_out[...] = rest[0:fold]
    live = rest[fold : fold + 1, 0:1]
    mean = mean_out[...] / live
    spread = spread_out[...] / live - mean * mean + 1e-06
    mean_out[...] = mean
    spread_out[...] = jnp.sqrt(spread)


def struct(*shape, dtype=F32):
    return jax.ShapeDtypeStruct(shape, dtype)


def whole(shape):
    return pl.BlockSpec(shape, lambda *unused: (0,) * len(shape))


LIMIT = pltpu.CompilerParams(vmem_limit_bytes=63 << 20)


def front(inner, before, conv_weight, conv_bias, xproj, width):
    rows, channels = inner.shape

    def part(height):
        return pl.BlockSpec((height, width), lambda q: (0, q))

    return pl.pallas_call(
        front_kernel,
        grid=(channels // width,),
        in_specs=[
            part(rows), part(8), part(conv_weight.shape[0]), part(1),
            pl.BlockSpec((width, xproj.shape[1]), lambda q: (q, 0)),
        ],
        out_specs=[part(rows), whole((rows, xproj.shape[1]))],
        out_shape=[struct(rows, channels), struct(rows, xproj.shape[1])],
        scratch_shapes=[pltpu.VMEM((rows + 8, width), F32), pltpu.VMEM((rows, width), BF16)],
        compiler_params=LIMIT,
        cost_estimate=cost(8),
        name="front",
    )(inner, before, conv_weight, conv_bias, xproj)


def local_ends(live, proj, dtproj, dt_bias, mixed, gate, grad_gated, rate, width):
    rows, channels = mixed.shape
    states = rate.shape[0]
    rank = dtproj.shape[1]

    def part(height):
        return pl.BlockSpec((height, width), lambda q: (0, q))

    return pl.pallas_call(
        ends_kernel,
        grid=(channels // width,),
        in_specs=[
            pl.BlockSpec(memory_space=pltpu.SMEM), whole(proj.shape),
            pl.BlockSpec((width, rank), lambda q: (q, 0)), part(1),
            part(rows), part(rows), part(rows), part(states),
        ],
        out_specs=[part(rows)] * 3 + [part(8), part(states), part(states), whole((2 * states, rows))],
        out_shape=[struct(rows, channels)] * 3
        + [struct(8, channels), struct(states, channels), struct(states, channels), struct(2 * states, rows)],
        scratch_shapes=[
            pltpu.VMEM((rows, 2 * states, 128), F32),
            pltpu.VMEM((rows, width), F32),
            pltpu.VMEM((rows, rank), BF16),
        ],
        compiler_params=LIMIT,
        cost_estimate=cost(40),
        name="ends",
    )(live, proj, dtproj, dt_bias, mixed, gate, grad_gated, rate)


def full_scan(
    order, cols, proj, rate, step, mixed, grad_y, sig, gate, grad_gated, state_in, grad_in, skip, dtproj,
    earlier,
):
    rows, channels = step.shape
    states = rate.shape[0]
    rank = dtproj.shape[1]
    width = channels // lax.axis_size("state")
    blocks = order.shape[0]

    def part(height):
        return pl.BlockSpec((height, width), lambda q, order: (0, order[q]))

    tall = pl.BlockSpec((width, rank), lambda q, order: (order[q], 0))
    rows_f32 = part(rows)
    in_specs = [
        whole(cols.shape), whole(proj.shape), part(states), rows_f32, rows_f32, rows_f32, rows_f32,
        rows_f32, rows_f32, part(states), part(states), part(1), tall,
    ]
    out_specs = [
        part(rows), part(rows), part(rows), part(states), part(8), tall, whole((rows, rank)),
        whole((2 * states, rows)),
    ] + [whole((rows, 2 * width))] * blocks
    out_shape = [
        struct(rows, channels, dtype=BF16), struct(rows, channels, dtype=BF16),
        struct(rows, channels), struct(states, channels),
        struct(8, channels), struct(channels, rank), struct(rows, rank), struct(2 * states, rows),
    ] + [struct(rows, 2 * width, dtype=BF16)] * blocks
    args = [
        order, cols, proj, rate, step, mixed, grad_y, sig, gate, grad_gated, state_in, grad_in, skip, dtproj,
    ]
    aliases = {}
    for out, value in earlier:
        aliases[len(args)] = out
        args.append(value)
        in_specs.append(pl.BlockSpec(memory_space=pl.ANY))
    block = pltpu.VMEM((rows, width), F32)
    return pl.pallas_call(
        functools.partial(scan_kernel, len(earlier)),
        grid_spec=pltpu.PrefetchScalarGridSpec(
            num_scalar_prefetch=1,
            grid=(blocks,),
            in_specs=in_specs,
            out_specs=out_specs,
            scratch_shapes=[
                pltpu.VMEM((rows, 2 * states, 128), F32),
                pltpu.VMEM((rows + 1, states, width), F32),
                pltpu.VMEM((rows, states, 128), F32),
                pltpu.VMEM((rows, states, 128), F32),
                block, block, block, block,
                pltpu.VMEM((rows, width), BF16),
                pltpu.VMEM((rows, rank), BF16),
            ],
        ),
        out_shape=out_shape,
        input_output_aliases=aliases,
        compiler_params=LIMIT,
        cost_estimate=cost(50),
        name="scan",
    )(*args)


def back(
    order, proj_grad, xproj, mix_grad, inner, before, ahead, conv_weight, conv_bias, rate_sums, scan_sums,
    step_sums, dtproj_grad,
):
    rows, channels = mix_grad.shape
    blocks = order.shape[0]
    seqs = lax.axis_size("seq")
    width = channels // blocks
    thin = width // seqs
    side = min(2, seqs // blocks)
    rank = dtproj_grad.shape[1]

    def part(height):
        return pl.BlockSpec((height, width), lambda q, order: (0, order[q]))

    def tall(columns):
        return pl.BlockSpec((width, columns), lambda q, order: (order[q], 0))

    return pl.pallas_call(
        back_kernel,
        grid_spec=pltpu.PrefetchScalarGridSpec(
            num_scalar_prefetch=1,
            grid=(blocks,),
            in_specs=[
                whole(proj_grad.shape), tall(xproj.shape[1]), part(rows), part(rows), part(8), part(8),
                part(conv_weight.shape[0]), part(1), part(rate_sums.shape[0]), part(8), part(8), tall(rank),
            ],
            out_specs=[part(rows), whole((blocks, seqs + seqs // side, thin, 128))]
            + [whole((rows + 64, width))] * blocks,
            scratch_shapes=[
                pltpu.VMEM((rows + 8, width), F32),
                pltpu.VMEM((rows + 8, width), F32),
                pltpu.VMEM((rows, width), BF16),
            ],
        ),
        out_shape=[
            struct(rows, channels, dtype=BF16), struct(blocks, seqs + seqs // side, thin, 128, dtype=BF16),
        ] + [struct(rows + 64, width, dtype=BF16)] * blocks,
        compiler_params=LIMIT,
        cost_estimate=cost(18),
        name="back",
    )(
        order, proj_grad, xproj, mix_grad, inner, before, ahead, conv_weight, conv_bias, rate_sums,
        scan_sums, step_sums, dtproj_grad,
    )


def cost(micros):
    return pl.CostEstimate(flops=int(micros), transcendentals=0, bytes_accessed=1024)


def places():
    me = lax.axis_index("state")
    core = lax.axis_index("seq") % 2
    return jnp.stack([core] + [me ^ d for d in range(lax.axis_size("state"))]).astype(jnp.int32)


def wide_grads(gates, masked, normed, seqs):
    count = len(gates)
    rows = gates[0].shape[0]
    width = gates[0].shape[1] // 2
    features = masked.shape[1]
    steps = max(1, width // 256)
    high = features // seqs
    chips = seqs // 2
    fixed = pl.BlockSpec((rows, width), lambda i, at: (0, 1))
    part = pl.BlockSpec((rows, width // steps), lambda i, at: (0, i))

    def wholly(d):
        return pl.BlockSpec((rows, features), lambda i, at: (at[d + 1], 0))

    def partly(d):
        return pl.BlockSpec((rows, features // steps), lambda i, at: (at[d + 1], i))

    return pl.pallas_call(
        functools.partial(wide_kernel, high),
        grid_spec=pltpu.PrefetchScalarGridSpec(
            num_scalar_prefetch=1,
            grid=(steps,),
            in_specs=[part] * count + [fixed] * count
            + [wholly(d) for d in range(count)] + [partly(d) for d in range(count)],
            out_specs=[whole((chips * 2 * high, width))] * 2,
        ),
        out_shape=[struct(chips * 2 * high, width)] * 2,
        compiler_params=LIMIT,
        cost_estimate=cost(10),
        name="wide",
    )(places(), *gates, *gates, *([masked] * count), *([normed] * count))


SUM_ROWS = 48


def inner_grads(normed, inners, thins, gain, live, seqs):
    count = len(inners)
    width = inners[0].shape[1]
    features = normed.shape[1]
    rows = normed.shape[0] // count
    steps = max(1, width // 256)
    chips = seqs // 2
    entry = features // seqs + thins[0].shape[1] * 256 // width

    def partly(d):
        return pl.BlockSpec((rows, features // steps), lambda i, at: (at[d + 1], i))

    shape = (chips * entry + SUM_ROWS, width)
    return pl.pallas_call(
        functools.partial(inner_kernel, seqs),
        grid_spec=pltpu.PrefetchScalarGridSpec(
            num_scalar_prefetch=1,
            grid=(steps,),
            in_specs=[partly(d) for d in range(count)]
            + [whole(inners[0].shape)] * count + [whole(thins[0].shape)] * count
            + [whole(gain.shape), pl.BlockSpec(memory_space=pltpu.SMEM)],
            out_specs=[whole(shape)] * 2,
        ),
        out_shape=[struct(*shape)] * 2,
        compiler_params=LIMIT,
        cost_estimate=cost(5),
        name="inner",
    )(places(), *([normed] * count), *inners, *thins, gain, live)


def assemble(wides, lasts, features, channels, seqs, taps, states, proj_width, rank):
    width = wides[0].shape[1]
    count = len(wides)
    rows = channels // seqs
    shapes = [
        (features // seqs, 2 * channels), (rows, features), (rows, proj_width), (rows, rank), (taps, channels),
        (1, channels), (1, channels), (1, channels), (1, channels), (1, channels),
        (states // count, channels), (features // width, width),
    ]
    return pl.pallas_call(
        assemble_kernel,
        in_specs=[pl.BlockSpec(memory_space=pltpu.SMEM)] + [pl.BlockSpec(memory_space=pltpu.VMEM)] * 2 * count,
        out_specs=[pl.BlockSpec(memory_space=pltpu.VMEM)] * len(shapes),
        out_shape=[struct(*shape) for shape in shapes],
        scratch_shapes=[pltpu.VMEM((rows, 256), F32)],
        compiler_params=LIMIT,
        cost_estimate=cost(4),
        name="assemble",
    )(places(), *wides, *lasts)


def dot(a, b, dims):
    return lax.dot_general(a, b, (dims, ((), ())), preferred_element_type=F32)


def body(
    tokens,
    lengths,
    grad_out,
    norm_gain,
    in_weight,
    conv_weight,
    conv_bias,
    xproj_weight,
    dtproj_weight,
    dt_bias,
    a_log,
    d_skip,
    out_weight,
):
    rows, features = tokens.shape
    channels = out_weight.shape[0]
    rank = dtproj_weight.shape[1]
    proj_width = xproj_weight.shape[1]
    states = (proj_width - rank) // 2
    taps = conv_weight.shape[0]
    group = lax.axis_size("state")
    seqs = lax.axis_size("seq")
    member = lax.axis_index("state")
    width = channels // group
    live_rows = jnp.clip(lengths - member * rows, 0, rows)
    alive = (jnp.arange(rows, dtype=jnp.int32) < live_rows[0]).astype(F32)[:, None]
    conv_row = conv_bias[None]
    xproj = jnp.pad(xproj_weight, ((0, 0), (0, 128 - proj_width)))

    a_full = placed(gathered(a_log), 0)
    rate2 = -jnp.exp(a_full) * LOG2E
    cotangent = grad_out.astype(F32)
    masked_low = (cotangent * alive).astype(BF16)
    masked_all = lax.all_gather(masked_low, "state", axis=0, tiled=True)
    inputs = tokens.astype(F32)
    inv_scale = lax.rsqrt(jnp.mean(inputs * inputs, axis=1, keepdims=True) + EPSILON)
    normed = inputs * inv_scale
    normed_low = (normed * norm_gain).astype(BF16)
    inner = jnp.dot(normed_low, in_weight[:, :channels], preferred_element_type=F32).astype(BF16)
    before = shifted(inner[rows - 8 :], "state", 1)
    gate_in = jnp.dot(normed_low, in_weight[:, channels:], preferred_element_type=F32)
    grad_gated = dot(masked_low, out_weight, ((1,), (1,)))
    mixed, proj = front(inner, before, conv_weight, conv_row, xproj, width)
    step, grad_y, sig, stats, state_end, grad_end, cols = local_ends(
        live_rows, proj, dtproj_weight, dt_bias[None], mixed, gate_in, grad_gated, rate2, width
    )

    sums_row = stats[0:8]
    pieces = [jnp.concatenate([state_end, sums_row], axis=0)]
    for d in range(1, group):
        chosen = jnp.where(member < (member ^ d), state_end, grad_end)
        pieces.append(swapped(jnp.concatenate([chosen, sums_row], axis=0), d))
    pieces = jnp.stack(pieces)
    state_in = jnp.zeros((states, channels), F32)
    grad_in = jnp.zeros((states, channels), F32)
    for k in range(group - 1):
        one = lax.dynamic_index_in_dim(pieces, member ^ k, 0, keepdims=False)
        passed = one[:states] + jnp.exp2(rate2 * one[states : states + 1]) * state_in
        state_in = jnp.where(k < member, passed, state_in)
    for k in range(group - 1, 0, -1):
        one = lax.dynamic_index_in_dim(pieces, member ^ k, 0, keepdims=False)
        passed = one[:states] + jnp.exp2(rate2 * one[states : states + 1]) * grad_in
        grad_in = jnp.where(k > member, passed, grad_in)

    normed_late, state_in = lax.optimization_barrier((normed_low, state_in))
    normed_all = lax.all_gather(normed_late, "state", axis=0, tiled=True)

    first = list(range(1, group // 2 + 1))
    second = list(range(group // 2 + 1, group)) + [0]
    call = (cols, proj, rate2, step, mixed, grad_y, sig, gate_in, grad_gated, state_in, grad_in)
    call += (d_skip[None], dtproj_weight)
    one = full_scan(jnp.stack([member ^ d for d in first]), *call, [])
    gates = {d: swapped(one[8 + q], d) for q, d in enumerate(first)}
    shared = [(k, one[k]) for k in (0, 1, 2, 3, 4, 5)]
    two = full_scan(jnp.stack([member ^ d for d in second]), *call, shared)
    gated_low, grad_gate_low, mix_grad, grad_a, scan_sums, grad_dtproj = two[:6]
    first_gates = [gates[d] for d in first]
    *first_gates, grad_rank = lax.optimization_barrier((*first_gates, one[6] + two[6]))
    gates.update(dict(zip(first, first_gates)))
    grad_bc = (one[7] + two[7]).T

    grad_proj = jnp.concatenate(
        [grad_rank, grad_bc, jnp.zeros((rows, 128 - proj_width), F32)], axis=1
    ).astype(BF16)
    window = jnp.concatenate([before, inner[:8]], axis=0).astype(F32)
    head_pre = conv_window(window, conv_weight, conv_row, 8)
    head_squash = jax.nn.sigmoid(head_pre)
    head_mixed = mix_grad[:8] + dot(grad_proj[:8], xproj, ((1,), (1,)))
    head_grad = head_mixed * head_squash * (1.0 + head_pre * (1.0 - head_squash))
    ahead = shifted(head_grad, "state", -1)
    late_sends = [two[8 + q] for q in range(len(second))]
    ahead, *late_sends = lax.optimization_barrier((ahead, *late_sends))
    gates.update({d: swapped(v, d) if d else v for d, v in zip(second, late_sends)})
    order = jnp.stack([member ^ d for d in range(1, group)] + [member])
    grad_inner_low, thin_sends, *inner_sends = back(
        order, grad_proj, xproj, mix_grad, inner, before, ahead, conv_weight, conv_row, grad_a, scan_sums,
        stats, grad_dtproj,
    )
    *last_gates, inner_sends = lax.optimization_barrier((*[gates[d] for d in second], inner_sends))
    gates.update(dict(zip(second, last_gates)))
    inner_pieces = [inner_sends[-1]] + [swapped(v, d + 1) for d, v in enumerate(inner_sends[:-1])]
    thin_pieces = [thin_sends[0]] + [swapped(thin_sends[d], d) for d in range(1, group)]
    fold = features // width
    high = features // seqs
    thin = width // seqs
    thin_rows = thin * 256 // width

    wide = wide_grads([gates[d] for d in range(group)], masked_all, normed_all, seqs)
    wide, _, (inner_pieces, thin_pieces), gated_late = seq_scatter(
        *wide, hold=(inner_pieces, thin_pieces), behind=gated_low
    )
    branch = jnp.dot(gated_late, out_weight, preferred_element_type=F32)
    output = (inputs + alive * branch).astype(BF16)
    owned = to_owner(wide[:high])

    grad_normed = dot(grad_inner_low, in_weight[:, :channels], ((1,), (1,))) + dot(
        grad_gate_low, in_weight[:, channels:], ((1,), (1,))
    )
    gain_part = jnp.sum(grad_normed * normed, axis=0).reshape(fold, width)
    scaled = grad_normed * norm_gain
    grad_tokens = cotangent + inv_scale * (
        scaled - normed * jnp.mean(scaled * normed, axis=1, keepdims=True)
    )

    last = inner_grads(normed_all, inner_pieces, thin_pieces, gain_part, live_rows.astype(F32), seqs)
    last, sums, _, owned = seq_scatter(*last, extra=SUM_ROWS, behind=owned)
    wide_pieces = gathered(jnp.concatenate([owned, wide[high:]], axis=0))
    *wide_pieces, last, sums = lax.optimization_barrier((*wide_pieces, last, sums))
    last = gathered(jnp.concatenate([last, sums], axis=0))

    (
        grad_in_w, grad_out_w, grad_xproj, grad_dtproj, grad_conv, grad_bias, grad_dtb, grad_skip, dt_mean,
        dt_spread, grad_a_log, grad_gain,
    ) = assemble(
        wide_pieces, last, features, channels, seqs, taps, states, proj_width, rank
    )
    return (
        output,
        grad_tokens,
        grad_gain.reshape(features),
        grad_in_w,
        grad_conv,
        grad_bias[0],
        grad_xproj,
        grad_dtproj,
        grad_dtb[0],
        grad_a_log,
        grad_skip[0],
        grad_out_w,
        dt_mean[0],
        dt_spread[0],
    )


def solution(mesh):
    rows = P(("seq", "state"), None)
    return jax.shard_map(
        body,
        mesh=mesh,
        in_specs=(rows, P("seq"), rows) + (P(),) * 7 + (P("state", None), P(), P()),
        out_specs=(rows, rows, P(), P("seq", None), P(), P(), P("seq", None), P("seq", None), P())
        + (P("state", None), P(), P("seq", None), P(), P()),
        check_vma=False,
    )
```

```python
import functools

import jax
import jax.numpy as jnp
from jax import lax
from jax.experimental import pallas as pl
from jax.experimental.pallas import tpu as pltpu
from jax.sharding import PartitionSpec as P

EPSILON = 1e-05
LOG2E = 1.4426950408889634
LN2 = 0.6931471805599453
F32 = jnp.float32
BF16 = jnp.bfloat16
ENDS_ROWS = 64
SCAN_ROWS = 64
BACK_ROWS = 64
WIDE_STEP = 128


def swapped(value, distance):
    count = lax.axis_size("state")
    return lax.ppermute(value, "state", [(i, i ^ distance) for i in range(count)])


def shifted(value, axis, steps):
    count = lax.axis_size(axis)
    leading, last = (max(0, -steps), min(count, count - steps))
    return lax.ppermute(value, axis, [(source, source + steps) for source in range(leading, last)])


def rotated(value, axis, steps):
    count = lax.axis_size(axis)
    return lax.ppermute(value, axis, [(i, (i + steps) % count) for i in range(count)])


def gathered(value):
    count = lax.axis_size("state")
    return [value] + [swapped(value, d) for d in range(1, count)]


def two_words(value):
    high = lax.reduce_precision(value, 8, 7)
    return jnp.concatenate([high.astype(BF16), (value - high).astype(BF16)], axis=0)


def one_word(value):
    count = value.shape[0] // 2
    return value[:count].astype(F32) + value[count:].astype(F32)


def seq_exchange(value, distance):
    count = lax.axis_size("seq")
    return lax.ppermute(value, "seq", [(i, i ^ distance) for i in range(count)])


def seq_scatter(mine, other, extra=0, hold=None, behind=None, late=None):
    seqs = lax.axis_size("seq")
    seq = lax.axis_index("seq")
    width = mine.shape[1]
    total = mine + seq_exchange(other, 1)
    if behind is not None:
        total, behind = lax.optimization_barrier((total, behind))
    chips = seqs // 2
    high = (total.shape[0] - extra) // chips
    total, sums = total[: chips * high], total[chips * high :]
    k = 1
    while chips > 1:
        chips //= 2
        total = total.reshape(chips, 2, high, width)
        bit = (seq >> k) & 1
        kept = lax.dynamic_index_in_dim(total, bit, 1, keepdims=False)
        away = lax.dynamic_index_in_dim(total, 1 - bit, 1, keepdims=False).astype(BF16)
        away = away.reshape(chips * high, width)
        if extra:
            away = jnp.concatenate([away, two_words(sums)], axis=0)
        got = seq_exchange(away, 1 << k)
        total = kept + got[: chips * high].astype(F32).reshape(kept.shape)
        if extra:
            sums = sums + one_word(got[chips * high :])
        if late is not None and k == 1:
            total, late = lax.optimization_barrier((total, late))
        k += 1
    total = total.reshape(high, width)
    if hold is not None:
        total, hold = lax.optimization_barrier((total, hold))
    return total, sums, hold, behind if late is None else late


def to_owner(value):
    seqs = lax.axis_size("seq")
    states = lax.axis_size("state")
    pairs = [(s * states + t, t * seqs + s) for s in range(seqs) for t in range(states)]
    return lax.ppermute(value, ("seq", "state"), pairs)


def placed(pieces, axis, out=None, start=0):
    me = lax.axis_index("state")
    size = pieces[0].shape[axis]
    if out is None:
        shape = list(pieces[0].shape)
        shape[axis] = size * len(pieces)
        out = jnp.zeros(shape, pieces[0].dtype)
    for d, piece in enumerate(pieces):
        out = lax.dynamic_update_slice_in_dim(out, piece, start + (me ^ d) * size, axis)
    return out


def fill_lanes(out_ref, cols_ref, rows):
    groups = 8
    states = cols_ref.shape[0]
    lanes = min(128, rows)

    def step(i, unused):
        tiles = []
        for u in range(groups):
            first = (i * groups + u) * 8
            base = pl.multiple_of((first // lanes) * lanes, lanes)
            tile = cols_ref[:, pl.ds(base, lanes)]
            tiles.append(pltpu.roll(tile, lax.rem(lanes - (first - base), lanes), axis=1))
        for u in range(groups):
            for r in range(8):
                out_ref[(i * groups + u) * 8 + r] = jnp.broadcast_to(
                    tiles[u][:, r : r + 1], (states, 128)
                )
        return 0

    lax.fori_loop(0, rows // (8 * groups), step, 0)


def sums_to_rows(values, sublane):
    step = 1
    while len(values) > 1:
        low = (sublane & step) == 0
        values = [
            jnp.where(low, a, b) + pltpu.roll(jnp.where(low, b, a), step, axis=0)
            for a, b in zip(values[::2], values[1::2])
        ]
        step *= 2
    return values[0]


def spread(ref, row, count):
    return jnp.broadcast_to(ref[pl.ds(row, 1), :], (count, ref.shape[1]))


def widened(value, times):
    return jnp.concatenate([value] * times, axis=1)


def conv_window(window, weight, bias, rows):
    taps = weight.shape[0]
    total = bias + weight[taps - 1 : taps] * window[8:]
    for s in range(1, taps):
        total = total + weight[taps - 1 - s : taps - s] * window[8 - s : 8 - s + rows]
    return total


def logistic(value):
    return 1.0 / (1.0 + jnp.exp(-value))


def rounded_grad(gate, grad_gated):
    return (grad_gated * (gate * logistic(gate))).astype(BF16).astype(F32)


def by_eight(value):
    total = value[0:8]
    for k in range(8, value.shape[0], 8):
        total = total + value[k : k + 8]
    return total


def widen_rows(ext, before, inner):
    rows = inner.shape[0]
    ext[0:8] = before[...].astype(F32)

    def move(i, unused):
        at = pl.multiple_of(i * 32, 32)
        ext[pl.ds(at + 8, 32), :] = inner[pl.ds(at, 32), :].astype(F32)
        return 0

    lax.fori_loop(0, rows // 32, move, 0)


def front_kernel(inner, before, conv_w, conv_b, xproj, mixed_out, proj_out, ext, low):
    rows = inner.shape[0]

    @pl.when(pl.program_id(0) == 0)
    def _():
        proj_out[...] = jnp.zeros_like(proj_out)

    widen_rows(ext, before, inner)
    weight = conv_w[...]
    bias = conv_b[...]

    def chunk(i, unused):
        at = pl.multiple_of(i * BACK_ROWS, BACK_ROWS)
        pre = conv_window(ext[pl.ds(at, BACK_ROWS + 8), :], weight, bias, BACK_ROWS)
        mixed = pre * logistic(pre)
        mixed_out[pl.ds(at, BACK_ROWS), :] = mixed
        low[pl.ds(at, BACK_ROWS), :] = mixed.astype(BF16)
        return 0

    lax.fori_loop(0, rows // BACK_ROWS, chunk, 0)
    proj_out[...] += dot(low[...], xproj[...], ((1,), (1,)))


def ends_kernel(
    live, proj, dtproj, dt_b, mixed, gate, grad_gated, rate,
    step_out, stat_out, state_out, grad_out, cols_out, lanes, drive, rank_low, raised_all, gy_out,
):
    rows, width = mixed.shape
    states = rate.shape[0]
    rank = dtproj.shape[0]
    reps = width // 128

    @pl.when(pl.program_id(0) == 0)
    def _():
        cols_out[...] = jnp.transpose(proj[...])[rank : rank + 2 * states]
        rank_low[...] = proj[:, :rank].astype(BF16)
        fill_lanes(lanes, cols_out, rows)

    raised_all[...] = dt_b[...] + jnp.dot(rank_low[...], dtproj[...], preferred_element_type=F32)
    count = ENDS_ROWS
    zero8 = jnp.zeros((8, width), F32)

    def prepare(i, sums):
        at = pl.ds(pl.multiple_of(i * count, count), count)
        raised = raised_all[at, :]
        small = jnp.exp(-jnp.abs(raised))
        step = jnp.maximum(raised, 0.0) + jnp.log1p(small)
        step_out[at, :] = step
        drive[at, :] = step * mixed[at, :]
        gy_out[at, :] = rounded_grad(gate[at, :], grad_gated[at, :])
        row = i * count + lax.broadcasted_iota(jnp.int32, (count, width), 0)
        seen = jnp.where(row < live[0], step, 0.0)
        return sums[0] + by_eight(step), sums[1] + by_eight(seen), sums[2] + by_eight(seen * step)

    sums = lax.fori_loop(0, rows // count, prepare, (zero8, zero8, zero8))
    stat_out[...] = zero8
    for k in range(3):
        stat_out[k : k + 1, :] = jnp.sum(sums[k], axis=0, keepdims=True)

    rates = rate[...]
    groups = rows // 8

    def body(i, carry):
        state, grad = carry
        for r in range(8):
            p = i * 8 + r
            factor = jnp.exp2(rates * spread(step_out, p, states))
            b_wide = widened(lanes[p, 0:states], reps)
            state = factor * state + spread(drive, p, states) * b_wide
        for r in range(7, -1, -1):
            p = (groups - 1 - i) * 8 + r
            factor = jnp.exp2(rates * spread(step_out, p, states))
            c_wide = widened(lanes[p, states : 2 * states], reps)
            grad = factor * (grad + spread(gy_out, p, states) * c_wide)
        return state, grad

    zero = jnp.zeros((states, width), F32)
    state, grad = lax.fori_loop(0, groups, body, (zero, zero))
    state_out[...] = state
    grad_out[...] = grad


def scan_kernel(
    skipped, order, cols, proj, rate, step, mixed, gate, grad_gated, state_in, grad_in, skip, dtproj,
    *rest,
):
    rest = rest[skipped:]
    gated_out, gate_out, mix_out, rate_out, vec_out, dtproj_out, rank_out, bc_out = rest[:8]
    sends = rest[8:-11]
    (
        lanes, held, b_sum, c_sum, drive, y_sum, decay_sum, source_sum, raised_low, rank_low, grad_y
    ) = rest[-11:]
    rows, width = step.shape
    states = rate.shape[0]
    rank = dtproj.shape[0]
    half = states // 2
    reps = width // 128
    block = pl.program_id(0)

    @pl.when(block == 0)
    def _():
        fill_lanes(lanes, cols, rows)
        rank_low[...] = proj[:, :rank].astype(BF16)
        b_sum[...] = jnp.zeros_like(b_sum)
        c_sum[...] = jnp.zeros_like(c_sum)
        rank_out[...] = jnp.zeros_like(rank_out)

    rates = rate[...]
    groups = rows // 8
    sublane = lax.broadcasted_iota(jnp.int32, (8, width), 0)
    held[0] = state_in[...]

    def forward(i, state):
        parts = []
        row = pl.ds(pl.multiple_of(i * 8, 8), 8)
        drive[row, :] = step[row, :] * mixed[row, :]
        grad_y[row, :] = rounded_grad(gate[row, :], grad_gated[row, :])
        for r in range(8):
            p = i * 8 + r
            factor = jnp.exp2(rates * spread(step, p, states))
            b_wide = widened(lanes[p, 0:states], reps)
            c_wide = widened(lanes[p, states : 2 * states], reps)
            state = factor * state + spread(drive, p, states) * b_wide
            held[p + 1] = state
            seen = state * c_wide
            parts.append(seen[:half] + seen[half:])
        y_sum[row, :] = sums_to_rows(parts, sublane)
        return state

    lax.fori_loop(0, groups, forward, state_in[...])

    def over_tiles(value):
        total = value[:, 0:128]
        for t in range(1, reps):
            total = total + value[:, 128 * t : 128 * t + 128]
        return total

    def backward(k, carry):
        grad_next, rate_sum = carry
        i = groups - 1 - k
        decay_parts = [None] * 8
        source_parts = [None] * 8
        here = held[i * 8 + 8]
        for r in range(7, -1, -1):
            p = i * 8 + r
            step_wide = spread(step, p, states)
            y_wide = spread(grad_y, p, states)
            factor = jnp.exp2(rates * step_wide)
            b_wide = widened(lanes[p, 0:states], reps)
            c_wide = widened(lanes[p, states : 2 * states], reps)
            grad = grad_next + y_wide * c_wide
            before = held[p]
            grad_next = factor * grad
            c_sum[p] += over_tiles(here * y_wide)
            b_sum[p] += over_tiles(grad * spread(drive, p, states))
            through = grad_next * before
            decay = through * rates
            rate_sum = rate_sum + through * step_wide
            source = grad * b_wide
            decay_parts[r] = decay[:half] + decay[half:]
            source_parts[r] = source[:half] + source[half:]
            here = before
        row = pl.ds(pl.multiple_of(i * 8, 8), 8)
        decay_sum[row, :] = sums_to_rows(decay_parts, sublane)
        source_sum[row, :] = sums_to_rows(source_parts, sublane)
        return grad_next, rate_sum

    zero = jnp.zeros((states, width), F32)
    unused, rate_sum = lax.fori_loop(0, groups, backward, (grad_in[...], zero))
    rate_out[...] = rate_sum * (rates * LN2)

    gain = skip[...]
    count = SCAN_ROWS
    zero8 = jnp.zeros((8, width), F32)

    def finish(i, sums):
        at = pl.ds(pl.multiple_of(i * count, count), count)
        value = gate[at, :]
        mix = mixed[at, :]
        upstream = grad_gated[at, :]
        full_y = y_sum[at, :] + gain * mix
        squash = logistic(value)
        act = value * squash
        gated = (full_y * act).astype(BF16)
        grad_gate = (upstream * full_y * squash * (1.0 + value * (1.0 - squash))).astype(BF16)
        gated_out[at, :] = gated
        gate_out[at, :] = grad_gate
        grad_full = upstream * act
        source = source_sum[at, :]
        width_step = step[at, :]
        grad_raised = (LN2 * decay_sum[at, :] + mix * source) * (1.0 - jnp.exp(-width_step))
        raised_low[at, :] = grad_raised.astype(BF16)
        mix_out[at, :] = width_step * source + grad_full * gain
        return sums[0] + by_eight(grad_raised), sums[1] + by_eight(grad_full * mix)

    sums = lax.fori_loop(0, rows // count, finish, (zero8, zero8))
    for d, send in enumerate(sends):

        @pl.when(block == d)
        def _(send=send):
            send[:, 0:width] = gated_out[...]
            send[:, width : 2 * width] = gate_out[...]

    vec_out[...] = zero8
    for k in range(2):
        vec_out[k : k + 1, :] = jnp.sum(sums[k], axis=0, keepdims=True)
    dtproj_out[...] = dot(raised_low[...], rank_low[...], ((0,), (0,)))
    rank_out[...] += dot(raised_low[...], dtproj[...], ((1,), (1,)))

    @pl.when(block == pl.num_programs(0) - 1)
    def _():
        lane = lax.broadcasted_iota(jnp.int32, (states, 128), 1)

        def tile(j, unused):
            def gather(i, carry):
                b_tile, c_tile = carry
                for r in range(16):
                    p = j * 128 + i * 16 + r
                    here = lane == i * 16 + r
                    b_tile = jnp.where(here, jnp.sum(b_sum[p], axis=1, keepdims=True), b_tile)
                    c_tile = jnp.where(here, jnp.sum(c_sum[p], axis=1, keepdims=True), c_tile)
                return b_tile, c_tile

            zero_tile = jnp.zeros((states, 128), F32)
            b_tile, c_tile = lax.fori_loop(0, 8, gather, (zero_tile, zero_tile))
            at = pl.ds(pl.multiple_of(j * 128, 128), 128)
            bc_out[0:states, at] = b_tile
            bc_out[states : 2 * states, at] = c_tile
            return 0

        lax.fori_loop(0, rows // 128, tile, 0)


def back_kernel(
    skipped, order, proj_grad, xproj, mix_grad, inner, before, ahead, conv_w, conv_b, rate_sums, scan_sums, step_sums,
    dtproj_grad, *rest,
):
    thin_before = rest[1] if skipped else None
    inner_out, thin_out, *rest = rest[skipped:]
    sends, (ext, pre_ext, low, mixed_grad) = rest[:-4], rest[-4:]
    rows, width = mix_grad.shape
    taps = conv_w.shape[0]
    states = rate_sums.shape[0]
    block = pl.program_id(0)
    if skipped:

        @pl.when(block == 0)
        def _():
            thin_out[...] = thin_before[...]

    widen_rows(ext, before, inner)
    weight = conv_w[...]
    bias = conv_b[...]
    pre_ext[rows : rows + 8, :] = ahead[...]
    mixed_grad[...] = mix_grad[...] + jnp.dot(proj_grad[...], xproj[...], preferred_element_type=F32)
    zero8 = jnp.zeros((8, width), F32)

    def chunk(i, sums):
        at = pl.multiple_of(i * BACK_ROWS, BACK_ROWS)
        window = ext[pl.ds(at, BACK_ROWS + 8), :]
        pre = conv_window(window, weight, bias, BACK_ROWS)
        squash = logistic(pre)
        low[pl.ds(at, BACK_ROWS), :] = (pre * squash).astype(BF16)
        grad_pre = mixed_grad[pl.ds(at, BACK_ROWS), :] * squash * (1.0 + pre * (1.0 - squash))
        pre_ext[pl.ds(at, BACK_ROWS), :] = grad_pre
        added = [sums[taps] + by_eight(grad_pre)]
        for k in range(taps - 1, -1, -1):
            shift = taps - 1 - k
            added.insert(0, sums[k] + by_eight(grad_pre * window[8 - shift : 8 + BACK_ROWS - shift]))
        return tuple(added)

    sums = lax.fori_loop(0, rows // BACK_ROWS, chunk, (zero8,) * (taps + 1))

    summed = jnp.concatenate(
        [rate_sums[...], scan_sums[0:2, :], step_sums[1:3, :]]
        + [jnp.sum(v, axis=0, keepdims=True) for v in sums]
        + [jnp.zeros((32 - states - 5 - taps, width), F32)],
        axis=0,
    )
    high = summed.astype(BF16)
    words = jnp.concatenate([high, (summed - high.astype(F32)).astype(BF16)], axis=0)

    xproj_grad = dot(low[...], proj_grad[...], ((0,), (0,)))
    xproj_grad = xproj_grad.astype(BF16)
    step_grad = dtproj_grad[...].astype(BF16)
    group, entries, thin, _ = thin_out.shape
    seqs = width // thin
    side = seqs // (entries - seqs)
    me = order[len(sends)]
    for c in range(seqs):
        chunk_index = order[block] * seqs + c
        place = lax.rem(chunk_index, group) ^ me
        thin_out[place, chunk_index // group] = xproj_grad[c * thin : (c + 1) * thin]
    for c in range(0, seqs, side * group):
        for t in range(group):
            parts = [
                step_grad[(c + k * group + t) * thin : (c + k * group + t + 1) * thin] for k in range(side)
            ]
            parts += [jnp.zeros_like(parts[0])] * (2 - side)
            at = (order[block] * seqs + c) // (group * side)
            thin_out[t ^ me, seqs + at] = jnp.concatenate(parts, axis=1)

    def spread_back(i, unused):
        at = pl.multiple_of(i * BACK_ROWS, BACK_ROWS)
        window = pre_ext[pl.ds(at, BACK_ROWS + 8), :]
        total = weight[taps - 1 : taps] * window[0:BACK_ROWS]
        for s in range(1, taps):
            total = total + weight[taps - 1 - s : taps - s] * window[s : s + BACK_ROWS]
        inner_out[pl.ds(at, BACK_ROWS), :] = total.astype(BF16)
        return 0

    lax.fori_loop(0, rows // BACK_ROWS, spread_back, 0)
    for d, send in enumerate(sends):

        @pl.when(block == d)
        def _(send=send):
            send[0:rows, :] = inner_out[...]
            send[rows : rows + 64, :] = words


def put_chunks(targets, total, core, step, entry, high, first_row, fold):
    width = targets[0].shape[1]
    rows = high // fold
    each = total.shape[0] // rows
    for c in range(each):
        first = pl.multiple_of((step * each + c) // 2 * entry, 8) + first_row
        for parity in range(2):

            @pl.when(lax.rem(core + c, 2) == parity)
            def _(parity=parity, first=first, c=c):
                for f in range(fold):
                    targets[parity][pl.ds(first + f * rows, rows), :] = total[
                        c * rows : (c + 1) * rows, f * width : (f + 1) * width
                    ]


def summed_products(lefts, rights):
    total = None
    for left, right in zip(lefts, rights):
        part = dot(left, right, ((0,), (0,)))
        total = part if total is None else total + part
    return total


def wide_kernel(high, at, *refs):
    count = (len(refs) - 2) // 4
    outs, gates, masked, normed = (refs[k * count : (k + 1) * count] for k in range(4))
    targets = refs[-2:]
    width = targets[0].shape[1]
    total = summed_products([r[...] for r in outs], [r[...] for r in masked])
    fold = masked[0].shape[1] // width
    step = pl.program_id(0)
    put_chunks(targets, total, at[0], step, 2 * high, high, 0, fold)
    total = summed_products([r[...] for r in normed], [r[...] for r in gates])
    put_chunks(targets, total, at[0], step, 2 * high, high, high, 1)


def inner_kernel(total_chunks, at, *refs):
    count = (len(refs) - 4) // 3
    normed, inners, thins = (refs[k * count : (k + 1) * count] for k in range(3))
    gain, live = refs[3 * count : 3 * count + 2]
    targets = refs[-2:]
    core = at[0]
    rows = normed[0].shape[0]
    width = inners[0].shape[1]
    entries, thin, _ = thins[0].shape
    columns = 256
    seqs = total_chunks
    side = seqs // (entries - seqs)
    chips = seqs // 2
    extra = 48 if gain.shape[0] <= 8 else 0
    entry = (targets[0].shape[0] - extra) // chips
    packed = thin * columns // width
    high = entry - packed
    step = pl.program_id(0)
    total = summed_products([r[...] for r in normed], [r[0:rows, :] for r in inners])
    each = total.shape[0] // high
    for c in range(each):
        first = pl.multiple_of((step * each + c) // 2 * entry, 8)
        for parity in range(2):

            @pl.when(lax.rem(core + c, 2) == parity)
            def _(parity=parity, first=first, c=c):
                targets[parity][pl.ds(first, high), :] = total[c * high : (c + 1) * high]

    @pl.when(step == 0)
    def _():
        for i in range(seqs):
            value = thins[0][i].astype(F32)
            near = thins[0][seqs + i // side].astype(F32)
            for r in thins[1:]:
                value = value + r[i].astype(F32)
                near = near + r[seqs + i // side].astype(F32)
            at_lane = (i % side) * 64
            near = near[:, at_lane : at_lane + 64]
            value = jnp.concatenate([value, near, jnp.zeros_like(near)], axis=1)
            first = i // 2 * entry + high
            for parity in range(2):

                @pl.when(lax.rem(core + i, 2) == parity)
                def _(parity=parity, first=first, value=value):
                    if columns >= width:
                        for f in range(columns // width):
                            targets[parity][first + f * thin : first + (f + 1) * thin, :] = value[
                                :, f * width : (f + 1) * width
                            ]
                    else:
                        for f in range(width // columns):
                            targets[parity][
                                first : first + packed, f * columns : (f + 1) * columns
                            ] = value[f * packed : (f + 1) * packed]

        sums = None
        for r in inners:
            words = r[rows : rows + 64, :]
            value = words[0:32].astype(F32) + words[32:64].astype(F32)
            sums = value if sums is None else sums + value
        tail = jnp.concatenate(
            [sums, gain[...], jnp.full((extra - 32 - gain.shape[0], width), live[0], F32)], axis=0
        )
        for target in targets:
            target[chips * entry : chips * entry + extra, :] = tail


def assemble_kernel(
    at, *refs
):
    in_out, out_out, xproj_out, dtproj_out, conv_out, bias_out, dtb_out, skip_out, mean_out, spread_out = refs[-13:-3]
    a_out, gain_out, narrow = refs[-3:]
    count = (len(refs) - 13) // 2
    wides, lasts = refs[:count], refs[count : 2 * count]
    high = in_out.shape[0]
    channels = in_out.shape[1] // 2
    width = wides[0].shape[1]
    fold = out_out.shape[1] // width
    strip = high // fold
    thin, columns = narrow.shape[0] // count, narrow.shape[1]
    packed = thin * columns // width
    taps = conv_out.shape[0]
    mine = a_out.shape[0]
    states = mine * count
    rest = None
    for d in range(count):
        them = at[d + 1]
        lanes = pl.ds(pl.multiple_of(them * width, 128), width)
        half = (lasts[d].shape[0] - high) // 2
        words = lasts[d][high : high + half, :].astype(F32) + lasts[d][high + half :, :].astype(F32)
        piece = words[packed:]
        in_out[:, lanes] = lasts[d][0:high, :].astype(F32)
        in_out[:, pl.ds(pl.multiple_of(channels + them * width, 128), width)] = wides[d][
            high : 2 * high, :
        ].astype(F32)
        for f in range(fold):
            rows = pl.ds(pl.multiple_of(them * strip, 8), strip)
            out_out[rows, f * width : (f + 1) * width] = wides[d][f * strip : (f + 1) * strip, :].astype(F32)
        if columns >= width:
            for f in range(columns // width):
                rows = pl.ds(pl.multiple_of(them * thin, 8), thin)
                narrow[rows, f * width : (f + 1) * width] = words[f * thin : (f + 1) * thin]
        else:
            for f in range(width // columns):
                rows = pl.ds(pl.multiple_of(them * thin + f * packed, 8), packed)
                narrow[rows, :] = words[0:packed, f * columns : (f + 1) * columns]
        for k in range(count):

            @pl.when(at[1] == k)
            def _(k=k, lanes=lanes, piece=piece):
                a_out[:, lanes] = piece[k * mine : (k + 1) * mine]

        dtb_out[:, lanes] = piece[states : states + 1]
        skip_out[:, lanes] = piece[states + 1 : states + 2]
        mean_out[:, lanes] = piece[states + 2 : states + 3]
        spread_out[:, lanes] = piece[states + 3 : states + 4]
        conv_out[:, lanes] = piece[states + 4 : states + 4 + taps]
        bias_out[:, lanes] = piece[states + 4 + taps : states + 5 + taps]
        tail = piece[32:48]
        rest = tail if rest is None else rest + tail
    turned = jnp.transpose(narrow[...])
    xproj_out[...] = turned[0 : xproj_out.shape[0]]
    dtproj_out[...] = turned[128 : 128 + dtproj_out.shape[0]]
    for f in range(fold):
        gain_out[:, f * width : (f + 1) * width] = rest[f : f + 1]
    live = rest[fold : fold + 1, 0:1]
    mean = mean_out[...] / live
    spread = spread_out[...] / live - mean * mean + 1e-06
    mean_out[...] = mean
    spread_out[...] = jnp.sqrt(spread)


def struct(*shape, dtype=F32):
    return jax.ShapeDtypeStruct(shape, dtype)


def whole(shape):
    return pl.BlockSpec(shape, lambda *unused: (0,) * len(shape))


LIMIT = pltpu.CompilerParams(vmem_limit_bytes=63 << 20)


def front(inner, before, conv_weight, conv_bias, xproj, width):
    rows, channels = inner.shape

    def part(height):
        return pl.BlockSpec((height, width), lambda q: (0, q))

    return pl.pallas_call(
        front_kernel,
        grid=(channels // width,),
        in_specs=[
            part(rows), part(8), part(conv_weight.shape[0]), part(1),
            part(xproj.shape[0]),
        ],
        out_specs=[part(rows), whole((rows, xproj.shape[0]))],
        out_shape=[struct(rows, channels), struct(rows, xproj.shape[0])],
        scratch_shapes=[pltpu.VMEM((rows + 8, width), F32), pltpu.VMEM((rows, width), BF16)],
        compiler_params=LIMIT,
        cost_estimate=cost(8),
        name="front",
    )(inner, before, conv_weight, conv_bias, xproj)


def local_ends(live, proj, dtproj, dt_bias, mixed, gate, grad_gated, rate, width):
    rows, channels = mixed.shape
    states = rate.shape[0]
    rank = dtproj.shape[0]

    def part(height):
        return pl.BlockSpec((height, width), lambda q: (0, q))

    return pl.pallas_call(
        ends_kernel,
        grid=(channels // width,),
        in_specs=[
            pl.BlockSpec(memory_space=pltpu.SMEM), whole(proj.shape),
            part(rank), part(1), part(rows), part(rows), part(rows), part(states),
        ],
        out_specs=[part(rows)] + [part(8), part(states), part(states), whole((2 * states, rows))],
        out_shape=[struct(rows, channels)]
        + [struct(8, channels), struct(states, channels), struct(states, channels), struct(2 * states, rows)],
        scratch_shapes=[
            pltpu.VMEM((rows, 2 * states, 128), F32),
            pltpu.VMEM((rows, width), F32),
            pltpu.VMEM((rows, rank), BF16),
            pltpu.VMEM((rows, width), F32),
            pltpu.VMEM((rows, width), F32),
        ],
        compiler_params=LIMIT,
        cost_estimate=cost(40),
        name="ends",
    )(live, proj, dtproj, dt_bias, mixed, gate, grad_gated, rate)


def full_scan(
    order, cols, proj, rate, step, mixed, gate, grad_gated, state_in, grad_in, skip, dtproj, earlier,
):
    rows, channels = step.shape
    states = rate.shape[0]
    rank = dtproj.shape[0]
    width = channels // lax.axis_size("state")
    blocks = order.shape[0]

    def part(height):
        return pl.BlockSpec((height, width), lambda q, order: (0, order[q]))

    tall = pl.BlockSpec((width, rank), lambda q, order: (order[q], 0))
    rows_f32 = part(rows)
    in_specs = [
        whole(cols.shape), whole(proj.shape), part(states), rows_f32, rows_f32, rows_f32, rows_f32,
        part(states), part(states), part(1), part(rank),
    ]
    out_specs = [
        part(rows), part(rows), part(rows), part(states), part(8), tall, whole((rows, rank)),
        whole((2 * states, rows)),
    ] + [whole((rows, 2 * width))] * blocks
    out_shape = [
        struct(rows, channels, dtype=BF16), struct(rows, channels, dtype=BF16),
        struct(rows, channels), struct(states, channels),
        struct(8, channels), struct(channels, rank), struct(rows, rank), struct(2 * states, rows),
    ] + [struct(rows, 2 * width, dtype=BF16)] * blocks
    args = [
        order, cols, proj, rate, step, mixed, gate, grad_gated, state_in, grad_in, skip, dtproj,
    ]
    aliases = {}
    for out, value in earlier:
        aliases[len(args)] = out
        args.append(value)
        in_specs.append(pl.BlockSpec(memory_space=pl.ANY))
    block = pltpu.VMEM((rows, width), F32)
    return pl.pallas_call(
        functools.partial(scan_kernel, len(earlier)),
        grid_spec=pltpu.PrefetchScalarGridSpec(
            num_scalar_prefetch=1,
            grid=(blocks,),
            in_specs=in_specs,
            out_specs=out_specs,
            scratch_shapes=[
                pltpu.VMEM((rows, 2 * states, 128), F32),
                pltpu.VMEM((rows + 1, states, width), F32),
                pltpu.VMEM((rows, states, 128), F32),
                pltpu.VMEM((rows, states, 128), F32),
                block, block, block, block,
                pltpu.VMEM((rows, width), BF16),
                pltpu.VMEM((rows, rank), BF16),
                block,
            ],
        ),
        out_shape=out_shape,
        input_output_aliases=aliases,
        compiler_params=LIMIT,
        cost_estimate=cost(50),
        name="scan",
    )(*args)


def back(
    order, proj_grad, xproj, mix_grad, inner, before, ahead, conv_weight, conv_bias, rate_sums, scan_sums,
    step_sums, dtproj_grad, earlier,
):
    rows, channels = mix_grad.shape
    blocks = order.shape[0] - 1
    seqs = lax.axis_size("seq")
    group = lax.axis_size("state")
    width = channels // group
    thin = width // seqs
    side = min(2, seqs // group)
    rank = dtproj_grad.shape[1]

    def part(height):
        return pl.BlockSpec((height, width), lambda q, order: (0, order[q]))

    def tall(columns):
        return pl.BlockSpec((width, columns), lambda q, order: (order[q], 0))

    in_specs = [
        whole(proj_grad.shape), part(xproj.shape[0]), part(rows), part(rows), part(8), part(8),
        part(conv_weight.shape[0]), part(1), part(rate_sums.shape[0]), part(8), part(8), tall(rank),
    ]
    args = [
        order, proj_grad, xproj, mix_grad, inner, before, ahead, conv_weight, conv_bias, rate_sums,
        scan_sums, step_sums, dtproj_grad,
    ]
    aliases = {}
    for out, value in earlier:
        aliases[len(args)] = out
        args.append(value)
        in_specs.append(pl.BlockSpec(memory_space=pl.ANY) if out == 0 else whole(value.shape))
    return pl.pallas_call(
        functools.partial(back_kernel, len(earlier)),
        grid_spec=pltpu.PrefetchScalarGridSpec(
            num_scalar_prefetch=1,
            grid=(blocks,),
            in_specs=in_specs,
            out_specs=[part(rows), whole((group, seqs + seqs // side, thin, 128))]
            + [whole((rows + 64, width))] * blocks,
            scratch_shapes=[
                pltpu.VMEM((rows + 8, width), F32),
                pltpu.VMEM((rows + 8, width), F32),
                pltpu.VMEM((rows, width), BF16),
                pltpu.VMEM((rows, width), F32),
            ],
        ),
        out_shape=[
            struct(rows, channels, dtype=BF16), struct(group, seqs + seqs // side, thin, 128, dtype=BF16),
        ] + [struct(rows + 64, width, dtype=BF16)] * blocks,
        input_output_aliases=aliases,
        compiler_params=LIMIT,
        cost_estimate=cost(18),
        name="back",
    )(*args)


def cost(micros):
    return pl.CostEstimate(flops=int(micros), transcendentals=0, bytes_accessed=1024)


def places():
    me = lax.axis_index("state")
    core = lax.axis_index("seq") % 2
    return jnp.stack([core] + [me ^ d for d in range(lax.axis_size("state"))]).astype(jnp.int32)


def wide_grads(gates, masked, normed, seqs):
    count = len(gates)
    rows = gates[0].shape[0]
    width = gates[0].shape[1] // 2
    features = masked[0].shape[1]
    steps = max(1, width // WIDE_STEP)
    high = features // seqs
    chips = seqs // 2
    fixed = pl.BlockSpec((rows, width), lambda i, at: (0, 1))
    part = pl.BlockSpec((rows, width // steps), lambda i, at: (0, i))

    wholly = pl.BlockSpec((rows, features), lambda i, at: (0, 0))
    partly = pl.BlockSpec((rows, features // steps), lambda i, at: (0, i))
    return pl.pallas_call(
        functools.partial(wide_kernel, high),
        grid_spec=pltpu.PrefetchScalarGridSpec(
            num_scalar_prefetch=1,
            grid=(steps,),
            in_specs=[part] * count + [fixed] * count
            + [wholly] * count + [partly] * count,
            out_specs=[whole((chips * 2 * high, width))] * 2,
        ),
        out_shape=[struct(chips * 2 * high, width)] * 2,
        compiler_params=LIMIT,
        cost_estimate=cost(10),
        name="wide",
    )(places(), *gates, *gates, *masked, *normed)


SUM_ROWS = 48


def inner_grads(normed, inners, thins, gain, live, seqs):
    count = len(inners)
    width = inners[0].shape[1]
    rows, features = normed[0].shape
    steps = max(1, width // WIDE_STEP)
    chips = seqs // 2
    entry = features // seqs + thins[0].shape[1] * 256 // width

    partly = pl.BlockSpec((rows, features // steps), lambda i, at: (0, i))
    shape = (chips * entry + SUM_ROWS, width)
    return pl.pallas_call(
        functools.partial(inner_kernel, seqs),
        grid_spec=pltpu.PrefetchScalarGridSpec(
            num_scalar_prefetch=1,
            grid=(steps,),
            in_specs=[partly] * count
            + [whole(inners[0].shape)] * count + [whole(thins[0].shape)] * count
            + [whole(gain.shape), pl.BlockSpec(memory_space=pltpu.SMEM)],
            out_specs=[whole(shape)] * 2,
        ),
        out_shape=[struct(*shape)] * 2,
        compiler_params=LIMIT,
        cost_estimate=cost(5),
        name="inner",
    )(places(), *normed, *inners, *thins, gain, live)


def assemble(wides, lasts, features, channels, seqs, taps, states, proj_width, rank):
    width = wides[0].shape[1]
    count = len(wides)
    rows = channels // seqs
    shapes = [
        (features // seqs, 2 * channels), (rows, features), (proj_width, rows), (rank, rows), (taps, channels),
        (1, channels), (1, channels), (1, channels), (1, channels), (1, channels),
        (states // count, channels), (1, features),
    ]
    return pl.pallas_call(
        assemble_kernel,
        in_specs=[pl.BlockSpec(memory_space=pltpu.SMEM)] + [pl.BlockSpec(memory_space=pltpu.VMEM)] * 2 * count,
        out_specs=[pl.BlockSpec(memory_space=pltpu.VMEM)] * len(shapes),
        out_shape=[struct(*shape) for shape in shapes],
        scratch_shapes=[pltpu.VMEM((rows, 256), F32)],
        compiler_params=LIMIT,
        cost_estimate=cost(4),
        name="assemble",
    )(places(), *wides, *lasts)


def dot(a, b, dims):
    return lax.dot_general(a, b, (dims, ((), ())), preferred_element_type=F32)


def body(
    tokens,
    lengths,
    grad_out,
    norm_gain,
    in_weight,
    conv_weight,
    conv_bias,
    xproj_weight,
    dtproj_weight,
    dt_bias,
    a_log,
    d_skip,
    out_weight,
):
    rows, features = tokens.shape
    channels = out_weight.shape[0]
    rank = dtproj_weight.shape[1]
    proj_width = xproj_weight.shape[1]
    states = (proj_width - rank) // 2
    taps = conv_weight.shape[0]
    group = lax.axis_size("state")
    seqs = lax.axis_size("seq")
    member = lax.axis_index("state")
    width = channels // group
    live_rows = jnp.clip(lengths - member * rows, 0, rows)
    alive = (jnp.arange(rows, dtype=jnp.int32) < live_rows[0]).astype(F32)[:, None]
    conv_row = conv_bias[None]
    xproj = jnp.pad(xproj_weight.T, ((0, 128 - proj_width), (0, 0)))

    a_full = placed(gathered(a_log), 0)
    rate2 = -jnp.exp(a_full) * LOG2E
    cotangent = grad_out.astype(F32)
    masked_low = (cotangent * alive).astype(BF16)
    inputs = tokens.astype(F32)
    inv_scale = lax.rsqrt(jnp.mean(inputs * inputs, axis=1, keepdims=True) + EPSILON)
    normed = inputs * inv_scale
    normed_low = (normed * norm_gain).astype(BF16)
    inner = jnp.dot(normed_low, in_weight[:, :channels], preferred_element_type=F32).astype(BF16)
    before = shifted(inner[rows - 8 :], "state", 1)
    gate_in = jnp.dot(normed_low, in_weight[:, channels:], preferred_element_type=F32)
    grad_gated = dot(masked_low, out_weight, ((1,), (1,)))
    mixed, proj = front(inner, before, conv_weight, conv_row, xproj, width)

    near = [d for d in range(1, group) if d & (d - 1) == 0]
    normed_late, mixed = lax.optimization_barrier((normed_low, mixed))
    normed_near = [swapped(normed_late, d) for d in near]
    step, stats, state_end, grad_end, cols = local_ends(
        live_rows, proj, dtproj_weight.T, dt_bias[None], mixed, gate_in, grad_gated, rate2, width
    )
    *normed_near, state_end = lax.optimization_barrier((*normed_near, state_end))
    normed_pieces = {0: normed_low, **dict(zip(near, normed_near))}

    sums_row = stats[0:8]
    pieces = [jnp.concatenate([state_end, sums_row], axis=0)]
    for d in range(1, group):
        chosen = jnp.where(member < (member ^ d), state_end, grad_end)
        pieces.append(swapped(jnp.concatenate([chosen, sums_row], axis=0), d))
    pieces = jnp.stack(pieces)
    state_in = jnp.zeros((states, channels), F32)
    grad_in = jnp.zeros((states, channels), F32)
    for k in range(group - 1):
        one = lax.dynamic_index_in_dim(pieces, member ^ k, 0, keepdims=False)
        passed = one[:states] + jnp.exp2(rate2 * one[states : states + 1]) * state_in
        state_in = jnp.where(k < member, passed, state_in)
    for k in range(group - 1, 0, -1):
        one = lax.dynamic_index_in_dim(pieces, member ^ k, 0, keepdims=False)
        passed = one[:states] + jnp.exp2(rate2 * one[states : states + 1]) * grad_in
        grad_in = jnp.where(k > member, passed, grad_in)

    masked_late, state_in = lax.optimization_barrier((masked_low, state_in))
    masked_pieces = gathered(masked_late)

    first = list(range(1, group // 2 + 1))
    second = list(range(group // 2 + 1, group)) + [0]
    call = (cols, proj, rate2, step, mixed, gate_in, grad_gated, state_in, grad_in)
    call += (d_skip[None], dtproj_weight.T)
    one = list(full_scan(jnp.stack([member ^ d for d in first]), *call, []))
    *masked_pieces, normed_late, one[0] = lax.optimization_barrier((*masked_pieces, normed_low, one[0]))
    normed_pieces.update({d: swapped(normed_late, d) for d in range(1, group) if d not in near})
    normed_pieces = [normed_pieces[d] for d in range(group)]
    gates = {d: swapped(one[8 + q], d) for q, d in enumerate(first)}
    shared = [(k, one[k]) for k in (0, 1, 2, 3, 4, 5)]
    two = full_scan(jnp.stack([member ^ d for d in second]), *call, shared)
    gated_low, grad_gate_low, mix_grad, grad_a, scan_sums, grad_dtproj = two[:6]
    first_gates = [gates[d] for d in first]
    *first_gates, grad_rank = lax.optimization_barrier((*first_gates, one[6] + two[6]))
    gates.update(dict(zip(first, first_gates)))
    grad_bc = (one[7] + two[7]).T

    grad_proj = jnp.concatenate(
        [grad_rank, grad_bc, jnp.zeros((rows, 128 - proj_width), F32)], axis=1
    ).astype(BF16)
    window = jnp.concatenate([before, inner[:8]], axis=0).astype(F32)
    head_pre = conv_window(window, conv_weight, conv_row, 8)
    head_squash = jax.nn.sigmoid(head_pre)
    head_mixed = mix_grad[:8] + jnp.dot(grad_proj[:8], xproj, preferred_element_type=F32)
    head_grad = head_mixed * head_squash * (1.0 + head_pre * (1.0 - head_squash))
    ahead = shifted(head_grad, "state", -1)
    late_sends = [two[8 + q] for q in range(len(second))]
    ahead, normed_pieces, *late_sends = lax.optimization_barrier((ahead, normed_pieces, *late_sends))
    gates.update({d: swapped(v, d) if d else v for d, v in zip(second, late_sends)})
    call = (grad_proj, xproj, mix_grad, inner, before, ahead, conv_weight, conv_row, grad_a, scan_sums, stats)
    call += (grad_dtproj,)
    one = back(jnp.stack([member ^ d for d in first] + [member]), *call, [])
    inner_pieces = {d: swapped(one[2 + q], d) for q, d in enumerate(first)}
    two = back(jnp.stack([member ^ d for d in second] + [member]), *call, [(0, one[0]), (1, one[1])])
    grad_inner_low, thin_sends = two[:2]
    inner_pieces.update({d: swapped(two[2 + q], d) if d else two[2 + q] for q, d in enumerate(second)})
    thin_pieces = [thin_sends[0]] + [swapped(thin_sends[d], d) for d in range(1, group)]
    arrived = [inner_pieces[d] for d in first]
    gates, arrived, thin_sends = lax.optimization_barrier((gates, arrived, thin_sends))
    inner_pieces.update(dict(zip(first, arrived)))
    inner_pieces = [inner_pieces[d] for d in range(group)]
    fold = features // width
    high = features // seqs
    thin = width // seqs
    thin_rows = thin * 256 // width

    wide = wide_grads([gates[d] for d in range(group)], masked_pieces, normed_pieces, seqs)
    wide, _, (inner_pieces, thin_pieces), (gated_late, grad_gate_low) = seq_scatter(
        *wide, hold=(inner_pieces, thin_pieces), late=(gated_low, grad_gate_low)
    )
    branch = jnp.dot(gated_late, out_weight, preferred_element_type=F32)
    output = (inputs + alive * branch).astype(BF16)
    wide = wide.astype(BF16)
    owned = to_owner(wide[:high])

    grad_normed = dot(grad_inner_low, in_weight[:, :channels], ((1,), (1,))) + dot(
        grad_gate_low, in_weight[:, channels:], ((1,), (1,))
    )
    gain_part = jnp.sum(grad_normed * normed, axis=0).reshape(fold, width)
    scaled = grad_normed * norm_gain
    grad_tokens = cotangent + inv_scale * (
        scaled - normed * jnp.mean(scaled * normed, axis=1, keepdims=True)
    )

    last = inner_grads(normed_pieces, inner_pieces, thin_pieces, gain_part, live_rows.astype(F32), seqs)
    last, sums, _, owned = seq_scatter(*last, extra=SUM_ROWS, late=owned)
    wide_pieces = gathered(jnp.concatenate([owned, wide[high:]], axis=0))
    *wide_pieces, last, sums = lax.optimization_barrier((*wide_pieces, last, sums))
    words = two_words(jnp.concatenate([last[high:], sums], axis=0))
    last = gathered(jnp.concatenate([last[:high].astype(BF16), words], axis=0))

    (
        grad_in_w, grad_out_w, grad_xproj, grad_dtproj, grad_conv, grad_bias, grad_dtb, grad_skip, dt_mean,
        dt_spread, grad_a_log, grad_gain,
    ) = assemble(
        wide_pieces, last, features, channels, seqs, taps, states, proj_width, rank
    )
    return (
        output,
        grad_tokens,
        grad_gain[0],
        grad_in_w,
        grad_conv,
        grad_bias[0],
        grad_xproj.T,
        grad_dtproj.T,
        grad_dtb[0],
        grad_a_log,
        grad_skip[0],
        grad_out_w,
        dt_mean[0],
        dt_spread[0],
    )


def solution(mesh):
    rows = P(("seq", "state"), None)
    return jax.shard_map(
        body,
        mesh=mesh,
        in_specs=(rows, P("seq"), rows) + (P(),) * 7 + (P("state", None), P(), P()),
        out_specs=(rows, rows, P(), P("seq", None), P(), P(), P("seq", None), P("seq", None), P())
        + (P("state", None), P(), P("seq", None), P(), P()),
        check_vma=False,
    )
```

```python
import functools

import jax
import jax.numpy as jnp
from jax import lax
from jax.experimental import pallas as pl
from jax.experimental.pallas import tpu as pltpu
from jax.sharding import PartitionSpec as P

EPSILON = 1e-05
LOG2E = 1.4426950408889634
LN2 = 0.6931471805599453
F32 = jnp.float32
BF16 = jnp.bfloat16
ENDS_ROWS = 64
SCAN_ROWS = 64
BACK_ROWS = 64
WIDE_STEP = 128


def swapped(value, distance):
    count = lax.axis_size("state")
    return lax.ppermute(value, "state", [(i, i ^ distance) for i in range(count)])


def shifted(value, axis, steps):
    count = lax.axis_size(axis)
    leading, last = (max(0, -steps), min(count, count - steps))
    return lax.ppermute(value, axis, [(source, source + steps) for source in range(leading, last)])


def rotated(value, axis, steps):
    count = lax.axis_size(axis)
    return lax.ppermute(value, axis, [(i, (i + steps) % count) for i in range(count)])


def gathered(value):
    count = lax.axis_size("state")
    return [value] + [swapped(value, d) for d in range(1, count)]


def two_words(value):
    high = lax.reduce_precision(value, 8, 7)
    return jnp.concatenate([high.astype(BF16), (value - high).astype(BF16)], axis=0)


def one_word(value):
    count = value.shape[0] // 2
    return value[:count].astype(F32) + value[count:].astype(F32)


def seq_exchange(value, distance):
    count = lax.axis_size("seq")
    return lax.ppermute(value, "seq", [(i, i ^ distance) for i in range(count)])


def seq_scatter(mine, other, extra=0, hold=None, behind=None, late=None):
    seqs = lax.axis_size("seq")
    seq = lax.axis_index("seq")
    width = mine.shape[1]
    total = mine + seq_exchange(other, 1)
    if behind is not None:
        total, behind = lax.optimization_barrier((total, behind))
    chips = seqs // 2
    high = (total.shape[0] - extra) // chips
    total, sums = total[: chips * high], total[chips * high :]
    k = 1
    while chips > 1:
        chips //= 2
        total = total.reshape(chips, 2, high, width)
        bit = (seq >> k) & 1
        kept = lax.dynamic_index_in_dim(total, bit, 1, keepdims=False)
        away = lax.dynamic_index_in_dim(total, 1 - bit, 1, keepdims=False).astype(BF16)
        away = away.reshape(chips * high, width)
        if extra:
            away = jnp.concatenate([away, two_words(sums)], axis=0)
        got = seq_exchange(away, 1 << k)
        total = kept + got[: chips * high].astype(F32).reshape(kept.shape)
        if extra:
            sums = sums + one_word(got[chips * high :])
        if late is not None and k == 1:
            total, late = lax.optimization_barrier((total, late))
        k += 1
    total = total.reshape(high, width)
    if hold is not None:
        total, hold = lax.optimization_barrier((total, hold))
    return total, sums, hold, behind if late is None else late


def to_owner(value):
    seqs = lax.axis_size("seq")
    states = lax.axis_size("state")
    there = [(s * states + t, s * states + (t ^ (s % states))) for s in range(seqs) for t in range(states)]
    value = lax.ppermute(value, ("seq", "state"), there)
    pairs = [
        (s * states + (t ^ (s % states)), (t * seqs + s) // states * states + (t ^ (s % states)))
        for s in range(seqs)
        for t in range(states)
    ]
    return lax.ppermute(value, ("seq", "state"), pairs)


def placed(pieces, axis, out=None, start=0):
    me = lax.axis_index("state")
    size = pieces[0].shape[axis]
    if out is None:
        shape = list(pieces[0].shape)
        shape[axis] = size * len(pieces)
        out = jnp.zeros(shape, pieces[0].dtype)
    for d, piece in enumerate(pieces):
        out = lax.dynamic_update_slice_in_dim(out, piece, start + (me ^ d) * size, axis)
    return out


def fill_lanes(out_ref, cols_ref, rows):
    groups = min(16, rows // 8)
    states = cols_ref.shape[0]
    lanes = min(128, rows)

    def step(i, unused):
        tiles = []
        for u in range(groups):
            first = (i * groups + u) * 8
            base = pl.multiple_of((first // lanes) * lanes, lanes)
            tile = cols_ref[:, pl.ds(base, lanes)]
            tiles.append(pltpu.roll(tile, lax.rem(lanes - (first - base), lanes), axis=1))
        for u in range(groups):
            for r in range(8):
                out_ref[(i * groups + u) * 8 + r] = jnp.broadcast_to(
                    tiles[u][:, r : r + 1], (states, 128)
                )
        return 0

    lax.fori_loop(0, rows // (8 * groups), step, 0)


def sums_to_rows(values, sublane):
    step = 1
    while len(values) > 1:
        low = (sublane & step) == 0
        values = [
            jnp.where(low, a, b) + pltpu.roll(jnp.where(low, b, a), step, axis=0)
            for a, b in zip(values[::2], values[1::2])
        ]
        step *= 2
    return values[0]


def spread(ref, row, count):
    return jnp.broadcast_to(ref[pl.ds(row, 1), :], (count, ref.shape[1]))


def widened(value, times):
    return jnp.concatenate([value] * times, axis=1)


def conv_window(window, weight, bias, rows):
    taps = weight.shape[0]
    total = bias + weight[taps - 1 : taps] * window[8:]
    for s in range(1, taps):
        total = total + weight[taps - 1 - s : taps - s] * window[8 - s : 8 - s + rows]
    return total


def logistic(value):
    return 1.0 / (1.0 + jnp.exp(-value))


def rounded_grad(gate, grad_gated):
    return (grad_gated * (gate * logistic(gate))).astype(BF16).astype(F32)


def by_eight(value):
    total = value[0:8]
    for k in range(8, value.shape[0], 8):
        total = total + value[k : k + 8]
    return total


def widen_rows(ext, before, inner):
    rows = inner.shape[0]
    ext[0:8] = before[...].astype(F32)

    def move(i, unused):
        at = pl.multiple_of(i * 32, 32)
        ext[pl.ds(at + 8, 32), :] = inner[pl.ds(at, 32), :].astype(F32)
        return 0

    lax.fori_loop(0, rows // 32, move, 0)


def front_kernel(inner, before, conv_w, conv_b, xproj, mixed_out, proj_out, ext, low):
    rows = inner.shape[0]

    @pl.when(pl.program_id(0) == 0)
    def _():
        proj_out[...] = jnp.zeros_like(proj_out)

    widen_rows(ext, before, inner)
    weight = conv_w[...]
    bias = conv_b[...]

    def chunk(i, unused):
        at = pl.multiple_of(i * BACK_ROWS, BACK_ROWS)
        pre = conv_window(ext[pl.ds(at, BACK_ROWS + 8), :], weight, bias, BACK_ROWS)
        mixed = pre * logistic(pre)
        mixed_out[pl.ds(at, BACK_ROWS), :] = mixed
        low[pl.ds(at, BACK_ROWS), :] = mixed.astype(BF16)
        return 0

    lax.fori_loop(0, rows // BACK_ROWS, chunk, 0)
    proj_out[...] += dot(low[...], xproj[...], ((1,), (1,)))


def ends_kernel(
    live, proj, dtproj, dt_b, mixed, gate, grad_gated, rate,
    step_out, stat_out, state_out, grad_out, cols_out, *rest,
):
    rows, width = mixed.shape
    states = rate.shape[0]
    rank = dtproj.shape[0]
    reps = width // 128
    messages, (lanes, drive, rank_low, raised_all, gy_out) = rest[:-5], rest[-5:]

    @pl.when(pl.program_id(0) == 0)
    def _():
        cols_out[...] = jnp.transpose(proj[...])[rank : rank + 2 * states]
        rank_low[...] = proj[:, :rank].astype(BF16)
        fill_lanes(lanes, cols_out, rows)

    raised_all[...] = dt_b[...] + jnp.dot(rank_low[...], dtproj[...], preferred_element_type=F32)
    count = ENDS_ROWS
    zero8 = jnp.zeros((8, width), F32)

    def prepare(i, sums):
        at = pl.ds(pl.multiple_of(i * count, count), count)
        raised = raised_all[at, :]
        small = jnp.exp(-jnp.abs(raised))
        step = jnp.maximum(raised, 0.0) + jnp.log1p(small)
        step_out[at, :] = step
        drive[at, :] = step * mixed[at, :]
        gy_out[at, :] = rounded_grad(gate[at, :], grad_gated[at, :])
        row = i * count + lax.broadcasted_iota(jnp.int32, (count, width), 0)
        seen = jnp.where(row < live[0], step, 0.0)
        return sums[0] + by_eight(step), sums[1] + by_eight(seen), sums[2] + by_eight(seen * step)

    sums = lax.fori_loop(0, rows // count, prepare, (zero8, zero8, zero8))
    stat_out[...] = zero8
    for k in range(3):
        stat_out[k : k + 1, :] = jnp.sum(sums[k], axis=0, keepdims=True)

    rates = rate[...]
    groups = rows // 8

    def body(i, carry):
        state, grad = carry
        for r in range(8):
            p = i * 8 + r
            factor = jnp.exp2(rates * spread(step_out, p, states))
            b_wide = widened(lanes[p, 0:states], reps)
            state = factor * state + spread(drive, p, states) * b_wide
        for r in range(7, -1, -1):
            p = (groups - 1 - i) * 8 + r
            factor = jnp.exp2(rates * spread(step_out, p, states))
            c_wide = widened(lanes[p, states : 2 * states], reps)
            grad = factor * (grad + spread(gy_out, p, states) * c_wide)
        return state, grad

    zero = jnp.zeros((states, width), F32)
    state, grad = lax.fori_loop(0, groups, body, (zero, zero))
    state_out[...] = state
    grad_out[...] = grad
    for d, message in enumerate(messages):
        message[0:states, :] = jnp.where(live[1] < (live[1] ^ (d + 1)), state, grad)
        message[states : states + 8, :] = stat_out[...]


def scan_kernel(
    skipped, order, cols, proj, rate, step, mixed, gate, grad_gated, state_in, grad_in, skip, dtproj,
    *rest,
):
    rest = rest[skipped:]
    gated_out, gate_out, mix_out, rate_out, vec_out, dtproj_out, rank_out, bc_out = rest[:8]
    sends = rest[8:-11]
    (
        lanes, held, b_sum, c_sum, drive, y_sum, decay_sum, source_sum, raised_low, rank_low, grad_y
    ) = rest[-11:]
    rows, width = step.shape
    states = rate.shape[0]
    rank = dtproj.shape[0]
    half = states // 2
    reps = width // 128
    block = pl.program_id(0)

    @pl.when(block == 0)
    def _():
        fill_lanes(lanes, cols, rows)
        rank_low[...] = proj[:, :rank].astype(BF16)
        b_sum[...] = jnp.zeros_like(b_sum)
        c_sum[...] = jnp.zeros_like(c_sum)
        rank_out[...] = jnp.zeros_like(rank_out)

    rates = rate[...]
    groups = rows // 8
    sublane = lax.broadcasted_iota(jnp.int32, (8, width), 0)
    held[0] = state_in[...]

    def forward(i, state):
        parts = []
        row = pl.ds(pl.multiple_of(i * 8, 8), 8)
        drive[row, :] = step[row, :] * mixed[row, :]
        grad_y[row, :] = rounded_grad(gate[row, :], grad_gated[row, :])
        for r in range(8):
            p = i * 8 + r
            factor = jnp.exp2(rates * spread(step, p, states))
            b_wide = widened(lanes[p, 0:states], reps)
            c_wide = widened(lanes[p, states : 2 * states], reps)
            state = factor * state + spread(drive, p, states) * b_wide
            held[p + 1] = state
            seen = state * c_wide
            parts.append(seen[:half] + seen[half:])
        y_sum[row, :] = sums_to_rows(parts, sublane)
        return state

    lax.fori_loop(0, groups, forward, state_in[...])

    def over_tiles(value):
        total = value[:, 0:128]
        for t in range(1, reps):
            total = total + value[:, 128 * t : 128 * t + 128]
        return total

    def backward(k, carry):
        grad_next, rate_sum = carry
        i = groups - 1 - k
        decay_parts = [None] * 8
        source_parts = [None] * 8
        here = held[i * 8 + 8]
        for r in range(7, -1, -1):
            p = i * 8 + r
            step_wide = spread(step, p, states)
            y_wide = spread(grad_y, p, states)
            factor = jnp.exp2(rates * step_wide)
            b_wide = widened(lanes[p, 0:states], reps)
            c_wide = widened(lanes[p, states : 2 * states], reps)
            grad = grad_next + y_wide * c_wide
            before = held[p]
            grad_next = factor * grad
            c_sum[p] += over_tiles(here * y_wide)
            b_sum[p] += over_tiles(grad * spread(drive, p, states))
            through = grad_next * before
            decay = through * rates
            rate_sum = rate_sum + through * step_wide
            source = grad * b_wide
            decay_parts[r] = decay[:half] + decay[half:]
            source_parts[r] = source[:half] + source[half:]
            here = before
        row = pl.ds(pl.multiple_of(i * 8, 8), 8)
        decay_sum[row, :] = sums_to_rows(decay_parts, sublane)
        source_sum[row, :] = sums_to_rows(source_parts, sublane)
        return grad_next, rate_sum

    zero = jnp.zeros((states, width), F32)
    unused, rate_sum = lax.fori_loop(0, groups, backward, (grad_in[...], zero))
    rate_out[...] = rate_sum * (rates * LN2)

    gain = skip[...]
    count = SCAN_ROWS
    zero8 = jnp.zeros((8, width), F32)

    def finish(i, sums):
        at = pl.ds(pl.multiple_of(i * count, count), count)
        value = gate[at, :]
        mix = mixed[at, :]
        upstream = grad_gated[at, :]
        full_y = y_sum[at, :] + gain * mix
        squash = logistic(value)
        act = value * squash
        gated = (full_y * act).astype(BF16)
        grad_gate = (upstream * full_y * squash * (1.0 + value * (1.0 - squash))).astype(BF16)
        gated_out[at, :] = gated
        gate_out[at, :] = grad_gate
        grad_full = upstream * act
        source = source_sum[at, :]
        width_step = step[at, :]
        grad_raised = (LN2 * decay_sum[at, :] + mix * source) * (1.0 - jnp.exp(-width_step))
        raised_low[at, :] = grad_raised.astype(BF16)
        mix_out[at, :] = width_step * source + grad_full * gain
        return sums[0] + by_eight(grad_raised), sums[1] + by_eight(grad_full * mix)

    sums = lax.fori_loop(0, rows // count, finish, (zero8, zero8))
    for d, send in enumerate(sends):

        @pl.when(block == d)
        def _(send=send):
            send[:, 0:width] = gated_out[...]
            send[:, width : 2 * width] = gate_out[...]

    vec_out[...] = zero8
    for k in range(2):
        vec_out[k : k + 1, :] = jnp.sum(sums[k], axis=0, keepdims=True)
    dtproj_out[...] = dot(raised_low[...], rank_low[...], ((0,), (0,)))
    rank_out[...] += dot(raised_low[...], dtproj[...], ((1,), (1,)))

    @pl.when(block == pl.num_programs(0) - 1)
    def _():
        lane = lax.broadcasted_iota(jnp.int32, (states, 128), 1)

        def tile(j, unused):
            def gather(i, carry):
                b_tile, c_tile = carry
                for r in range(16):
                    p = j * 128 + i * 16 + r
                    here = lane == i * 16 + r
                    b_tile = jnp.where(here, jnp.sum(b_sum[p], axis=1, keepdims=True), b_tile)
                    c_tile = jnp.where(here, jnp.sum(c_sum[p], axis=1, keepdims=True), c_tile)
                return b_tile, c_tile

            zero_tile = jnp.zeros((states, 128), F32)
            b_tile, c_tile = lax.fori_loop(0, 8, gather, (zero_tile, zero_tile))
            at = pl.ds(pl.multiple_of(j * 128, 128), 128)
            bc_out[0:states, at] = b_tile
            bc_out[states : 2 * states, at] = c_tile
            return 0

        lax.fori_loop(0, rows // 128, tile, 0)


def back_kernel(
    skipped, order, proj_grad, xproj, mix_grad, inner, before, ahead, conv_w, conv_b, rate_sums, scan_sums, step_sums,
    dtproj_grad, *rest,
):
    thin_before = rest[1] if skipped else None
    inner_out, thin_out, *rest = rest[skipped:]
    sends, (ext, pre_ext, low, mixed_grad) = rest[:-4], rest[-4:]
    rows, width = mix_grad.shape
    taps = conv_w.shape[0]
    states = rate_sums.shape[0]
    block = pl.program_id(0)
    if skipped:

        @pl.when(block == 0)
        def _():
            thin_out[...] = thin_before[...]

    widen_rows(ext, before, inner)
    weight = conv_w[...]
    bias = conv_b[...]
    pre_ext[rows : rows + 8, :] = ahead[...]
    mixed_grad[...] = mix_grad[...] + jnp.dot(proj_grad[...], xproj[...], preferred_element_type=F32)
    zero8 = jnp.zeros((8, width), F32)

    def chunk(i, sums):
        at = pl.multiple_of(i * BACK_ROWS, BACK_ROWS)
        window = ext[pl.ds(at, BACK_ROWS + 8), :]
        pre = conv_window(window, weight, bias, BACK_ROWS)
        squash = logistic(pre)
        low[pl.ds(at, BACK_ROWS), :] = (pre * squash).astype(BF16)
        grad_pre = mixed_grad[pl.ds(at, BACK_ROWS), :] * squash * (1.0 + pre * (1.0 - squash))
        pre_ext[pl.ds(at, BACK_ROWS), :] = grad_pre
        added = [sums[taps] + by_eight(grad_pre)]
        for k in range(taps - 1, -1, -1):
            shift = taps - 1 - k
            added.insert(0, sums[k] + by_eight(grad_pre * window[8 - shift : 8 + BACK_ROWS - shift]))
        return tuple(added)

    sums = lax.fori_loop(0, rows // BACK_ROWS, chunk, (zero8,) * (taps + 1))

    summed = jnp.concatenate(
        [rate_sums[...], scan_sums[0:2, :], step_sums[1:3, :]]
        + [jnp.sum(v, axis=0, keepdims=True) for v in sums]
        + [jnp.zeros((32 - states - 5 - taps, width), F32)],
        axis=0,
    )
    high = summed.astype(BF16)
    words = jnp.concatenate([high, (summed - high.astype(F32)).astype(BF16)], axis=0)

    xproj_grad = dot(low[...], proj_grad[...], ((0,), (0,)))
    xproj_grad = xproj_grad.astype(BF16)
    step_grad = dtproj_grad[...].astype(BF16)
    group, entries, thin, _ = thin_out.shape
    seqs = width // thin
    side = seqs // (entries - seqs)
    me = order[len(sends)]
    for c in range(seqs):
        chunk_index = order[block] * seqs + c
        place = lax.rem(chunk_index, group) ^ me
        thin_out[place, chunk_index // group] = xproj_grad[c * thin : (c + 1) * thin]
    for c in range(0, seqs, side * group):
        for t in range(group):
            parts = [
                step_grad[(c + k * group + t) * thin : (c + k * group + t + 1) * thin] for k in range(side)
            ]
            parts += [jnp.zeros_like(parts[0])] * (2 - side)
            at = (order[block] * seqs + c) // (group * side)
            thin_out[t ^ me, seqs + at] = jnp.concatenate(parts, axis=1)

    def spread_back(i, unused):
        at = pl.multiple_of(i * BACK_ROWS, BACK_ROWS)
        window = pre_ext[pl.ds(at, BACK_ROWS + 8), :]
        total = weight[taps - 1 : taps] * window[0:BACK_ROWS]
        for s in range(1, taps):
            total = total + weight[taps - 1 - s : taps - s] * window[s : s + BACK_ROWS]
        inner_out[pl.ds(at, BACK_ROWS), :] = total.astype(BF16)
        return 0

    lax.fori_loop(0, rows // BACK_ROWS, spread_back, 0)
    for d, send in enumerate(sends):

        @pl.when(block == d)
        def _(send=send):
            send[0:rows, :] = inner_out[...]
            send[rows : rows + 64, :] = words


def put_chunks(targets, total, core, step, entry, high, first_row, fold):
    width = targets[0].shape[1]
    rows = high // fold
    each = total.shape[0] // rows
    for c in range(each):
        first = pl.multiple_of((step * each + c) // 2 * entry, 8) + first_row
        for parity in range(2):

            @pl.when(lax.rem(core + c, 2) == parity)
            def _(parity=parity, first=first, c=c):
                for f in range(fold):
                    targets[parity][pl.ds(first + f * rows, rows), :] = total[
                        c * rows : (c + 1) * rows, f * width : (f + 1) * width
                    ]


def summed_products(lefts, rights):
    total = None
    for left, right in zip(lefts, rights):
        part = dot(left, right, ((0,), (0,)))
        total = part if total is None else total + part
    return total


def wide_kernel(high, at, *refs):
    count = (len(refs) - 2) // 4
    outs, gates, masked, normed = (refs[k * count : (k + 1) * count] for k in range(4))
    targets = refs[-2:]
    width = targets[0].shape[1]
    total = summed_products([r[...] for r in outs], [r[...] for r in masked])
    fold = masked[0].shape[1] // width
    step = pl.program_id(0)
    put_chunks(targets, total, at[0], step, 2 * high, high, 0, fold)
    total = summed_products([r[...] for r in normed], [r[...] for r in gates])
    put_chunks(targets, total, at[0], step, 2 * high, high, high, 1)


def inner_kernel(total_chunks, at, *refs):
    count = (len(refs) - 4) // 3
    normed, inners, thins = (refs[k * count : (k + 1) * count] for k in range(3))
    gain, live = refs[3 * count : 3 * count + 2]
    targets = refs[-2:]
    core = at[0]
    rows = normed[0].shape[0]
    width = inners[0].shape[1]
    entries, thin, _ = thins[0].shape
    columns = 256
    seqs = total_chunks
    side = seqs // (entries - seqs)
    chips = seqs // 2
    extra = 48 if gain.shape[0] <= 8 else 0
    entry = (targets[0].shape[0] - extra) // chips
    packed = thin * columns // width
    high = entry - packed
    step = pl.program_id(0)
    total = summed_products([r[...] for r in normed], [r[0:rows, :] for r in inners])
    each = total.shape[0] // high
    for c in range(each):
        first = pl.multiple_of((step * each + c) // 2 * entry, 8)
        for parity in range(2):

            @pl.when(lax.rem(core + c, 2) == parity)
            def _(parity=parity, first=first, c=c):
                targets[parity][pl.ds(first, high), :] = total[c * high : (c + 1) * high]

    @pl.when(step == 0)
    def _():
        for i in range(seqs):
            value = thins[0][i].astype(F32)
            near = thins[0][seqs + i // side].astype(F32)
            for r in thins[1:]:
                value = value + r[i].astype(F32)
                near = near + r[seqs + i // side].astype(F32)
            at_lane = (i % side) * 64
            near = near[:, at_lane : at_lane + 64]
            value = jnp.concatenate([value, near, jnp.zeros_like(near)], axis=1)
            first = i // 2 * entry + high
            for parity in range(2):

                @pl.when(lax.rem(core + i, 2) == parity)
                def _(parity=parity, first=first, value=value):
                    if columns >= width:
                        for f in range(columns // width):
                            targets[parity][first + f * thin : first + (f + 1) * thin, :] = value[
                                :, f * width : (f + 1) * width
                            ]
                    else:
                        for f in range(width // columns):
                            targets[parity][
                                first : first + packed, f * columns : (f + 1) * columns
                            ] = value[f * packed : (f + 1) * packed]

        sums = None
        for r in inners:
            words = r[rows : rows + 64, :]
            value = words[0:32].astype(F32) + words[32:64].astype(F32)
            sums = value if sums is None else sums + value
        tail = jnp.concatenate(
            [sums, gain[...], jnp.full((extra - 32 - gain.shape[0], width), live[0], F32)], axis=0
        )
        for target in targets:
            target[chips * entry : chips * entry + extra, :] = tail


def assemble_kernel(
    at, *refs
):
    in_out, out_out, xproj_out, dtproj_out, conv_out, bias_out, dtb_out, skip_out, mean_out, spread_out = refs[-13:-3]
    a_out, gain_out, narrow = refs[-3:]
    count = (len(refs) - 13) // 2
    wides, lasts = refs[:count], refs[count : 2 * count]
    high = in_out.shape[0]
    channels = in_out.shape[1] // 2
    width = wides[0].shape[1]
    fold = out_out.shape[1] // width
    strip = high // fold
    thin, columns = narrow.shape[0] // count, narrow.shape[1]
    packed = thin * columns // width
    taps = conv_out.shape[0]
    mine = a_out.shape[0]
    states = mine * count
    rest = None
    for d in range(count):
        them = at[d + 1]
        lanes = pl.ds(pl.multiple_of(them * width, 128), width)
        half = (lasts[d].shape[0] - high) // 2
        words = lasts[d][high : high + half, :].astype(F32) + lasts[d][high + half :, :].astype(F32)
        piece = words[packed:]
        in_out[:, lanes] = lasts[d][0:high, :].astype(F32)
        in_out[:, pl.ds(pl.multiple_of(channels + them * width, 128), width)] = wides[d][
            high : 2 * high, :
        ].astype(F32)
        for f in range(fold):
            rows = pl.ds(pl.multiple_of(at[1 + count + d] * strip, 8), strip)
            out_out[rows, f * width : (f + 1) * width] = wides[d][f * strip : (f + 1) * strip, :].astype(F32)
        if columns >= width:
            for f in range(columns // width):
                rows = pl.ds(pl.multiple_of(them * thin, 8), thin)
                narrow[rows, f * width : (f + 1) * width] = words[f * thin : (f + 1) * thin]
        else:
            for f in range(width // columns):
                rows = pl.ds(pl.multiple_of(them * thin + f * packed, 8), packed)
                narrow[rows, :] = words[0:packed, f * columns : (f + 1) * columns]
        for k in range(count):

            @pl.when(at[1] == k)
            def _(k=k, lanes=lanes, piece=piece):
                a_out[:, lanes] = piece[k * mine : (k + 1) * mine]

        dtb_out[:, lanes] = piece[states : states + 1]
        skip_out[:, lanes] = piece[states + 1 : states + 2]
        mean_out[:, lanes] = piece[states + 2 : states + 3]
        spread_out[:, lanes] = piece[states + 3 : states + 4]
        conv_out[:, lanes] = piece[states + 4 : states + 4 + taps]
        bias_out[:, lanes] = piece[states + 4 + taps : states + 5 + taps]
        tail = piece[32:48]
        rest = tail if rest is None else rest + tail
    turned = jnp.transpose(narrow[...])
    xproj_out[...] = turned[0 : xproj_out.shape[0]]
    dtproj_out[...] = turned[128 : 128 + dtproj_out.shape[0]]
    for f in range(fold):
        gain_out[:, f * width : (f + 1) * width] = rest[f : f + 1]
    live = rest[fold : fold + 1, 0:1]
    mean = mean_out[...] / live
    spread = spread_out[...] / live - mean * mean + 1e-06
    mean_out[...] = mean
    spread_out[...] = jnp.sqrt(spread)


def struct(*shape, dtype=F32):
    return jax.ShapeDtypeStruct(shape, dtype)


def whole(shape):
    return pl.BlockSpec(shape, lambda *unused: (0,) * len(shape))


LIMIT = pltpu.CompilerParams(vmem_limit_bytes=63 << 20)


def front(inner, before, conv_weight, conv_bias, xproj, width):
    rows, channels = inner.shape

    def part(height):
        return pl.BlockSpec((height, width), lambda q: (0, q))

    return pl.pallas_call(
        front_kernel,
        grid=(channels // width,),
        in_specs=[
            part(rows), part(8), part(conv_weight.shape[0]), part(1),
            part(xproj.shape[0]),
        ],
        out_specs=[part(rows), whole((rows, xproj.shape[0]))],
        out_shape=[struct(rows, channels), struct(rows, xproj.shape[0])],
        scratch_shapes=[pltpu.VMEM((rows + 8, width), F32), pltpu.VMEM((rows, width), BF16)],
        compiler_params=LIMIT,
        cost_estimate=cost(8),
        name="front",
    )(inner, before, conv_weight, conv_bias, xproj)


def local_ends(live, proj, dtproj, dt_bias, mixed, gate, grad_gated, rate, width):
    rows, channels = mixed.shape
    states = rate.shape[0]
    rank = dtproj.shape[0]
    group = channels // width

    def part(height):
        return pl.BlockSpec((height, width), lambda q: (0, q))

    return pl.pallas_call(
        ends_kernel,
        grid=(channels // width,),
        in_specs=[
            pl.BlockSpec(memory_space=pltpu.SMEM), whole(proj.shape),
            part(rank), part(1), part(rows), part(rows), part(rows), part(states),
        ],
        out_specs=[part(rows)] + [part(8), part(states), part(states), whole((2 * states, rows))]
        + [part(states + 8)] * (group - 1),
        out_shape=[struct(rows, channels)]
        + [struct(8, channels), struct(states, channels), struct(states, channels), struct(2 * states, rows)]
        + [struct(states + 8, channels)] * (group - 1),
        scratch_shapes=[
            pltpu.VMEM((rows, 2 * states, 128), F32),
            pltpu.VMEM((rows, width), F32),
            pltpu.VMEM((rows, rank), BF16),
            pltpu.VMEM((rows, width), F32),
            pltpu.VMEM((rows, width), F32),
        ],
        compiler_params=LIMIT,
        cost_estimate=cost(40),
        name="ends",
    )(live, proj, dtproj, dt_bias, mixed, gate, grad_gated, rate)


def full_scan(
    order, cols, proj, rate, step, mixed, gate, grad_gated, state_in, grad_in, skip, dtproj, earlier,
):
    rows, channels = step.shape
    states = rate.shape[0]
    rank = dtproj.shape[0]
    width = channels // lax.axis_size("state")
    blocks = order.shape[0]

    def part(height):
        return pl.BlockSpec((height, width), lambda q, order: (0, order[q]))

    tall = pl.BlockSpec((width, rank), lambda q, order: (order[q], 0))
    rows_f32 = part(rows)
    in_specs = [
        whole(cols.shape), whole(proj.shape), part(states), rows_f32, rows_f32, rows_f32, rows_f32,
        part(states), part(states), part(1), part(rank),
    ]
    out_specs = [
        part(rows), part(rows), part(rows), part(states), part(8), tall, whole((rows, rank)),
        whole((2 * states, rows)),
    ] + [whole((rows, 2 * width))] * blocks
    out_shape = [
        struct(rows, channels, dtype=BF16), struct(rows, channels, dtype=BF16),
        struct(rows, channels), struct(states, channels),
        struct(8, channels), struct(channels, rank), struct(rows, rank), struct(2 * states, rows),
    ] + [struct(rows, 2 * width, dtype=BF16)] * blocks
    args = [
        order, cols, proj, rate, step, mixed, gate, grad_gated, state_in, grad_in, skip, dtproj,
    ]
    aliases = {}
    for out, value in earlier:
        aliases[len(args)] = out
        args.append(value)
        in_specs.append(pl.BlockSpec(memory_space=pl.ANY))
    block = pltpu.VMEM((rows, width), F32)
    return pl.pallas_call(
        functools.partial(scan_kernel, len(earlier)),
        grid_spec=pltpu.PrefetchScalarGridSpec(
            num_scalar_prefetch=1,
            grid=(blocks,),
            in_specs=in_specs,
            out_specs=out_specs,
            scratch_shapes=[
                pltpu.VMEM((rows, 2 * states, 128), F32),
                pltpu.VMEM((rows + 1, states, width), F32),
                pltpu.VMEM((rows, states, 128), F32),
                pltpu.VMEM((rows, states, 128), F32),
                block, block, block, block,
                pltpu.VMEM((rows, width), BF16),
                pltpu.VMEM((rows, rank), BF16),
                block,
            ],
        ),
        out_shape=out_shape,
        input_output_aliases=aliases,
        compiler_params=LIMIT,
        cost_estimate=cost(50),
        name="scan",
    )(*args)


def back(
    order, proj_grad, xproj, mix_grad, inner, before, ahead, conv_weight, conv_bias, rate_sums, scan_sums,
    step_sums, dtproj_grad, earlier,
):
    rows, channels = mix_grad.shape
    blocks = order.shape[0] - 1
    seqs = lax.axis_size("seq")
    group = lax.axis_size("state")
    width = channels // group
    thin = width // seqs
    side = min(2, seqs // group)
    rank = dtproj_grad.shape[1]

    def part(height):
        return pl.BlockSpec((height, width), lambda q, order: (0, order[q]))

    def tall(columns):
        return pl.BlockSpec((width, columns), lambda q, order: (order[q], 0))

    in_specs = [
        whole(proj_grad.shape), part(xproj.shape[0]), part(rows), part(rows), part(8), part(8),
        part(conv_weight.shape[0]), part(1), part(rate_sums.shape[0]), part(8), part(8), tall(rank),
    ]
    args = [
        order, proj_grad, xproj, mix_grad, inner, before, ahead, conv_weight, conv_bias, rate_sums,
        scan_sums, step_sums, dtproj_grad,
    ]
    aliases = {}
    for out, value in earlier:
        aliases[len(args)] = out
        args.append(value)
        in_specs.append(pl.BlockSpec(memory_space=pl.ANY) if out == 0 else whole(value.shape))
    return pl.pallas_call(
        functools.partial(back_kernel, len(earlier)),
        grid_spec=pltpu.PrefetchScalarGridSpec(
            num_scalar_prefetch=1,
            grid=(blocks,),
            in_specs=in_specs,
            out_specs=[part(rows), whole((group, seqs + seqs // side, thin, 128))]
            + [whole((rows + 64, width))] * blocks,
            scratch_shapes=[
                pltpu.VMEM((rows + 8, width), F32),
                pltpu.VMEM((rows + 8, width), F32),
                pltpu.VMEM((rows, width), BF16),
                pltpu.VMEM((rows, width), F32),
            ],
        ),
        out_shape=[
            struct(rows, channels, dtype=BF16), struct(group, seqs + seqs // side, thin, 128, dtype=BF16),
        ] + [struct(rows + 64, width, dtype=BF16)] * blocks,
        input_output_aliases=aliases,
        compiler_params=LIMIT,
        cost_estimate=cost(18),
        name="back",
    )(*args)


def cost(micros):
    return pl.CostEstimate(flops=int(micros), transcendentals=0, bytes_accessed=1024)


def places():
    me = lax.axis_index("state")
    core = lax.axis_index("seq") % 2
    group = lax.axis_size("state")
    base = lax.axis_index("seq") * group // lax.axis_size("seq")
    order = [me ^ d for d in range(group)]
    return jnp.stack([core] + order + [base ^ k for k in order]).astype(jnp.int32)


def wide_grads(gates, masked, normed, seqs):
    count = len(gates)
    rows = gates[0].shape[0]
    width = gates[0].shape[1] // 2
    features = masked[0].shape[1]
    steps = max(1, width // WIDE_STEP)
    high = features // seqs
    chips = seqs // 2
    fixed = pl.BlockSpec((rows, width), lambda i, at: (0, 1))
    part = pl.BlockSpec((rows, width // steps), lambda i, at: (0, i))

    wholly = pl.BlockSpec((rows, features), lambda i, at: (0, 0))
    partly = pl.BlockSpec((rows, features // steps), lambda i, at: (0, i))
    return pl.pallas_call(
        functools.partial(wide_kernel, high),
        grid_spec=pltpu.PrefetchScalarGridSpec(
            num_scalar_prefetch=1,
            grid=(steps,),
            in_specs=[part] * count + [fixed] * count
            + [wholly] * count + [partly] * count,
            out_specs=[whole((chips * 2 * high, width))] * 2,
        ),
        out_shape=[struct(chips * 2 * high, width)] * 2,
        compiler_params=LIMIT,
        cost_estimate=cost(10),
        name="wide",
    )(places(), *gates, *gates, *masked, *normed)


SUM_ROWS = 48


def inner_grads(normed, inners, thins, gain, live, seqs):
    count = len(inners)
    width = inners[0].shape[1]
    rows, features = normed[0].shape
    steps = max(1, width // WIDE_STEP)
    chips = seqs // 2
    entry = features // seqs + thins[0].shape[1] * 256 // width

    partly = pl.BlockSpec((rows, features // steps), lambda i, at: (0, i))
    shape = (chips * entry + SUM_ROWS, width)
    return pl.pallas_call(
        functools.partial(inner_kernel, seqs),
        grid_spec=pltpu.PrefetchScalarGridSpec(
            num_scalar_prefetch=1,
            grid=(steps,),
            in_specs=[partly] * count
            + [whole(inners[0].shape)] * count + [whole(thins[0].shape)] * count
            + [whole(gain.shape), pl.BlockSpec(memory_space=pltpu.SMEM)],
            out_specs=[whole(shape)] * 2,
        ),
        out_shape=[struct(*shape)] * 2,
        compiler_params=LIMIT,
        cost_estimate=cost(5),
        name="inner",
    )(places(), *normed, *inners, *thins, gain, live)


def assemble(wides, lasts, features, channels, seqs, taps, states, proj_width, rank):
    width = wides[0].shape[1]
    count = len(wides)
    rows = channels // seqs
    shapes = [
        (features // seqs, 2 * channels), (rows, features), (proj_width, rows), (rank, rows), (taps, channels),
        (1, channels), (1, channels), (1, channels), (1, channels), (1, channels),
        (states // count, channels), (1, features),
    ]
    return pl.pallas_call(
        assemble_kernel,
        in_specs=[pl.BlockSpec(memory_space=pltpu.SMEM)] + [pl.BlockSpec(memory_space=pltpu.VMEM)] * 2 * count,
        out_specs=[pl.BlockSpec(memory_space=pltpu.VMEM)] * len(shapes),
        out_shape=[struct(*shape) for shape in shapes],
        scratch_shapes=[pltpu.VMEM((rows, 256), F32)],
        compiler_params=LIMIT,
        cost_estimate=cost(4),
        name="assemble",
    )(places(), *wides, *lasts)


def dot(a, b, dims):
    return lax.dot_general(a, b, (dims, ((), ())), preferred_element_type=F32)


def body(
    tokens,
    lengths,
    grad_out,
    norm_gain,
    in_weight,
    conv_weight,
    conv_bias,
    xproj_weight,
    dtproj_weight,
    dt_bias,
    a_log,
    d_skip,
    out_weight,
):
    rows, features = tokens.shape
    channels = out_weight.shape[0]
    rank = dtproj_weight.shape[1]
    proj_width = xproj_weight.shape[1]
    states = (proj_width - rank) // 2
    taps = conv_weight.shape[0]
    group = lax.axis_size("state")
    seqs = lax.axis_size("seq")
    member = lax.axis_index("state")
    width = channels // group
    live_rows = jnp.clip(lengths - member * rows, 0, rows)
    alive = (jnp.arange(rows, dtype=jnp.int32) < live_rows[0]).astype(F32)[:, None]
    conv_row = conv_bias[None]
    xproj = jnp.pad(xproj_weight.T, ((0, 128 - proj_width), (0, 0)))

    a_full = placed(gathered(a_log), 0)
    rate2 = -jnp.exp(a_full) * LOG2E
    cotangent = grad_out.astype(F32)
    masked_low = (cotangent * alive).astype(BF16)
    inputs = tokens.astype(F32)
    inv_scale = lax.rsqrt(jnp.mean(inputs * inputs, axis=1, keepdims=True) + EPSILON)
    normed = inputs * inv_scale
    normed_low = (normed * norm_gain).astype(BF16)
    inner = jnp.dot(normed_low, in_weight[:, :channels], preferred_element_type=F32).astype(BF16)
    before = shifted(inner[rows - 8 :], "state", 1)
    gate_in = jnp.dot(normed_low, in_weight[:, channels:], preferred_element_type=F32)
    grad_gated = dot(masked_low, out_weight, ((1,), (1,)))
    mixed, proj = front(inner, before, conv_weight, conv_row, xproj, width)

    near = [d for d in range(1, group) if d & (d - 1) == 0]
    normed_late, mixed = lax.optimization_barrier((normed_low, mixed))
    normed_near = [swapped(normed_late, d) for d in near]
    step, stats, state_end, grad_end, cols, *offers = local_ends(
        jnp.stack([live_rows[0], member]), proj, dtproj_weight.T, dt_bias[None], mixed, gate_in, grad_gated, rate2, width
    )
    *normed_near, offers = lax.optimization_barrier((*normed_near, offers))
    normed_pieces = {0: normed_low, **dict(zip(near, normed_near))}

    pieces = [jnp.concatenate([state_end, stats], axis=0)]
    pieces += [swapped(offer, d + 1) for d, offer in enumerate(offers)]
    pieces = jnp.stack(pieces)
    state_in = jnp.zeros((states, channels), F32)
    grad_in = jnp.zeros((states, channels), F32)
    for k in range(group - 1):
        one = lax.dynamic_index_in_dim(pieces, member ^ k, 0, keepdims=False)
        passed = one[:states] + jnp.exp2(rate2 * one[states : states + 1]) * state_in
        state_in = jnp.where(k < member, passed, state_in)
    for k in range(group - 1, 0, -1):
        one = lax.dynamic_index_in_dim(pieces, member ^ k, 0, keepdims=False)
        passed = one[:states] + jnp.exp2(rate2 * one[states : states + 1]) * grad_in
        grad_in = jnp.where(k > member, passed, grad_in)

    masked_late, state_in = lax.optimization_barrier((masked_low, state_in))
    masked_pieces = gathered(masked_late)

    first = list(range(1, group // 2 + 1))
    second = list(range(group // 2 + 1, group)) + [0]
    call = (cols, proj, rate2, step, mixed, gate_in, grad_gated, state_in, grad_in)
    call += (d_skip[None], dtproj_weight.T)
    one = list(full_scan(jnp.stack([member ^ d for d in first]), *call, []))
    *masked_pieces, normed_late, one[0] = lax.optimization_barrier((*masked_pieces, normed_low, one[0]))
    normed_pieces.update({d: swapped(normed_late, d) for d in range(1, group) if d not in near})
    normed_pieces = [normed_pieces[d] for d in range(group)]
    gates = {d: swapped(one[8 + q], d) for q, d in enumerate(first)}
    shared = [(k, one[k]) for k in (0, 1, 2, 3, 4, 5)]
    two = full_scan(jnp.stack([member ^ d for d in second]), *call, shared)
    gated_low, grad_gate_low, mix_grad, grad_a, scan_sums, grad_dtproj = two[:6]
    first_gates = [gates[d] for d in first]
    normed_pieces, *first_gates, grad_rank = lax.optimization_barrier(
        (normed_pieces, *first_gates, one[6] + two[6])
    )
    gates.update(dict(zip(first, first_gates)))
    grad_bc = (one[7] + two[7]).T

    grad_proj = jnp.concatenate(
        [grad_rank, grad_bc, jnp.zeros((rows, 128 - proj_width), F32)], axis=1
    ).astype(BF16)
    window = jnp.concatenate([before, inner[:8]], axis=0).astype(F32)
    head_pre = conv_window(window, conv_weight, conv_row, 8)
    head_squash = jax.nn.sigmoid(head_pre)
    head_mixed = mix_grad[:8] + jnp.dot(grad_proj[:8], xproj, preferred_element_type=F32)
    head_grad = head_mixed * head_squash * (1.0 + head_pre * (1.0 - head_squash))
    ahead = shifted(head_grad, "state", -1)
    late_sends = [two[8 + q] for q in range(len(second))]
    ahead, *late_sends = lax.optimization_barrier((ahead, *late_sends))
    gates.update({d: swapped(v, d) if d else v for d, v in zip(second, late_sends)})
    call = (grad_proj, xproj, mix_grad, inner, before, ahead, conv_weight, conv_row, grad_a, scan_sums, stats)
    call += (grad_dtproj,)
    one = back(jnp.stack([member ^ d for d in first] + [member]), *call, [])
    inner_pieces = {d: swapped(one[2 + q], d) for q, d in enumerate(first)}
    two = back(jnp.stack([member ^ d for d in second] + [member]), *call, [(0, one[0]), (1, one[1])])
    grad_inner_low, thin_sends = two[:2]
    inner_pieces.update({d: swapped(two[2 + q], d) if d else two[2 + q] for q, d in enumerate(second)})
    thin_pieces = [thin_sends[0]] + [swapped(thin_sends[d], d) for d in range(1, group)]
    arrived = [inner_pieces[d] for d in first]
    gates, arrived, thin_sends = lax.optimization_barrier((gates, arrived, thin_sends))
    inner_pieces.update(dict(zip(first, arrived)))
    inner_pieces = [inner_pieces[d] for d in range(group)]
    fold = features // width
    high = features // seqs
    thin = width // seqs
    thin_rows = thin * 256 // width

    wide = wide_grads([gates[d] for d in range(group)], masked_pieces, normed_pieces, seqs)
    wide, _, (inner_pieces, thin_pieces), (gated_late, grad_gate_low) = seq_scatter(
        *wide, hold=(inner_pieces, thin_pieces), late=(gated_low, grad_gate_low)
    )
    branch = jnp.dot(gated_late, out_weight, preferred_element_type=F32)
    output = (inputs + alive * branch).astype(BF16)
    wide = wide.astype(BF16)
    owned = to_owner(wide[:high])

    grad_normed = dot(grad_inner_low, in_weight[:, :channels], ((1,), (1,))) + dot(
        grad_gate_low, in_weight[:, channels:], ((1,), (1,))
    )
    gain_part = jnp.sum(grad_normed * normed, axis=0).reshape(fold, width)
    scaled = grad_normed * norm_gain
    grad_tokens = cotangent + inv_scale * (
        scaled - normed * jnp.mean(scaled * normed, axis=1, keepdims=True)
    )

    last = inner_grads(normed_pieces, inner_pieces, thin_pieces, gain_part, live_rows.astype(F32), seqs)
    last, sums, _, owned = seq_scatter(*last, extra=SUM_ROWS, late=owned)
    wide_pieces = gathered(jnp.concatenate([owned, wide[high:]], axis=0))
    *wide_pieces, last, sums = lax.optimization_barrier((*wide_pieces, last, sums))
    words = two_words(jnp.concatenate([last[high:], sums], axis=0))
    last = gathered(jnp.concatenate([last[:high].astype(BF16), words], axis=0))

    (
        grad_in_w, grad_out_w, grad_xproj, grad_dtproj, grad_conv, grad_bias, grad_dtb, grad_skip, dt_mean,
        dt_spread, grad_a_log, grad_gain,
    ) = assemble(
        wide_pieces, last, features, channels, seqs, taps, states, proj_width, rank
    )
    return (
        output,
        grad_tokens,
        grad_gain[0],
        grad_in_w,
        grad_conv,
        grad_bias[0],
        grad_xproj.T,
        grad_dtproj.T,
        grad_dtb[0],
        grad_a_log,
        grad_skip[0],
        grad_out_w,
        dt_mean[0],
        dt_spread[0],
    )


def solution(mesh):
    rows = P(("seq", "state"), None)
    return jax.shard_map(
        body,
        mesh=mesh,
        in_specs=(rows, P("seq"), rows) + (P(),) * 7 + (P("state", None), P(), P()),
        out_specs=(rows, rows, P(), P("seq", None), P(), P(), P("seq", None), P("seq", None), P())
        + (P("state", None), P(), P("seq", None), P(), P()),
        check_vma=False,
    )
```

```python
import functools

import jax
import jax.numpy as jnp
from jax import lax
from jax.experimental import pallas as pl
from jax.experimental.pallas import tpu as pltpu
from jax.sharding import PartitionSpec as P

EPSILON = 1e-05
LOG2E = 1.4426950408889634
LN2 = 0.6931471805599453
F32 = jnp.float32
BF16 = jnp.bfloat16
ENDS_ROWS = 64
SCAN_ROWS = 64
BACK_ROWS = 64
WIDE_STEP = 128


def swapped(value, distance):
    count = lax.axis_size("state")
    return lax.ppermute(value, "state", [(i, i ^ distance) for i in range(count)])


def shifted(value, axis, steps):
    count = lax.axis_size(axis)
    leading, last = (max(0, -steps), min(count, count - steps))
    return lax.ppermute(value, axis, [(source, source + steps) for source in range(leading, last)])


def rotated(value, axis, steps):
    count = lax.axis_size(axis)
    return lax.ppermute(value, axis, [(i, (i + steps) % count) for i in range(count)])


def gathered(value):
    count = lax.axis_size("state")
    return [value] + [swapped(value, d) for d in range(1, count)]


def two_words(value):
    high = lax.reduce_precision(value, 8, 7)
    return jnp.concatenate([high.astype(BF16), (value - high).astype(BF16)], axis=0)


def one_word(value):
    count = value.shape[0] // 2
    return value[:count].astype(F32) + value[count:].astype(F32)


def seq_exchange(value, distance):
    count = lax.axis_size("seq")
    return lax.ppermute(value, "seq", [(i, i ^ distance) for i in range(count)])


def seq_scatter(mine, other, extra=0, hold=None, behind=None, late=None):
    seqs = lax.axis_size("seq")
    seq = lax.axis_index("seq")
    width = mine.shape[1]
    total = mine + seq_exchange(other, 1)
    if behind is not None:
        total, behind = lax.optimization_barrier((total, behind))
    chips = seqs // 2
    high = (total.shape[0] - extra) // chips
    total, sums = total[: chips * high], total[chips * high :]
    k = 1
    while chips > 1:
        chips //= 2
        total = total.reshape(chips, 2, high, width)
        bit = (seq >> k) & 1
        kept = lax.dynamic_index_in_dim(total, bit, 1, keepdims=False)
        away = lax.dynamic_index_in_dim(total, 1 - bit, 1, keepdims=False).astype(BF16)
        away = away.reshape(chips * high, width)
        if extra:
            away = jnp.concatenate([away, two_words(sums)], axis=0)
        got = seq_exchange(away, 1 << k)
        total = kept + got[: chips * high].astype(F32).reshape(kept.shape)
        if extra:
            sums = sums + one_word(got[chips * high :])
        if late is not None and k == 1:
            total, late = lax.optimization_barrier((total, late))
        k += 1
    total = total.reshape(high, width)
    if hold is not None:
        total, hold = lax.optimization_barrier((total, hold))
    return total, sums, hold, behind if late is None else late


def to_owner(value):
    seqs = lax.axis_size("seq")
    states = lax.axis_size("state")
    there = [(s * states + t, s * states + (t ^ (s % states))) for s in range(seqs) for t in range(states)]
    value = lax.ppermute(value, ("seq", "state"), there)
    pairs = [
        (s * states + (t ^ (s % states)), (t * seqs + s) // states * states + (t ^ (s % states)))
        for s in range(seqs)
        for t in range(states)
    ]
    return lax.ppermute(value, ("seq", "state"), pairs)


def placed(pieces, axis, out=None, start=0):
    me = lax.axis_index("state")
    size = pieces[0].shape[axis]
    if out is None:
        shape = list(pieces[0].shape)
        shape[axis] = size * len(pieces)
        out = jnp.zeros(shape, pieces[0].dtype)
    for d, piece in enumerate(pieces):
        out = lax.dynamic_update_slice_in_dim(out, piece, start + (me ^ d) * size, axis)
    return out


def fill_lanes(out_ref, cols_ref, rows):
    groups = min(16, rows // 8)
    states = cols_ref.shape[0]
    lanes = min(128, rows)

    def step(i, unused):
        tiles = []
        for u in range(groups):
            first = (i * groups + u) * 8
            base = pl.multiple_of((first // lanes) * lanes, lanes)
            tile = cols_ref[:, pl.ds(base, lanes)]
            tiles.append(pltpu.roll(tile, lax.rem(lanes - (first - base), lanes), axis=1))
        for u in range(groups):
            for r in range(8):
                out_ref[(i * groups + u) * 8 + r] = jnp.broadcast_to(
                    tiles[u][:, r : r + 1], (states, 128)
                )
        return 0

    lax.fori_loop(0, rows // (8 * groups), step, 0)


def sums_to_rows(values, sublane):
    step = 1
    while len(values) > 1:
        low = (sublane & step) == 0
        values = [
            jnp.where(low, a, b) + pltpu.roll(jnp.where(low, b, a), step, axis=0)
            for a, b in zip(values[::2], values[1::2])
        ]
        step *= 2
    return values[0]


def spread(ref, row, count):
    return jnp.broadcast_to(ref[pl.ds(row, 1), :], (count, ref.shape[1]))


def widened(value, times):
    return jnp.concatenate([value] * times, axis=1)


def conv_window(window, weight, bias, rows):
    taps = weight.shape[0]
    total = bias + weight[taps - 1 : taps] * window[8:]
    for s in range(1, taps):
        total = total + weight[taps - 1 - s : taps - s] * window[8 - s : 8 - s + rows]
    return total


def logistic(value):
    return 1.0 / (1.0 + jnp.exp(-value))


def rounded_grad(gate, grad_gated):
    return (grad_gated * (gate * logistic(gate))).astype(BF16).astype(F32)


def by_eight(value):
    total = value[0:8]
    for k in range(8, value.shape[0], 8):
        total = total + value[k : k + 8]
    return total


def widen_rows(ext, before, inner):
    rows = inner.shape[0]
    ext[0:8] = before[...].astype(F32)

    def move(i, unused):
        at = pl.multiple_of(i * 32, 32)
        ext[pl.ds(at + 8, 32), :] = inner[pl.ds(at, 32), :].astype(F32)
        return 0

    lax.fori_loop(0, rows // 32, move, 0)


def front_kernel(
    normed, halo, in_w, conv_w, conv_b, xproj, mixed_out, proj_out, inner, before, ext, low
):
    rows = inner.shape[0]

    @pl.when(pl.program_id(0) == 0)
    def _():
        proj_out[...] = jnp.zeros_like(proj_out)

    inner[...] = jnp.dot(normed[...], in_w[...], preferred_element_type=F32).astype(BF16)
    before[...] = jnp.dot(halo[...], in_w[...], preferred_element_type=F32).astype(BF16)
    widen_rows(ext, before, inner)
    weight = conv_w[...]
    bias = conv_b[...]

    def chunk(i, unused):
        at = pl.multiple_of(i * BACK_ROWS, BACK_ROWS)
        pre = conv_window(ext[pl.ds(at, BACK_ROWS + 8), :], weight, bias, BACK_ROWS)
        mixed = pre * logistic(pre)
        mixed_out[pl.ds(at, BACK_ROWS), :] = mixed
        low[pl.ds(at, BACK_ROWS), :] = mixed.astype(BF16)
        return 0

    lax.fori_loop(0, rows // BACK_ROWS, chunk, 0)
    proj_out[...] += dot(low[...], xproj[...], ((1,), (1,)))


def ends_kernel(
    live, proj, dtproj, dt_b, mixed, normed, gate_w, masked, out_w, rate,
    step_out, gate, grad_gated, stat_out, state_out, grad_out, cols_out, *rest,
):
    rows, width = mixed.shape
    states = rate.shape[0]
    rank = dtproj.shape[0]
    reps = width // 128
    messages, (lanes, drive, rank_low, raised_all, gy_out) = rest[:-5], rest[-5:]

    @pl.when(pl.program_id(0) == 0)
    def _():
        cols_out[...] = jnp.transpose(proj[...])[rank : rank + 2 * states]
        rank_low[...] = proj[:, :rank].astype(BF16)
        fill_lanes(lanes, cols_out, rows)

    gate[...] = jnp.dot(normed[...], gate_w[...], preferred_element_type=F32)
    grad_gated[...] = dot(masked[...], out_w[...], ((1,), (1,)))
    raised_all[...] = dt_b[...] + jnp.dot(rank_low[...], dtproj[...], preferred_element_type=F32)
    count = ENDS_ROWS
    zero8 = jnp.zeros((8, width), F32)

    def prepare(i, sums):
        at = pl.ds(pl.multiple_of(i * count, count), count)
        raised = raised_all[at, :]
        small = jnp.exp(-jnp.abs(raised))
        step = jnp.maximum(raised, 0.0) + jnp.log1p(small)
        step_out[at, :] = step
        drive[at, :] = step * mixed[at, :]
        gy_out[at, :] = rounded_grad(gate[at, :], grad_gated[at, :])
        row = i * count + lax.broadcasted_iota(jnp.int32, (count, width), 0)
        seen = jnp.where(row < live[0], step, 0.0)
        return sums[0] + by_eight(step), sums[1] + by_eight(seen), sums[2] + by_eight(seen * step)

    sums = lax.fori_loop(0, rows // count, prepare, (zero8, zero8, zero8))
    stat_out[...] = zero8
    for k in range(3):
        stat_out[k : k + 1, :] = jnp.sum(sums[k], axis=0, keepdims=True)

    rates = rate[...]
    groups = rows // 8

    def body(i, carry):
        state, grad = carry
        for r in range(8):
            p = i * 8 + r
            factor = jnp.exp2(rates * spread(step_out, p, states))
            b_wide = widened(lanes[p, 0:states], reps)
            state = factor * state + spread(drive, p, states) * b_wide
        for r in range(7, -1, -1):
            p = (groups - 1 - i) * 8 + r
            factor = jnp.exp2(rates * spread(step_out, p, states))
            c_wide = widened(lanes[p, states : 2 * states], reps)
            grad = factor * (grad + spread(gy_out, p, states) * c_wide)
        return state, grad

    zero = jnp.zeros((states, width), F32)
    state, grad = lax.fori_loop(0, groups, body, (zero, zero))
    state_out[...] = state
    grad_out[...] = grad
    for d, message in enumerate(messages):
        message[0:states, :] = jnp.where(live[1] < (live[1] ^ (d + 1)), state, grad)
        message[states : states + 8, :] = stat_out[...]


def scan_kernel(
    skipped, order, cols, proj, rate, step, mixed, gate, grad_gated, state_in, grad_in, skip, dtproj,
    *rest,
):
    rank_before, bc_before = rest[skipped - 2 : skipped] if skipped else (None, None)
    rest = rest[skipped:]
    gated_out, gate_out, mix_out, rate_out, vec_out, dtproj_out, rank_out, bc_out, proj_grad = rest[:9]
    sends = rest[9:-11]
    (
        lanes, held, b_sum, c_sum, drive, y_sum, decay_sum, source_sum, raised_low, rank_low, grad_y
    ) = rest[-11:]
    rows, width = step.shape
    states = rate.shape[0]
    rank = dtproj.shape[0]
    half = states // 2
    reps = width // 128
    block = pl.program_id(0)

    @pl.when(block == 0)
    def _():
        fill_lanes(lanes, cols, rows)
        rank_low[...] = proj[:, :rank].astype(BF16)
        b_sum[...] = jnp.zeros_like(b_sum)
        c_sum[...] = jnp.zeros_like(c_sum)
        rank_out[...] = rank_before[...] if skipped else jnp.zeros_like(rank_out)

    rates = rate[...]
    groups = rows // 8
    sublane = lax.broadcasted_iota(jnp.int32, (8, width), 0)
    held[0] = state_in[...]

    def forward(i, state):
        parts = []
        row = pl.ds(pl.multiple_of(i * 8, 8), 8)
        drive[row, :] = step[row, :] * mixed[row, :]
        grad_y[row, :] = rounded_grad(gate[row, :], grad_gated[row, :])
        for r in range(8):
            p = i * 8 + r
            factor = jnp.exp2(rates * spread(step, p, states))
            b_wide = widened(lanes[p, 0:states], reps)
            c_wide = widened(lanes[p, states : 2 * states], reps)
            state = factor * state + spread(drive, p, states) * b_wide
            held[p + 1] = state
            seen = state * c_wide
            parts.append(seen[:half] + seen[half:])
        y_sum[row, :] = sums_to_rows(parts, sublane)
        return state

    lax.fori_loop(0, groups, forward, state_in[...])

    def over_tiles(value):
        total = value[:, 0:128]
        for t in range(1, reps):
            total = total + value[:, 128 * t : 128 * t + 128]
        return total

    def backward(k, carry):
        grad_next, rate_sum = carry
        i = groups - 1 - k
        decay_parts = [None] * 8
        source_parts = [None] * 8
        here = held[i * 8 + 8]
        for r in range(7, -1, -1):
            p = i * 8 + r
            step_wide = spread(step, p, states)
            y_wide = spread(grad_y, p, states)
            factor = jnp.exp2(rates * step_wide)
            b_wide = widened(lanes[p, 0:states], reps)
            c_wide = widened(lanes[p, states : 2 * states], reps)
            grad = grad_next + y_wide * c_wide
            before = held[p]
            grad_next = factor * grad
            c_sum[p] += over_tiles(here * y_wide)
            b_sum[p] += over_tiles(grad * spread(drive, p, states))
            through = grad_next * before
            decay = through * rates
            rate_sum = rate_sum + through * step_wide
            source = grad * b_wide
            decay_parts[r] = decay[:half] + decay[half:]
            source_parts[r] = source[:half] + source[half:]
            here = before
        row = pl.ds(pl.multiple_of(i * 8, 8), 8)
        decay_sum[row, :] = sums_to_rows(decay_parts, sublane)
        source_sum[row, :] = sums_to_rows(source_parts, sublane)
        return grad_next, rate_sum

    zero = jnp.zeros((states, width), F32)
    unused, rate_sum = lax.fori_loop(0, groups, backward, (grad_in[...], zero))
    rate_out[...] = rate_sum * (rates * LN2)

    gain = skip[...]
    count = SCAN_ROWS
    zero8 = jnp.zeros((8, width), F32)

    def finish(i, sums):
        at = pl.ds(pl.multiple_of(i * count, count), count)
        value = gate[at, :]
        mix = mixed[at, :]
        upstream = grad_gated[at, :]
        full_y = y_sum[at, :] + gain * mix
        squash = logistic(value)
        act = value * squash
        gated = (full_y * act).astype(BF16)
        grad_gate = (upstream * full_y * squash * (1.0 + value * (1.0 - squash))).astype(BF16)
        gated_out[at, :] = gated
        gate_out[at, :] = grad_gate
        grad_full = upstream * act
        source = source_sum[at, :]
        width_step = step[at, :]
        grad_raised = (LN2 * decay_sum[at, :] + mix * source) * (1.0 - jnp.exp(-width_step))
        raised_low[at, :] = grad_raised.astype(BF16)
        mix_out[at, :] = width_step * source + grad_full * gain
        return sums[0] + by_eight(grad_raised), sums[1] + by_eight(grad_full * mix)

    sums = lax.fori_loop(0, rows // count, finish, (zero8, zero8))
    for d, send in enumerate(sends):

        @pl.when(block == d)
        def _(send=send):
            send[:, 0:width] = gated_out[...]
            send[:, width : 2 * width] = gate_out[...]

    vec_out[...] = zero8
    for k in range(2):
        vec_out[k : k + 1, :] = jnp.sum(sums[k], axis=0, keepdims=True)
    dtproj_out[...] = dot(raised_low[...], rank_low[...], ((0,), (0,)))
    rank_out[...] += dot(raised_low[...], dtproj[...], ((1,), (1,)))

    @pl.when(block == pl.num_programs(0) - 1)
    def _():
        lane = lax.broadcasted_iota(jnp.int32, (states, 128), 1)

        def tile(j, unused):
            def gather(i, carry):
                b_tile, c_tile = carry
                for r in range(16):
                    p = j * 128 + i * 16 + r
                    here = lane == i * 16 + r
                    b_tile = jnp.where(here, jnp.sum(b_sum[p], axis=1, keepdims=True), b_tile)
                    c_tile = jnp.where(here, jnp.sum(c_sum[p], axis=1, keepdims=True), c_tile)
                return b_tile, c_tile

            zero_tile = jnp.zeros((states, 128), F32)
            b_tile, c_tile = lax.fori_loop(0, 8, gather, (zero_tile, zero_tile))
            at = pl.ds(pl.multiple_of(j * 128, 128), 128)
            bc_out[0:states, at] = b_tile
            bc_out[states : 2 * states, at] = c_tile
            return 0

        lax.fori_loop(0, rows // 128, tile, 0)
        if skipped:
            bc_out[...] += bc_before[...]
        turned = jnp.transpose(bc_out[...])
        proj_grad[...] = jnp.concatenate(
            [rank_out[...], turned, jnp.zeros((rows, 128 - rank - 2 * states), F32)], axis=1
        ).astype(BF16)


def back_kernel(
    skipped, order, proj_grad, xproj, mix_grad, inner, before, ahead, conv_w, conv_b, rate_sums, scan_sums, step_sums,
    dtproj_grad, *rest,
):
    thin_before = rest[1] if skipped else None
    inner_out, thin_out, *rest = rest[skipped:]
    sends, (ext, pre_ext, low, mixed_grad) = rest[:-4], rest[-4:]
    rows, width = mix_grad.shape
    taps = conv_w.shape[0]
    states = rate_sums.shape[0]
    block = pl.program_id(0)
    if skipped:

        @pl.when(block == 0)
        def _():
            thin_out[...] = thin_before[...]

    widen_rows(ext, before, inner)
    weight = conv_w[...]
    bias = conv_b[...]
    pre_ext[rows : rows + 8, :] = ahead[...]
    mixed_grad[...] = mix_grad[...] + jnp.dot(proj_grad[...], xproj[...], preferred_element_type=F32)
    zero8 = jnp.zeros((8, width), F32)

    def chunk(i, sums):
        at = pl.multiple_of(i * BACK_ROWS, BACK_ROWS)
        window = ext[pl.ds(at, BACK_ROWS + 8), :]
        pre = conv_window(window, weight, bias, BACK_ROWS)
        squash = logistic(pre)
        low[pl.ds(at, BACK_ROWS), :] = (pre * squash).astype(BF16)
        grad_pre = mixed_grad[pl.ds(at, BACK_ROWS), :] * squash * (1.0 + pre * (1.0 - squash))
        pre_ext[pl.ds(at, BACK_ROWS), :] = grad_pre
        added = [sums[taps] + by_eight(grad_pre)]
        for k in range(taps - 1, -1, -1):
            shift = taps - 1 - k
            added.insert(0, sums[k] + by_eight(grad_pre * window[8 - shift : 8 + BACK_ROWS - shift]))
        return tuple(added)

    sums = lax.fori_loop(0, rows // BACK_ROWS, chunk, (zero8,) * (taps + 1))

    summed = jnp.concatenate(
        [rate_sums[...], scan_sums[0:2, :], step_sums[1:3, :]]
        + [jnp.sum(v, axis=0, keepdims=True) for v in sums]
        + [jnp.zeros((32 - states - 5 - taps, width), F32)],
        axis=0,
    )
    high = summed.astype(BF16)
    words = jnp.concatenate([high, (summed - high.astype(F32)).astype(BF16)], axis=0)

    xproj_grad = dot(low[...], proj_grad[...], ((0,), (0,)))
    xproj_grad = xproj_grad.astype(BF16)
    step_grad = dtproj_grad[...].astype(BF16)
    group, entries, thin, _ = thin_out.shape
    seqs = width // thin
    side = seqs // (entries - seqs)
    me = order[len(sends)]
    for c in range(seqs):
        chunk_index = order[block] * seqs + c
        place = lax.rem(chunk_index, group) ^ me
        thin_out[place, chunk_index // group] = xproj_grad[c * thin : (c + 1) * thin]
    for c in range(0, seqs, side * group):
        for t in range(group):
            parts = [
                step_grad[(c + k * group + t) * thin : (c + k * group + t + 1) * thin] for k in range(side)
            ]
            parts += [jnp.zeros_like(parts[0])] * (2 - side)
            at = (order[block] * seqs + c) // (group * side)
            thin_out[t ^ me, seqs + at] = jnp.concatenate(parts, axis=1)

    def spread_back(i, unused):
        at = pl.multiple_of(i * BACK_ROWS, BACK_ROWS)
        window = pre_ext[pl.ds(at, BACK_ROWS + 8), :]
        total = weight[taps - 1 : taps] * window[0:BACK_ROWS]
        for s in range(1, taps):
            total = total + weight[taps - 1 - s : taps - s] * window[s : s + BACK_ROWS]
        inner_out[pl.ds(at, BACK_ROWS), :] = total.astype(BF16)
        return 0

    lax.fori_loop(0, rows // BACK_ROWS, spread_back, 0)
    for d, send in enumerate(sends):

        @pl.when(block == d)
        def _(send=send):
            send[0:rows, :] = inner_out[...]
            send[rows : rows + 64, :] = words


def put_chunks(targets, total, core, step, entry, high, first_row, fold):
    width = targets[0].shape[1]
    rows = high // fold
    each = total.shape[0] // rows
    for c in range(each):
        first = pl.multiple_of((step * each + c) // 2 * entry, 8) + first_row
        for parity in range(2):

            @pl.when(lax.rem(core + c, 2) == parity)
            def _(parity=parity, first=first, c=c):
                for f in range(fold):
                    targets[parity][pl.ds(first + f * rows, rows), :] = total[
                        c * rows : (c + 1) * rows, f * width : (f + 1) * width
                    ]


def summed_products(lefts, rights):
    total = None
    for left, right in zip(lefts, rights):
        part = dot(left, right, ((0,), (0,)))
        total = part if total is None else total + part
    return total


def wide_kernel(high, at, *refs):
    count = (len(refs) - 2) // 4
    outs, gates, masked, normed = (refs[k * count : (k + 1) * count] for k in range(4))
    targets = refs[-2:]
    width = targets[0].shape[1]
    total = summed_products([r[...] for r in outs], [r[...] for r in masked])
    fold = masked[0].shape[1] // width
    step = pl.program_id(0)
    put_chunks(targets, total, at[0], step, 2 * high, high, 0, fold)
    total = summed_products([r[...] for r in normed], [r[...] for r in gates])
    put_chunks(targets, total, at[0], step, 2 * high, high, high, 1)


def inner_kernel(total_chunks, at, *refs):
    count = (len(refs) - 4) // 3
    normed, inners, thins = (refs[k * count : (k + 1) * count] for k in range(3))
    gain, live = refs[3 * count : 3 * count + 2]
    targets = refs[-2:]
    core = at[0]
    rows = normed[0].shape[0]
    width = inners[0].shape[1]
    entries, thin, _ = thins[0].shape
    columns = 256
    seqs = total_chunks
    side = seqs // (entries - seqs)
    chips = seqs // 2
    extra = 48 if gain.shape[0] <= 8 else 0
    entry = (targets[0].shape[0] - extra) // chips
    packed = thin * columns // width
    high = entry - packed
    step = pl.program_id(0)
    total = summed_products([r[...] for r in normed], [r[0:rows, :] for r in inners])
    each = total.shape[0] // high
    for c in range(each):
        first = pl.multiple_of((step * each + c) // 2 * entry, 8)
        for parity in range(2):

            @pl.when(lax.rem(core + c, 2) == parity)
            def _(parity=parity, first=first, c=c):
                targets[parity][pl.ds(first, high), :] = total[c * high : (c + 1) * high]

    @pl.when(step == 0)
    def _():
        for i in range(seqs):
            value = thins[0][i].astype(F32)
            near = thins[0][seqs + i // side].astype(F32)
            for r in thins[1:]:
                value = value + r[i].astype(F32)
                near = near + r[seqs + i // side].astype(F32)
            at_lane = (i % side) * 64
            near = near[:, at_lane : at_lane + 64]
            value = jnp.concatenate([value, near, jnp.zeros_like(near)], axis=1)
            first = i // 2 * entry + high
            for parity in range(2):

                @pl.when(lax.rem(core + i, 2) == parity)
                def _(parity=parity, first=first, value=value):
                    if columns >= width:
                        for f in range(columns // width):
                            targets[parity][first + f * thin : first + (f + 1) * thin, :] = value[
                                :, f * width : (f + 1) * width
                            ]
                    else:
                        for f in range(width // columns):
                            targets[parity][
                                first : first + packed, f * columns : (f + 1) * columns
                            ] = value[f * packed : (f + 1) * packed]

        sums = None
        for r in inners:
            words = r[rows : rows + 64, :]
            value = words[0:32].astype(F32) + words[32:64].astype(F32)
            sums = value if sums is None else sums + value
        tail = jnp.concatenate(
            [sums, gain[...], jnp.full((extra - 32 - gain.shape[0], width), live[0], F32)], axis=0
        )
        for target in targets:
            target[chips * entry : chips * entry + extra, :] = tail


def assemble_kernel(
    at, *refs
):
    in_out, out_out, xproj_out, dtproj_out, conv_out, bias_out, dtb_out, skip_out, mean_out, spread_out = refs[-13:-3]
    a_out, gain_out, narrow = refs[-3:]
    count = (len(refs) - 13) // 2
    wides, lasts = refs[:count], refs[count : 2 * count]
    high = in_out.shape[0]
    channels = in_out.shape[1] // 2
    width = wides[0].shape[1]
    fold = out_out.shape[1] // width
    strip = high // fold
    thin, columns = narrow.shape[0] // count, narrow.shape[1]
    packed = thin * columns // width
    taps = conv_out.shape[0]
    mine = a_out.shape[0]
    states = mine * count
    rest = None
    for d in range(count):
        them = at[d + 1]
        lanes = pl.ds(pl.multiple_of(them * width, 128), width)
        half = (lasts[d].shape[0] - high) // 2
        words = lasts[d][high : high + half, :].astype(F32) + lasts[d][high + half :, :].astype(F32)
        piece = words[packed:]
        in_out[:, lanes] = lasts[d][0:high, :].astype(F32)
        in_out[:, pl.ds(pl.multiple_of(channels + them * width, 128), width)] = wides[d][
            high : 2 * high, :
        ].astype(F32)
        for f in range(fold):
            rows = pl.ds(pl.multiple_of(at[1 + count + d] * strip, 8), strip)
            out_out[rows, f * width : (f + 1) * width] = wides[d][f * strip : (f + 1) * strip, :].astype(F32)
        if columns >= width:
            for f in range(columns // width):
                rows = pl.ds(pl.multiple_of(them * thin, 8), thin)
                narrow[rows, f * width : (f + 1) * width] = words[f * thin : (f + 1) * thin]
        else:
            for f in range(width // columns):
                rows = pl.ds(pl.multiple_of(them * thin + f * packed, 8), packed)
                narrow[rows, :] = words[0:packed, f * columns : (f + 1) * columns]
        for k in range(count):

            @pl.when(at[1] == k)
            def _(k=k, lanes=lanes, piece=piece):
                a_out[:, lanes] = piece[k * mine : (k + 1) * mine]

        dtb_out[:, lanes] = piece[states : states + 1]
        skip_out[:, lanes] = piece[states + 1 : states + 2]
        mean_out[:, lanes] = piece[states + 2 : states + 3]
        spread_out[:, lanes] = piece[states + 3 : states + 4]
        conv_out[:, lanes] = piece[states + 4 : states + 4 + taps]
        bias_out[:, lanes] = piece[states + 4 + taps : states + 5 + taps]
        tail = piece[32:48]
        rest = tail if rest is None else rest + tail
    turned = jnp.transpose(narrow[...])
    xproj_out[...] = turned[0 : xproj_out.shape[0]]
    dtproj_out[...] = turned[128 : 128 + dtproj_out.shape[0]]
    for f in range(fold):
        gain_out[:, f * width : (f + 1) * width] = rest[f : f + 1]
    live = rest[fold : fold + 1, 0:1]
    mean = mean_out[...] / live
    spread = spread_out[...] / live - mean * mean + 1e-06
    mean_out[...] = mean
    spread_out[...] = jnp.sqrt(spread)


def struct(*shape, dtype=F32):
    return jax.ShapeDtypeStruct(shape, dtype)


def whole(shape):
    return pl.BlockSpec(shape, lambda *unused: (0,) * len(shape))


LIMIT = pltpu.CompilerParams(vmem_limit_bytes=63 << 20)


def front(normed, halo, in_weight, conv_weight, conv_bias, xproj, width):
    rows, features = normed.shape
    channels = in_weight.shape[1] // 2

    def part(height):
        return pl.BlockSpec((height, width), lambda q: (0, q))

    return pl.pallas_call(
        front_kernel,
        grid=(channels // width,),
        in_specs=[
            whole(normed.shape), whole(halo.shape), part(features), part(conv_weight.shape[0]), part(1),
            part(xproj.shape[0]),
        ],
        out_specs=[part(rows), whole((rows, xproj.shape[0])), part(rows), part(8)],
        out_shape=[
            struct(rows, channels), struct(rows, xproj.shape[0]), struct(rows, channels, dtype=BF16),
            struct(8, channels, dtype=BF16),
        ],
        scratch_shapes=[pltpu.VMEM((rows + 8, width), F32), pltpu.VMEM((rows, width), BF16)],
        compiler_params=LIMIT,
        cost_estimate=cost(8),
        name="front",
    )(normed, halo, in_weight, conv_weight, conv_bias, xproj)


def local_ends(live, proj, dtproj, dt_bias, mixed, normed, in_weight, masked, out_weight, rate, width):
    rows, channels = mixed.shape
    features = normed.shape[1]
    states = rate.shape[0]
    rank = dtproj.shape[0]
    group = channels // width

    def part(height):
        return pl.BlockSpec((height, width), lambda q: (0, q))

    return pl.pallas_call(
        ends_kernel,
        grid=(channels // width,),
        in_specs=[
            pl.BlockSpec(memory_space=pltpu.SMEM), whole(proj.shape),
            part(rank), part(1), part(rows), whole(normed.shape),
            pl.BlockSpec((features, width), lambda q: (0, q + group)), whole(masked.shape),
            pl.BlockSpec((width, features), lambda q: (q, 0)), part(states),
        ],
        out_specs=[part(rows)] * 3 + [part(8), part(states), part(states), whole((2 * states, rows))]
        + [part(states + 8)] * (group - 1),
        out_shape=[struct(rows, channels)] * 3
        + [struct(8, channels), struct(states, channels), struct(states, channels), struct(2 * states, rows)]
        + [struct(states + 8, channels)] * (group - 1),
        scratch_shapes=[
            pltpu.VMEM((rows, 2 * states, 128), F32),
            pltpu.VMEM((rows, width), F32),
            pltpu.VMEM((rows, rank), BF16),
            pltpu.VMEM((rows, width), F32),
            pltpu.VMEM((rows, width), F32),
        ],
        compiler_params=LIMIT,
        cost_estimate=cost(40),
        name="ends",
    )(live, proj, dtproj, dt_bias, mixed, normed, in_weight, masked, out_weight, rate)


def full_scan(
    order, cols, proj, rate, step, mixed, gate, grad_gated, state_in, grad_in, skip, dtproj, earlier,
):
    rows, channels = step.shape
    states = rate.shape[0]
    rank = dtproj.shape[0]
    width = channels // lax.axis_size("state")
    blocks = order.shape[0]

    def part(height):
        return pl.BlockSpec((height, width), lambda q, order: (0, order[q]))

    tall = pl.BlockSpec((width, rank), lambda q, order: (order[q], 0))
    rows_f32 = part(rows)
    in_specs = [
        whole(cols.shape), whole(proj.shape), part(states), rows_f32, rows_f32, rows_f32, rows_f32,
        part(states), part(states), part(1), part(rank),
    ]
    out_specs = [
        part(rows), part(rows), part(rows), part(states), part(8), tall, whole((rows, rank)),
        whole((2 * states, rows)), whole((rows, 128)),
    ] + [whole((rows, 2 * width))] * blocks
    out_shape = [
        struct(rows, channels, dtype=BF16), struct(rows, channels, dtype=BF16),
        struct(rows, channels), struct(states, channels),
        struct(8, channels), struct(channels, rank), struct(rows, rank), struct(2 * states, rows),
        struct(rows, 128, dtype=BF16),
    ] + [struct(rows, 2 * width, dtype=BF16)] * blocks
    args = [
        order, cols, proj, rate, step, mixed, gate, grad_gated, state_in, grad_in, skip, dtproj,
    ]
    aliases = {}
    for out, value in earlier:
        aliases[len(args)] = out
        args.append(value)
        in_specs.append(pl.BlockSpec(memory_space=pl.ANY) if out < 6 else whole(value.shape))
    block = pltpu.VMEM((rows, width), F32)
    return pl.pallas_call(
        functools.partial(scan_kernel, len(earlier)),
        grid_spec=pltpu.PrefetchScalarGridSpec(
            num_scalar_prefetch=1,
            grid=(blocks,),
            in_specs=in_specs,
            out_specs=out_specs,
            scratch_shapes=[
                pltpu.VMEM((rows, 2 * states, 128), F32),
                pltpu.VMEM((rows + 1, states, width), F32),
                pltpu.VMEM((rows, states, 128), F32),
                pltpu.VMEM((rows, states, 128), F32),
                block, block, block, block,
                pltpu.VMEM((rows, width), BF16),
                pltpu.VMEM((rows, rank), BF16),
                block,
            ],
        ),
        out_shape=out_shape,
        input_output_aliases=aliases,
        compiler_params=LIMIT,
        cost_estimate=cost(50),
        name="scan",
    )(*args)


def back(
    order, proj_grad, xproj, mix_grad, inner, before, ahead, conv_weight, conv_bias, rate_sums, scan_sums,
    step_sums, dtproj_grad, earlier,
):
    rows, channels = mix_grad.shape
    blocks = order.shape[0] - 1
    seqs = lax.axis_size("seq")
    group = lax.axis_size("state")
    width = channels // group
    thin = width // seqs
    side = min(2, seqs // group)
    rank = dtproj_grad.shape[1]

    def part(height):
        return pl.BlockSpec((height, width), lambda q, order: (0, order[q]))

    def tall(columns):
        return pl.BlockSpec((width, columns), lambda q, order: (order[q], 0))

    in_specs = [
        whole(proj_grad.shape), part(xproj.shape[0]), part(rows), part(rows), part(8), part(8),
        part(conv_weight.shape[0]), part(1), part(rate_sums.shape[0]), part(8), part(8), tall(rank),
    ]
    args = [
        order, proj_grad, xproj, mix_grad, inner, before, ahead, conv_weight, conv_bias, rate_sums,
        scan_sums, step_sums, dtproj_grad,
    ]
    aliases = {}
    for out, value in earlier:
        aliases[len(args)] = out
        args.append(value)
        in_specs.append(pl.BlockSpec(memory_space=pl.ANY) if out == 0 else whole(value.shape))
    return pl.pallas_call(
        functools.partial(back_kernel, len(earlier)),
        grid_spec=pltpu.PrefetchScalarGridSpec(
            num_scalar_prefetch=1,
            grid=(blocks,),
            in_specs=in_specs,
            out_specs=[part(rows), whole((group, seqs + seqs // side, thin, 128))]
            + [whole((rows + 64, width))] * blocks,
            scratch_shapes=[
                pltpu.VMEM((rows + 8, width), F32),
                pltpu.VMEM((rows + 8, width), F32),
                pltpu.VMEM((rows, width), BF16),
                pltpu.VMEM((rows, width), F32),
            ],
        ),
        out_shape=[
            struct(rows, channels, dtype=BF16), struct(group, seqs + seqs // side, thin, 128, dtype=BF16),
        ] + [struct(rows + 64, width, dtype=BF16)] * blocks,
        input_output_aliases=aliases,
        compiler_params=LIMIT,
        cost_estimate=cost(18),
        name="back",
    )(*args)


def cost(micros):
    return pl.CostEstimate(flops=int(micros), transcendentals=0, bytes_accessed=1024)


def places():
    me = lax.axis_index("state")
    core = lax.axis_index("seq") % 2
    group = lax.axis_size("state")
    base = lax.axis_index("seq") * group // lax.axis_size("seq")
    order = [me ^ d for d in range(group)]
    return jnp.stack([core] + order + [base ^ k for k in order]).astype(jnp.int32)


def wide_grads(gates, masked, normed, seqs):
    count = len(gates)
    rows = gates[0].shape[0]
    width = gates[0].shape[1] // 2
    features = masked[0].shape[1]
    steps = max(1, width // WIDE_STEP)
    high = features // seqs
    chips = seqs // 2
    fixed = pl.BlockSpec((rows, width), lambda i, at: (0, 1))
    part = pl.BlockSpec((rows, width // steps), lambda i, at: (0, i))

    wholly = pl.BlockSpec((rows, features), lambda i, at: (0, 0))
    partly = pl.BlockSpec((rows, features // steps), lambda i, at: (0, i))
    return pl.pallas_call(
        functools.partial(wide_kernel, high),
        grid_spec=pltpu.PrefetchScalarGridSpec(
            num_scalar_prefetch=1,
            grid=(steps,),
            in_specs=[part] * count + [fixed] * count
            + [wholly] * count + [partly] * count,
            out_specs=[whole((chips * 2 * high, width))] * 2,
        ),
        out_shape=[struct(chips * 2 * high, width)] * 2,
        compiler_params=LIMIT,
        cost_estimate=cost(10),
        name="wide",
    )(places(), *gates, *gates, *masked, *normed)


SUM_ROWS = 48


def inner_grads(normed, inners, thins, gain, live, seqs):
    count = len(inners)
    width = inners[0].shape[1]
    rows, features = normed[0].shape
    steps = max(1, width // WIDE_STEP)
    chips = seqs // 2
    entry = features // seqs + thins[0].shape[1] * 256 // width

    partly = pl.BlockSpec((rows, features // steps), lambda i, at: (0, i))
    shape = (chips * entry + SUM_ROWS, width)
    return pl.pallas_call(
        functools.partial(inner_kernel, seqs),
        grid_spec=pltpu.PrefetchScalarGridSpec(
            num_scalar_prefetch=1,
            grid=(steps,),
            in_specs=[partly] * count
            + [whole(inners[0].shape)] * count + [whole(thins[0].shape)] * count
            + [whole(gain.shape), pl.BlockSpec(memory_space=pltpu.SMEM)],
            out_specs=[whole(shape)] * 2,
        ),
        out_shape=[struct(*shape)] * 2,
        compiler_params=LIMIT,
        cost_estimate=cost(5),
        name="inner",
    )(places(), *normed, *inners, *thins, gain, live)


def assemble(wides, lasts, features, channels, seqs, taps, states, proj_width, rank):
    width = wides[0].shape[1]
    count = len(wides)
    rows = channels // seqs
    shapes = [
        (features // seqs, 2 * channels), (rows, features), (proj_width, rows), (rank, rows), (taps, channels),
        (1, channels), (1, channels), (1, channels), (1, channels), (1, channels),
        (states // count, channels), (1, features),
    ]
    return pl.pallas_call(
        assemble_kernel,
        in_specs=[pl.BlockSpec(memory_space=pltpu.SMEM)] + [pl.BlockSpec(memory_space=pltpu.VMEM)] * 2 * count,
        out_specs=[pl.BlockSpec(memory_space=pltpu.VMEM)] * len(shapes),
        out_shape=[struct(*shape) for shape in shapes],
        scratch_shapes=[pltpu.VMEM((rows, 256), F32)],
        compiler_params=LIMIT,
        cost_estimate=cost(4),
        name="assemble",
    )(places(), *wides, *lasts)


def dot(a, b, dims):
    return lax.dot_general(a, b, (dims, ((), ())), preferred_element_type=F32)


def body(
    tokens,
    lengths,
    grad_out,
    norm_gain,
    in_weight,
    conv_weight,
    conv_bias,
    xproj_weight,
    dtproj_weight,
    dt_bias,
    a_log,
    d_skip,
    out_weight,
):
    rows, features = tokens.shape
    channels = out_weight.shape[0]
    rank = dtproj_weight.shape[1]
    proj_width = xproj_weight.shape[1]
    states = (proj_width - rank) // 2
    taps = conv_weight.shape[0]
    group = lax.axis_size("state")
    seqs = lax.axis_size("seq")
    member = lax.axis_index("state")
    width = channels // group
    live_rows = jnp.clip(lengths - member * rows, 0, rows)
    alive = (jnp.arange(rows, dtype=jnp.int32) < live_rows[0]).astype(F32)[:, None]
    conv_row = conv_bias[None]
    xproj = jnp.pad(xproj_weight.T, ((0, 128 - proj_width), (0, 0)))

    a_full = placed(gathered(a_log), 0)
    rate2 = -jnp.exp(a_full) * LOG2E
    cotangent = grad_out.astype(F32)
    masked_low = (cotangent * alive).astype(BF16)
    inputs = tokens.astype(F32)
    inv_scale = lax.rsqrt(jnp.mean(inputs * inputs, axis=1, keepdims=True) + EPSILON)
    normed = inputs * inv_scale
    normed_low = (normed * norm_gain).astype(BF16)
    halo = shifted(normed_low[rows - 8 :], "state", 1)
    mixed, proj, inner, before = front(normed_low, halo, in_weight, conv_weight, conv_row, xproj, width)

    near = [d for d in range(1, group) if d & (d - 1) == 0]
    normed_late, mixed = lax.optimization_barrier((normed_low, mixed))
    normed_near = [swapped(normed_late, d) for d in near]
    step, gate_in, grad_gated, stats, state_end, grad_end, cols, *offers = local_ends(
        jnp.stack([live_rows[0], member]), proj, dtproj_weight.T, dt_bias[None], mixed, normed_low, in_weight,
        masked_low, out_weight, rate2, width,
    )
    *normed_near, offers = lax.optimization_barrier((*normed_near, offers))
    normed_pieces = {0: normed_low, **dict(zip(near, normed_near))}

    pieces = [jnp.concatenate([state_end, stats], axis=0)]
    pieces += [swapped(offer, d + 1) for d, offer in enumerate(offers)]
    pieces = jnp.stack(pieces)
    state_in = jnp.zeros((states, channels), F32)
    grad_in = jnp.zeros((states, channels), F32)
    for k in range(group - 1):
        one = lax.dynamic_index_in_dim(pieces, member ^ k, 0, keepdims=False)
        passed = one[:states] + jnp.exp2(rate2 * one[states : states + 1]) * state_in
        state_in = jnp.where(k < member, passed, state_in)
    for k in range(group - 1, 0, -1):
        one = lax.dynamic_index_in_dim(pieces, member ^ k, 0, keepdims=False)
        passed = one[:states] + jnp.exp2(rate2 * one[states : states + 1]) * grad_in
        grad_in = jnp.where(k > member, passed, grad_in)

    masked_late, state_in = lax.optimization_barrier((masked_low, state_in))
    masked_pieces = gathered(masked_late)

    first = list(range(1, group // 2 + 1))
    second = list(range(group // 2 + 1, group)) + [0]
    call = (cols, proj, rate2, step, mixed, gate_in, grad_gated, state_in, grad_in)
    call += (d_skip[None], dtproj_weight.T)
    one = list(full_scan(jnp.stack([member ^ d for d in first]), *call, []))
    *masked_pieces, normed_late, one[0] = lax.optimization_barrier((*masked_pieces, normed_low, one[0]))
    normed_pieces.update({d: swapped(normed_late, d) for d in range(1, group) if d not in near})
    normed_pieces = [normed_pieces[d] for d in range(group)]
    gates = {d: swapped(one[9 + q], d) for q, d in enumerate(first)}
    shared = [(k, one[k]) for k in range(8)]
    two = full_scan(jnp.stack([member ^ d for d in second]), *call, shared)
    gated_low, grad_gate_low, mix_grad, grad_a, scan_sums, grad_dtproj = two[:6]
    first_gates = [gates[d] for d in first]
    normed_pieces, *first_gates, grad_proj = lax.optimization_barrier((normed_pieces, *first_gates, two[8]))
    gates.update(dict(zip(first, first_gates)))

    window = jnp.concatenate([before, inner[:8]], axis=0).astype(F32)
    head_pre = conv_window(window, conv_weight, conv_row, 8)
    head_squash = jax.nn.sigmoid(head_pre)
    head_mixed = mix_grad[:8] + jnp.dot(grad_proj[:8], xproj, preferred_element_type=F32)
    head_grad = head_mixed * head_squash * (1.0 + head_pre * (1.0 - head_squash))
    ahead = shifted(head_grad, "state", -1)
    late_sends = [two[9 + q] for q in range(len(second))]
    ahead, *late_sends = lax.optimization_barrier((ahead, *late_sends))
    gates.update({d: swapped(v, d) if d else v for d, v in zip(second, late_sends)})
    call = (grad_proj, xproj, mix_grad, inner, before, ahead, conv_weight, conv_row, grad_a, scan_sums, stats)
    call += (grad_dtproj,)
    one = back(jnp.stack([member ^ d for d in first] + [member]), *call, [])
    inner_pieces = {d: swapped(one[2 + q], d) for q, d in enumerate(first)}
    two = back(jnp.stack([member ^ d for d in second] + [member]), *call, [(0, one[0]), (1, one[1])])
    grad_inner_low, thin_sends = two[:2]
    inner_pieces.update({d: swapped(two[2 + q], d) if d else two[2 + q] for q, d in enumerate(second)})
    thin_pieces = [thin_sends[0]] + [swapped(thin_sends[d], d) for d in range(1, group)]
    arrived = [inner_pieces[d] for d in first]
    gates, arrived, thin_sends = lax.optimization_barrier((gates, arrived, thin_sends))
    inner_pieces.update(dict(zip(first, arrived)))
    inner_pieces = [inner_pieces[d] for d in range(group)]
    fold = features // width
    high = features // seqs
    thin = width // seqs
    thin_rows = thin * 256 // width

    wide = wide_grads([gates[d] for d in range(group)], masked_pieces, normed_pieces, seqs)
    wide, _, (inner_pieces, thin_pieces), (gated_late, grad_gate_low) = seq_scatter(
        *wide, hold=(inner_pieces, thin_pieces), late=(gated_low, grad_gate_low)
    )
    branch = jnp.dot(gated_late, out_weight, preferred_element_type=F32)
    output = (inputs + alive * branch).astype(BF16)
    wide = wide.astype(BF16)
    owned = to_owner(wide[:high])

    grad_normed = dot(grad_inner_low, in_weight[:, :channels], ((1,), (1,))) + dot(
        grad_gate_low, in_weight[:, channels:], ((1,), (1,))
    )
    gain_part = jnp.sum(grad_normed * normed, axis=0).reshape(fold, width)
    scaled = grad_normed * norm_gain
    grad_tokens = cotangent + inv_scale * (
        scaled - normed * jnp.mean(scaled * normed, axis=1, keepdims=True)
    )

    last = inner_grads(normed_pieces, inner_pieces, thin_pieces, gain_part, live_rows.astype(F32), seqs)
    last, sums, _, owned = seq_scatter(*last, extra=SUM_ROWS, late=owned)
    wide_pieces = gathered(jnp.concatenate([owned, wide[high:]], axis=0))
    *wide_pieces, last, sums = lax.optimization_barrier((*wide_pieces, last, sums))
    words = two_words(jnp.concatenate([last[high:], sums], axis=0))
    last = gathered(jnp.concatenate([last[:high].astype(BF16), words], axis=0))

    (
        grad_in_w, grad_out_w, grad_xproj, grad_dtproj, grad_conv, grad_bias, grad_dtb, grad_skip, dt_mean,
        dt_spread, grad_a_log, grad_gain,
    ) = assemble(
        wide_pieces, last, features, channels, seqs, taps, states, proj_width, rank
    )
    return (
        output,
        grad_tokens,
        grad_gain[0],
        grad_in_w,
        grad_conv,
        grad_bias[0],
        grad_xproj.T,
        grad_dtproj.T,
        grad_dtb[0],
        grad_a_log,
        grad_skip[0],
        grad_out_w,
        dt_mean[0],
        dt_spread[0],
    )


def solution(mesh):
    rows = P(("seq", "state"), None)
    return jax.shard_map(
        body,
        mesh=mesh,
        in_specs=(rows, P("seq"), rows) + (P(),) * 7 + (P("state", None), P(), P()),
        out_specs=(rows, rows, P(), P("seq", None), P(), P(), P("seq", None), P("seq", None), P())
        + (P("state", None), P(), P("seq", None), P(), P()),
        check_vma=False,
    )
```

```python
import functools

import jax
import jax.numpy as jnp
from jax import lax
from jax.experimental import pallas as pl
from jax.experimental.pallas import tpu as pltpu
from jax.sharding import PartitionSpec as P

EPSILON = 1e-05
LOG2E = 1.4426950408889634
LN2 = 0.6931471805599453
F32 = jnp.float32
BF16 = jnp.bfloat16
ENDS_ROWS = 64
SCAN_ROWS = 64
BACK_ROWS = 64
WIDE_STEP = 256


def swapped(value, distance):
    count = lax.axis_size("state")
    return lax.ppermute(value, "state", [(i, i ^ distance) for i in range(count)])


def shifted(value, axis, steps):
    count = lax.axis_size(axis)
    leading, last = (max(0, -steps), min(count, count - steps))
    return lax.ppermute(value, axis, [(source, source + steps) for source in range(leading, last)])


def rotated(value, axis, steps):
    count = lax.axis_size(axis)
    return lax.ppermute(value, axis, [(i, (i + steps) % count) for i in range(count)])


def gathered(value):
    count = lax.axis_size("state")
    return [value] + [swapped(value, d) for d in range(1, count)]


def two_words(value):
    high = lax.reduce_precision(value, 8, 7)
    return jnp.concatenate([high.astype(BF16), (value - high).astype(BF16)], axis=0)


def one_word(value):
    count = value.shape[0] // 2
    return value[:count].astype(F32) + value[count:].astype(F32)


def seq_exchange(value, distance):
    count = lax.axis_size("seq")
    return lax.ppermute(value, "seq", [(i, i ^ distance) for i in range(count)])


def seq_scatter(mine, other, extra=0, hold=None, behind=None, late=None):
    seqs = lax.axis_size("seq")
    seq = lax.axis_index("seq")
    width = mine.shape[1]
    total = mine + seq_exchange(other, 1)
    if behind is not None:
        total, behind = lax.optimization_barrier((total, behind))
    chips = seqs // 2
    high = (total.shape[0] - extra) // chips
    total, sums = total[: chips * high], total[chips * high :]
    k = 1
    while chips > 1:
        chips //= 2
        total = total.reshape(chips, 2, high, width)
        bit = (seq >> k) & 1
        kept = lax.dynamic_index_in_dim(total, bit, 1, keepdims=False)
        away = lax.dynamic_index_in_dim(total, 1 - bit, 1, keepdims=False).astype(BF16)
        away = away.reshape(chips * high, width)
        if extra:
            away = jnp.concatenate([away, two_words(sums)], axis=0)
        got = seq_exchange(away, 1 << k)
        total = kept + got[: chips * high].astype(F32).reshape(kept.shape)
        if extra:
            sums = sums + one_word(got[chips * high :])
        if late is not None and k == 1:
            total, late = lax.optimization_barrier((total, late))
        k += 1
    total = total.reshape(high, width)
    if hold is not None:
        total, hold = lax.optimization_barrier((total, hold))
    return total, sums, hold, behind if late is None else late


def to_owner(value):
    seqs = lax.axis_size("seq")
    states = lax.axis_size("state")
    there = [(s * states + t, s * states + (t ^ (s % states))) for s in range(seqs) for t in range(states)]
    value = lax.ppermute(value, ("seq", "state"), there)
    pairs = [
        (s * states + (t ^ (s % states)), (t * seqs + s) // states * states + (t ^ (s % states)))
        for s in range(seqs)
        for t in range(states)
    ]
    return lax.ppermute(value, ("seq", "state"), pairs)


def placed(pieces, axis, out=None, start=0):
    me = lax.axis_index("state")
    size = pieces[0].shape[axis]
    if out is None:
        shape = list(pieces[0].shape)
        shape[axis] = size * len(pieces)
        out = jnp.zeros(shape, pieces[0].dtype)
    for d, piece in enumerate(pieces):
        out = lax.dynamic_update_slice_in_dim(out, piece, start + (me ^ d) * size, axis)
    return out


def fill_lanes(out_ref, cols_ref, rows):
    groups = min(16, rows // 8)
    states = cols_ref.shape[0]
    lanes = min(128, rows)

    def step(i, unused):
        tiles = []
        for u in range(groups):
            first = (i * groups + u) * 8
            base = pl.multiple_of((first // lanes) * lanes, lanes)
            tile = cols_ref[:, pl.ds(base, lanes)]
            tiles.append(pltpu.roll(tile, lax.rem(lanes - (first - base), lanes), axis=1))
        for u in range(groups):
            for r in range(8):
                out_ref[(i * groups + u) * 8 + r] = jnp.broadcast_to(
                    tiles[u][:, r : r + 1], (states, 128)
                )
        return 0

    lax.fori_loop(0, rows // (8 * groups), step, 0)


def sums_to_rows(values, sublane):
    step = 1
    while len(values) > 1:
        low = (sublane & step) == 0
        values = [
            jnp.where(low, a, b) + pltpu.roll(jnp.where(low, b, a), step, axis=0)
            for a, b in zip(values[::2], values[1::2])
        ]
        step *= 2
    return values[0]


def spread(ref, row, count):
    return jnp.broadcast_to(ref[pl.ds(row, 1), :], (count, ref.shape[1]))


def widened(value, times):
    return jnp.concatenate([value] * times, axis=1)


def conv_window(window, weight, bias, rows):
    taps = weight.shape[0]
    total = bias + weight[taps - 1 : taps] * window[8:]
    for s in range(1, taps):
        total = total + weight[taps - 1 - s : taps - s] * window[8 - s : 8 - s + rows]
    return total


def logistic(value):
    return 1.0 / (1.0 + jnp.exp(-value))


def rounded_grad(gate, grad_gated):
    return (grad_gated * (gate * logistic(gate))).astype(BF16).astype(F32)


def by_eight(value):
    total = value[0:8]
    for k in range(8, value.shape[0], 8):
        total = total + value[k : k + 8]
    return total


def widen_rows(ext, before, inner):
    rows = inner.shape[0]
    ext[0:8] = before[...].astype(F32)

    def move(i, unused):
        at = pl.multiple_of(i * 32, 32)
        ext[pl.ds(at + 8, 32), :] = inner[pl.ds(at, 32), :].astype(F32)
        return 0

    lax.fori_loop(0, rows // 32, move, 0)


def front_kernel(
    normed, halo, in_w, conv_w, conv_b, xproj, mixed_out, proj_out, inner, before, ext, low
):
    rows = inner.shape[0]

    @pl.when(pl.program_id(0) == 0)
    def _():
        proj_out[...] = jnp.zeros_like(proj_out)

    inner[...] = jnp.dot(normed[...], in_w[...], preferred_element_type=F32).astype(BF16)
    before[...] = jnp.dot(halo[...], in_w[...], preferred_element_type=F32).astype(BF16)
    widen_rows(ext, before, inner)
    weight = conv_w[...]
    bias = conv_b[...]

    def chunk(i, unused):
        at = pl.multiple_of(i * BACK_ROWS, BACK_ROWS)
        pre = conv_window(ext[pl.ds(at, BACK_ROWS + 8), :], weight, bias, BACK_ROWS)
        mixed = pre * logistic(pre)
        mixed_out[pl.ds(at, BACK_ROWS), :] = mixed
        low[pl.ds(at, BACK_ROWS), :] = mixed.astype(BF16)
        return 0

    lax.fori_loop(0, rows // BACK_ROWS, chunk, 0)
    proj_out[...] += dot(low[...], xproj[...], ((1,), (1,)))


def ends_kernel(
    live, proj, dtproj, dt_b, mixed, normed, gate_w, masked, out_w, rate,
    step_out, gate, grad_gated, stat_out, state_out, grad_out, cols_out, *rest,
):
    rows, width = mixed.shape
    states = rate.shape[0]
    rank = dtproj.shape[0]
    reps = width // 128
    messages, (lanes, drive, rank_low, raised_all, gy_out) = rest[:-5], rest[-5:]

    @pl.when(pl.program_id(0) == 0)
    def _():
        cols_out[...] = jnp.transpose(proj[...])[rank : rank + 2 * states]
        rank_low[...] = proj[:, :rank].astype(BF16)
        fill_lanes(lanes, cols_out, rows)

    gate[...] = jnp.dot(normed[...], gate_w[...], preferred_element_type=F32)
    grad_gated[...] = dot(masked[...], out_w[...], ((1,), (1,)))
    raised_all[...] = dt_b[...] + jnp.dot(rank_low[...], dtproj[...], preferred_element_type=F32)
    count = ENDS_ROWS
    zero8 = jnp.zeros((8, width), F32)

    def prepare(i, sums):
        at = pl.ds(pl.multiple_of(i * count, count), count)
        raised = raised_all[at, :]
        small = jnp.exp(-jnp.abs(raised))
        step = jnp.maximum(raised, 0.0) + jnp.log1p(small)
        step_out[at, :] = step
        drive[at, :] = step * mixed[at, :]
        gy_out[at, :] = rounded_grad(gate[at, :], grad_gated[at, :])
        row = i * count + lax.broadcasted_iota(jnp.int32, (count, width), 0)
        seen = jnp.where(row < live[0], step, 0.0)
        return sums[0] + by_eight(step), sums[1] + by_eight(seen), sums[2] + by_eight(seen * step)

    sums = lax.fori_loop(0, rows // count, prepare, (zero8, zero8, zero8))
    stat_out[...] = zero8
    for k in range(3):
        stat_out[k : k + 1, :] = jnp.sum(sums[k], axis=0, keepdims=True)

    rates = rate[...]
    groups = rows // 8

    def body(i, carry):
        state, grad = carry
        for r in range(8):
            p = i * 8 + r
            factor = jnp.exp2(rates * spread(step_out, p, states))
            b_wide = widened(lanes[p, 0:states], reps)
            state = factor * state + spread(drive, p, states) * b_wide
        for r in range(7, -1, -1):
            p = (groups - 1 - i) * 8 + r
            factor = jnp.exp2(rates * spread(step_out, p, states))
            c_wide = widened(lanes[p, states : 2 * states], reps)
            grad = factor * (grad + spread(gy_out, p, states) * c_wide)
        return state, grad

    zero = jnp.zeros((states, width), F32)
    state, grad = lax.fori_loop(0, groups, body, (zero, zero))
    state_out[...] = state
    grad_out[...] = grad
    for d, message in enumerate(messages):
        message[0:states, :] = jnp.where(live[1] < (live[1] ^ (d + 1)), state, grad)
        message[states : states + 8, :] = stat_out[...]


def scan_kernel(
    skipped, order, cols, proj, rate, step, mixed, gate, grad_gated, state_in, grad_in, skip, dtproj,
    *rest,
):
    rank_before, bc_before = rest[skipped - 2 : skipped] if skipped else (None, None)
    rest = rest[skipped:]
    gated_out, gate_out, mix_out, rate_out, vec_out, dtproj_out, rank_out, bc_out, proj_grad = rest[:9]
    sends = rest[9:-11]
    (
        lanes, held, b_sum, c_sum, drive, y_sum, decay_sum, source_sum, raised_low, rank_low, grad_y
    ) = rest[-11:]
    rows, width = step.shape
    states = rate.shape[0]
    rank = dtproj.shape[0]
    half = states // 2
    reps = width // 128
    block = pl.program_id(0)

    @pl.when(block == 0)
    def _():
        fill_lanes(lanes, cols, rows)
        rank_low[...] = proj[:, :rank].astype(BF16)
        b_sum[...] = jnp.zeros_like(b_sum)
        c_sum[...] = jnp.zeros_like(c_sum)
        rank_out[...] = rank_before[...] if skipped else jnp.zeros_like(rank_out)

    rates = rate[...]
    groups = rows // 8
    sublane = lax.broadcasted_iota(jnp.int32, (8, width), 0)
    held[0] = state_in[...]

    def forward(i, state):
        parts = []
        row = pl.ds(pl.multiple_of(i * 8, 8), 8)
        drive[row, :] = step[row, :] * mixed[row, :]
        grad_y[row, :] = rounded_grad(gate[row, :], grad_gated[row, :])
        for r in range(8):
            p = i * 8 + r
            factor = jnp.exp2(rates * spread(step, p, states))
            b_wide = widened(lanes[p, 0:states], reps)
            c_wide = widened(lanes[p, states : 2 * states], reps)
            state = factor * state + spread(drive, p, states) * b_wide
            held[p + 1] = state
            seen = state * c_wide
            parts.append(seen[:half] + seen[half:])
        y_sum[row, :] = sums_to_rows(parts, sublane)
        return state

    lax.fori_loop(0, groups, forward, state_in[...])

    def over_tiles(value):
        total = value[:, 0:128]
        for t in range(1, reps):
            total = total + value[:, 128 * t : 128 * t + 128]
        return total

    def backward(k, carry):
        grad_next, rate_sum = carry
        i = groups - 1 - k
        decay_parts = [None] * 8
        source_parts = [None] * 8
        here = held[i * 8 + 8]
        for r in range(7, -1, -1):
            p = i * 8 + r
            step_wide = spread(step, p, states)
            y_wide = spread(grad_y, p, states)
            factor = jnp.exp2(rates * step_wide)
            b_wide = widened(lanes[p, 0:states], reps)
            c_wide = widened(lanes[p, states : 2 * states], reps)
            grad = grad_next + y_wide * c_wide
            before = held[p]
            grad_next = factor * grad
            c_sum[p] += over_tiles(here * y_wide)
            b_sum[p] += over_tiles(grad * spread(drive, p, states))
            through = grad_next * before
            decay = through * rates
            rate_sum = rate_sum + through * step_wide
            source = grad * b_wide
            decay_parts[r] = decay[:half] + decay[half:]
            source_parts[r] = source[:half] + source[half:]
            here = before
        row = pl.ds(pl.multiple_of(i * 8, 8), 8)
        decay_sum[row, :] = sums_to_rows(decay_parts, sublane)
        source_sum[row, :] = sums_to_rows(source_parts, sublane)
        return grad_next, rate_sum

    zero = jnp.zeros((states, width), F32)
    unused, rate_sum = lax.fori_loop(0, groups, backward, (grad_in[...], zero))
    rate_out[...] = rate_sum * (rates * LN2)

    gain = skip[...]
    count = SCAN_ROWS
    zero8 = jnp.zeros((8, width), F32)

    def finish(i, sums):
        at = pl.ds(pl.multiple_of(i * count, count), count)
        value = gate[at, :]
        mix = mixed[at, :]
        upstream = grad_gated[at, :]
        full_y = y_sum[at, :] + gain * mix
        squash = logistic(value)
        act = value * squash
        gated = (full_y * act).astype(BF16)
        grad_gate = (upstream * full_y * squash * (1.0 + value * (1.0 - squash))).astype(BF16)
        gated_out[at, :] = gated
        gate_out[at, :] = grad_gate
        grad_full = upstream * act
        source = source_sum[at, :]
        width_step = step[at, :]
        grad_raised = (LN2 * decay_sum[at, :] + mix * source) * (1.0 - jnp.exp(-width_step))
        raised_low[at, :] = grad_raised.astype(BF16)
        mix_out[at, :] = width_step * source + grad_full * gain
        return sums[0] + by_eight(grad_raised), sums[1] + by_eight(grad_full * mix)

    sums = lax.fori_loop(0, rows // count, finish, (zero8, zero8))
    for d, send in enumerate(sends):

        @pl.when(block == d)
        def _(send=send):
            send[:, 0:width] = gated_out[...]
            send[:, width : 2 * width] = gate_out[...]

    vec_out[...] = zero8
    for k in range(2):
        vec_out[k : k + 1, :] = jnp.sum(sums[k], axis=0, keepdims=True)
    dtproj_out[...] = dot(raised_low[...], rank_low[...], ((0,), (0,)))
    rank_out[...] += dot(raised_low[...], dtproj[...], ((1,), (1,)))

    @pl.when(block == pl.num_programs(0) - 1)
    def _():
        lane = lax.broadcasted_iota(jnp.int32, (states, 128), 1)

        def tile(j, unused):
            def gather(i, carry):
                b_tile, c_tile = carry
                for r in range(16):
                    p = j * 128 + i * 16 + r
                    here = lane == i * 16 + r
                    b_tile = jnp.where(here, jnp.sum(b_sum[p], axis=1, keepdims=True), b_tile)
                    c_tile = jnp.where(here, jnp.sum(c_sum[p], axis=1, keepdims=True), c_tile)
                return b_tile, c_tile

            zero_tile = jnp.zeros((states, 128), F32)
            b_tile, c_tile = lax.fori_loop(0, 8, gather, (zero_tile, zero_tile))
            at = pl.ds(pl.multiple_of(j * 128, 128), 128)
            bc_out[0:states, at] = b_tile
            bc_out[states : 2 * states, at] = c_tile
            return 0

        lax.fori_loop(0, rows // 128, tile, 0)
        if skipped:
            bc_out[...] += bc_before[...]
        turned = jnp.transpose(bc_out[...])
        proj_grad[...] = jnp.concatenate(
            [rank_out[...], turned, jnp.zeros((rows, 128 - rank - 2 * states), F32)], axis=1
        ).astype(BF16)


def back_kernel(
    skipped, order, proj_grad, xproj, mix_grad, inner, before, ahead, conv_w, conv_b, rate_sums, scan_sums, step_sums,
    dtproj_grad, *rest,
):
    thin_before = rest[1] if skipped else None
    inner_out, thin_out, *rest = rest[skipped:]
    sends, (ext, pre_ext, low, mixed_grad) = rest[:-4], rest[-4:]
    rows, width = mix_grad.shape
    taps = conv_w.shape[0]
    states = rate_sums.shape[0]
    block = pl.program_id(0)
    if skipped:

        @pl.when(block == 0)
        def _():
            thin_out[...] = thin_before[...]

    widen_rows(ext, before, inner)
    weight = conv_w[...]
    bias = conv_b[...]
    pre_ext[rows : rows + 8, :] = ahead[...]
    mixed_grad[...] = mix_grad[...] + jnp.dot(proj_grad[...], xproj[...], preferred_element_type=F32)
    zero8 = jnp.zeros((8, width), F32)

    def chunk(i, sums):
        at = pl.multiple_of(i * BACK_ROWS, BACK_ROWS)
        window = ext[pl.ds(at, BACK_ROWS + 8), :]
        pre = conv_window(window, weight, bias, BACK_ROWS)
        squash = logistic(pre)
        low[pl.ds(at, BACK_ROWS), :] = (pre * squash).astype(BF16)
        grad_pre = mixed_grad[pl.ds(at, BACK_ROWS), :] * squash * (1.0 + pre * (1.0 - squash))
        pre_ext[pl.ds(at, BACK_ROWS), :] = grad_pre
        added = [sums[taps] + by_eight(grad_pre)]
        for k in range(taps - 1, -1, -1):
            shift = taps - 1 - k
            added.insert(0, sums[k] + by_eight(grad_pre * window[8 - shift : 8 + BACK_ROWS - shift]))
        return tuple(added)

    sums = lax.fori_loop(0, rows // BACK_ROWS, chunk, (zero8,) * (taps + 1))

    summed = jnp.concatenate(
        [rate_sums[...], scan_sums[0:2, :], step_sums[1:3, :]]
        + [jnp.sum(v, axis=0, keepdims=True) for v in sums]
        + [jnp.zeros((32 - states - 5 - taps, width), F32)],
        axis=0,
    )
    high = summed.astype(BF16)
    words = jnp.concatenate([high, (summed - high.astype(F32)).astype(BF16)], axis=0)

    xproj_grad = dot(low[...], proj_grad[...], ((0,), (0,)))
    xproj_grad = xproj_grad.astype(BF16)
    step_grad = dtproj_grad[...].astype(BF16)
    group, entries, thin, _ = thin_out.shape
    seqs = width // thin
    side = seqs // (entries - seqs)
    me = order[len(sends)]
    for c in range(seqs):
        chunk_index = order[block] * seqs + c
        place = lax.rem(chunk_index, group) ^ me
        thin_out[place, chunk_index // group] = xproj_grad[c * thin : (c + 1) * thin]
    for c in range(0, seqs, side * group):
        for t in range(group):
            parts = [
                step_grad[(c + k * group + t) * thin : (c + k * group + t + 1) * thin] for k in range(side)
            ]
            parts += [jnp.zeros_like(parts[0])] * (2 - side)
            at = (order[block] * seqs + c) // (group * side)
            thin_out[t ^ me, seqs + at] = jnp.concatenate(parts, axis=1)

    def spread_back(i, unused):
        at = pl.multiple_of(i * BACK_ROWS, BACK_ROWS)
        window = pre_ext[pl.ds(at, BACK_ROWS + 8), :]
        total = weight[taps - 1 : taps] * window[0:BACK_ROWS]
        for s in range(1, taps):
            total = total + weight[taps - 1 - s : taps - s] * window[s : s + BACK_ROWS]
        inner_out[pl.ds(at, BACK_ROWS), :] = total.astype(BF16)
        return 0

    lax.fori_loop(0, rows // BACK_ROWS, spread_back, 0)
    for d, send in enumerate(sends):

        @pl.when(block == d)
        def _(send=send):
            send[0:rows, :] = inner_out[...]
            send[rows : rows + 64, :] = words


def put_chunks(targets, total, core, step, entry, high, first_row, fold):
    width = targets[0].shape[1]
    rows = high // fold
    each = total.shape[0] // rows
    for c in range(each):
        first = pl.multiple_of((step * each + c) // 2 * entry, 8) + first_row
        for parity in range(2):

            @pl.when(lax.rem(core + c, 2) == parity)
            def _(parity=parity, first=first, c=c):
                for f in range(fold):
                    targets[parity][pl.ds(first + f * rows, rows), :] = total[
                        c * rows : (c + 1) * rows, f * width : (f + 1) * width
                    ]


def summed_products(lefts, rights):
    total = None
    for left, right in zip(lefts, rights):
        part = dot(left, right, ((0,), (0,)))
        total = part if total is None else total + part
    return total


def wide_kernel(high, at, *refs):
    count = (len(refs) - 2) // 4
    outs, gates, masked, normed = (refs[k * count : (k + 1) * count] for k in range(4))
    targets = refs[-2:]
    width = targets[0].shape[1]
    total = summed_products([r[...] for r in outs], [r[...] for r in masked])
    fold = masked[0].shape[1] // width
    step = pl.program_id(0)
    put_chunks(targets, total, at[0], step, 2 * high, high, 0, fold)
    total = summed_products([r[...] for r in normed], [r[...] for r in gates])
    put_chunks(targets, total, at[0], step, 2 * high, high, high, 1)


def sum_rows(used, gains):
    return -(-(used + gains + 1) // 16) * 16


def inner_kernel(total_chunks, used, at, *refs):
    count = (len(refs) - 4) // 3
    normed, inners, thins = (refs[k * count : (k + 1) * count] for k in range(3))
    gain, live = refs[3 * count : 3 * count + 2]
    targets = refs[-2:]
    core = at[0]
    rows = normed[0].shape[0]
    width = inners[0].shape[1]
    entries, thin, _ = thins[0].shape
    columns = 256
    seqs = total_chunks
    side = seqs // (entries - seqs)
    chips = seqs // 2
    extra = sum_rows(used, gain.shape[0])
    entry = (targets[0].shape[0] - extra) // chips
    packed = thin * columns // width
    high = entry - packed
    step = pl.program_id(0)
    total = summed_products([r[...] for r in normed], [r[0:rows, :] for r in inners])
    each = total.shape[0] // high
    for c in range(each):
        first = pl.multiple_of((step * each + c) // 2 * entry, 8)
        for parity in range(2):

            @pl.when(lax.rem(core + c, 2) == parity)
            def _(parity=parity, first=first, c=c):
                targets[parity][pl.ds(first, high), :] = total[c * high : (c + 1) * high]

    @pl.when(step == 0)
    def _():
        for i in range(seqs):
            value = thins[0][i].astype(F32)
            near = thins[0][seqs + i // side].astype(F32)
            for r in thins[1:]:
                value = value + r[i].astype(F32)
                near = near + r[seqs + i // side].astype(F32)
            at_lane = (i % side) * 64
            near = near[:, at_lane : at_lane + 64]
            value = jnp.concatenate([value, near, jnp.zeros_like(near)], axis=1)
            first = i // 2 * entry + high
            for parity in range(2):

                @pl.when(lax.rem(core + i, 2) == parity)
                def _(parity=parity, first=first, value=value):
                    if columns >= width:
                        for f in range(columns // width):
                            targets[parity][first + f * thin : first + (f + 1) * thin, :] = value[
                                :, f * width : (f + 1) * width
                            ]
                    else:
                        for f in range(width // columns):
                            targets[parity][
                                first : first + packed, f * columns : (f + 1) * columns
                            ] = value[f * packed : (f + 1) * packed]

        sums = None
        for r in inners:
            words = r[rows : rows + 64, :]
            value = words[0:32].astype(F32) + words[32:64].astype(F32)
            sums = value if sums is None else sums + value
        tail = jnp.concatenate(
            [
                sums[0:used],
                gain[...],
                jnp.full((extra - used - gain.shape[0], width), live[0], F32),
            ],
            axis=0,
        )
        for target in targets:
            target[chips * entry : chips * entry + extra, :] = tail


def assemble_kernel(
    at, *refs
):
    in_out, out_out, xproj_out, dtproj_out, conv_out, bias_out, dtb_out, skip_out, mean_out, spread_out = refs[-13:-3]
    a_out, gain_out, narrow = refs[-3:]
    count = (len(refs) - 13) // 2
    wides, lasts = refs[:count], refs[count : 2 * count]
    high = in_out.shape[0]
    channels = in_out.shape[1] // 2
    width = wides[0].shape[1]
    fold = out_out.shape[1] // width
    strip = high // fold
    thin, columns = narrow.shape[0] // count, narrow.shape[1]
    packed = thin * columns // width
    taps = conv_out.shape[0]
    mine = a_out.shape[0]
    states = mine * count
    rest = None
    for d in range(count):
        them = at[d + 1]
        lanes = pl.ds(pl.multiple_of(them * width, 128), width)
        half = (lasts[d].shape[0] - high) // 2
        words = lasts[d][high : high + half, :].astype(F32) + lasts[d][high + half :, :].astype(F32)
        piece = words[packed:]
        in_out[:, lanes] = lasts[d][0:high, :].astype(F32)
        in_out[:, pl.ds(pl.multiple_of(channels + them * width, 128), width)] = wides[d][
            high : 2 * high, :
        ].astype(F32)
        for f in range(fold):
            rows = pl.ds(pl.multiple_of(at[1 + count + d] * strip, 8), strip)
            out_out[rows, f * width : (f + 1) * width] = wides[d][f * strip : (f + 1) * strip, :].astype(F32)
        if columns >= width:
            for f in range(columns // width):
                rows = pl.ds(pl.multiple_of(them * thin, 8), thin)
                narrow[rows, f * width : (f + 1) * width] = words[f * thin : (f + 1) * thin]
        else:
            for f in range(width // columns):
                rows = pl.ds(pl.multiple_of(them * thin + f * packed, 8), packed)
                narrow[rows, :] = words[0:packed, f * columns : (f + 1) * columns]
        for k in range(count):

            @pl.when(at[1] == k)
            def _(k=k, lanes=lanes, piece=piece):
                a_out[:, lanes] = piece[k * mine : (k + 1) * mine]

        dtb_out[:, lanes] = piece[states : states + 1]
        skip_out[:, lanes] = piece[states + 1 : states + 2]
        mean_out[:, lanes] = piece[states + 2 : states + 3]
        spread_out[:, lanes] = piece[states + 3 : states + 4]
        conv_out[:, lanes] = piece[states + 4 : states + 4 + taps]
        bias_out[:, lanes] = piece[states + 4 + taps : states + 5 + taps]
        tail = piece[states + 5 + taps : states + 6 + taps + fold]
        rest = tail if rest is None else rest + tail
    turned = jnp.transpose(narrow[...])
    xproj_out[...] = turned[0 : xproj_out.shape[0]]
    dtproj_out[...] = turned[128 : 128 + dtproj_out.shape[0]]
    for f in range(fold):
        gain_out[:, f * width : (f + 1) * width] = rest[f : f + 1]
    live = rest[fold : fold + 1, 0:1]
    mean = mean_out[...] / live
    spread = spread_out[...] / live - mean * mean + 1e-06
    mean_out[...] = mean
    spread_out[...] = jnp.sqrt(spread)


def struct(*shape, dtype=F32):
    return jax.ShapeDtypeStruct(shape, dtype)


def whole(shape):
    return pl.BlockSpec(shape, lambda *unused: (0,) * len(shape))


LIMIT = pltpu.CompilerParams(vmem_limit_bytes=63 << 20)


def front(normed, halo, in_weight, conv_weight, conv_bias, xproj, width):
    rows, features = normed.shape
    channels = in_weight.shape[1] // 2

    def part(height):
        return pl.BlockSpec((height, width), lambda q: (0, q))

    return pl.pallas_call(
        front_kernel,
        grid=(channels // width,),
        in_specs=[
            whole(normed.shape), whole(halo.shape), part(features), part(conv_weight.shape[0]), part(1),
            part(xproj.shape[0]),
        ],
        out_specs=[part(rows), whole((rows, xproj.shape[0])), part(rows), part(8)],
        out_shape=[
            struct(rows, channels), struct(rows, xproj.shape[0]), struct(rows, channels, dtype=BF16),
            struct(8, channels, dtype=BF16),
        ],
        scratch_shapes=[pltpu.VMEM((rows + 8, width), F32), pltpu.VMEM((rows, width), BF16)],
        compiler_params=LIMIT,
        cost_estimate=cost(8),
        name="front",
    )(normed, halo, in_weight, conv_weight, conv_bias, xproj)


def local_ends(live, proj, dtproj, dt_bias, mixed, normed, in_weight, masked, out_weight, rate, width):
    rows, channels = mixed.shape
    features = normed.shape[1]
    states = rate.shape[0]
    rank = dtproj.shape[0]
    group = channels // width

    def part(height):
        return pl.BlockSpec((height, width), lambda q: (0, q))

    return pl.pallas_call(
        ends_kernel,
        grid=(channels // width,),
        in_specs=[
            pl.BlockSpec(memory_space=pltpu.SMEM), whole(proj.shape),
            part(rank), part(1), part(rows), whole(normed.shape),
            pl.BlockSpec((features, width), lambda q: (0, q + group)), whole(masked.shape),
            pl.BlockSpec((width, features), lambda q: (q, 0)), part(states),
        ],
        out_specs=[part(rows)] * 3 + [part(8), part(states), part(states), whole((2 * states, rows))]
        + [part(states + 8)] * (group - 1),
        out_shape=[struct(rows, channels)] * 3
        + [struct(8, channels), struct(states, channels), struct(states, channels), struct(2 * states, rows)]
        + [struct(states + 8, channels)] * (group - 1),
        scratch_shapes=[
            pltpu.VMEM((rows, 2 * states, 128), F32),
            pltpu.VMEM((rows, width), F32),
            pltpu.VMEM((rows, rank), BF16),
            pltpu.VMEM((rows, width), F32),
            pltpu.VMEM((rows, width), F32),
        ],
        compiler_params=LIMIT,
        cost_estimate=cost(40),
        name="ends",
    )(live, proj, dtproj, dt_bias, mixed, normed, in_weight, masked, out_weight, rate)


def full_scan(
    order, cols, proj, rate, step, mixed, gate, grad_gated, state_in, grad_in, skip, dtproj, earlier,
):
    rows, channels = step.shape
    states = rate.shape[0]
    rank = dtproj.shape[0]
    width = channels // lax.axis_size("state")
    blocks = order.shape[0]

    def part(height):
        return pl.BlockSpec((height, width), lambda q, order: (0, order[q]))

    tall = pl.BlockSpec((width, rank), lambda q, order: (order[q], 0))
    rows_f32 = part(rows)
    in_specs = [
        whole(cols.shape), whole(proj.shape), part(states), rows_f32, rows_f32, rows_f32, rows_f32,
        part(states), part(states), part(1), part(rank),
    ]
    out_specs = [
        part(rows), part(rows), part(rows), part(states), part(8), tall, whole((rows, rank)),
        whole((2 * states, rows)), whole((rows, 128)),
    ] + [whole((rows, 2 * width))] * blocks
    out_shape = [
        struct(rows, channels, dtype=BF16), struct(rows, channels, dtype=BF16),
        struct(rows, channels), struct(states, channels),
        struct(8, channels), struct(channels, rank), struct(rows, rank), struct(2 * states, rows),
        struct(rows, 128, dtype=BF16),
    ] + [struct(rows, 2 * width, dtype=BF16)] * blocks
    args = [
        order, cols, proj, rate, step, mixed, gate, grad_gated, state_in, grad_in, skip, dtproj,
    ]
    aliases = {}
    for out, value in earlier:
        aliases[len(args)] = out
        args.append(value)
        in_specs.append(pl.BlockSpec(memory_space=pl.ANY) if out < 6 else whole(value.shape))
    block = pltpu.VMEM((rows, width), F32)
    return pl.pallas_call(
        functools.partial(scan_kernel, len(earlier)),
        grid_spec=pltpu.PrefetchScalarGridSpec(
            num_scalar_prefetch=1,
            grid=(blocks,),
            in_specs=in_specs,
            out_specs=out_specs,
            scratch_shapes=[
                pltpu.VMEM((rows, 2 * states, 128), F32),
                pltpu.VMEM((rows + 1, states, width), F32),
                pltpu.VMEM((rows, states, 128), F32),
                pltpu.VMEM((rows, states, 128), F32),
                block, block, block, block,
                pltpu.VMEM((rows, width), BF16),
                pltpu.VMEM((rows, rank), BF16),
                block,
            ],
        ),
        out_shape=out_shape,
        input_output_aliases=aliases,
        compiler_params=LIMIT,
        cost_estimate=cost(50),
        name="scan",
    )(*args)


def back(
    order, proj_grad, xproj, mix_grad, inner, before, ahead, conv_weight, conv_bias, rate_sums, scan_sums,
    step_sums, dtproj_grad, earlier,
):
    rows, channels = mix_grad.shape
    blocks = order.shape[0] - 1
    seqs = lax.axis_size("seq")
    group = lax.axis_size("state")
    width = channels // group
    thin = width // seqs
    side = min(2, seqs // group)
    rank = dtproj_grad.shape[1]

    def part(height):
        return pl.BlockSpec((height, width), lambda q, order: (0, order[q]))

    def tall(columns):
        return pl.BlockSpec((width, columns), lambda q, order: (order[q], 0))

    in_specs = [
        whole(proj_grad.shape), part(xproj.shape[0]), part(rows), part(rows), part(8), part(8),
        part(conv_weight.shape[0]), part(1), part(rate_sums.shape[0]), part(8), part(8), tall(rank),
    ]
    args = [
        order, proj_grad, xproj, mix_grad, inner, before, ahead, conv_weight, conv_bias, rate_sums,
        scan_sums, step_sums, dtproj_grad,
    ]
    aliases = {}
    for out, value in earlier:
        aliases[len(args)] = out
        args.append(value)
        in_specs.append(pl.BlockSpec(memory_space=pl.ANY) if out == 0 else whole(value.shape))
    return pl.pallas_call(
        functools.partial(back_kernel, len(earlier)),
        grid_spec=pltpu.PrefetchScalarGridSpec(
            num_scalar_prefetch=1,
            grid=(blocks,),
            in_specs=in_specs,
            out_specs=[part(rows), whole((group, seqs + seqs // side, thin, 128))]
            + [whole((rows + 64, width))] * blocks,
            scratch_shapes=[
                pltpu.VMEM((rows + 8, width), F32),
                pltpu.VMEM((rows + 8, width), F32),
                pltpu.VMEM((rows, width), BF16),
                pltpu.VMEM((rows, width), F32),
            ],
        ),
        out_shape=[
            struct(rows, channels, dtype=BF16), struct(group, seqs + seqs // side, thin, 128, dtype=BF16),
        ] + [struct(rows + 64, width, dtype=BF16)] * blocks,
        input_output_aliases=aliases,
        compiler_params=LIMIT,
        cost_estimate=cost(18),
        name="back",
    )(*args)


def cost(micros):
    return pl.CostEstimate(flops=int(micros), transcendentals=0, bytes_accessed=1024)


def places():
    me = lax.axis_index("state")
    core = lax.axis_index("seq") % 2
    group = lax.axis_size("state")
    base = lax.axis_index("seq") * group // lax.axis_size("seq")
    order = [me ^ d for d in range(group)]
    return jnp.stack([core] + order + [base ^ k for k in order]).astype(jnp.int32)


def wide_grads(gates, masked, normed, seqs):
    count = len(gates)
    rows = gates[0].shape[0]
    width = gates[0].shape[1] // 2
    features = masked[0].shape[1]
    steps = max(1, width // WIDE_STEP)
    high = features // seqs
    chips = seqs // 2
    fixed = pl.BlockSpec((rows, width), lambda i, at: (0, 1))
    part = pl.BlockSpec((rows, width // steps), lambda i, at: (0, i))

    wholly = pl.BlockSpec((rows, features), lambda i, at: (0, 0))
    partly = pl.BlockSpec((rows, features // steps), lambda i, at: (0, i))
    return pl.pallas_call(
        functools.partial(wide_kernel, high),
        grid_spec=pltpu.PrefetchScalarGridSpec(
            num_scalar_prefetch=1,
            grid=(steps,),
            in_specs=[part] * count + [fixed] * count
            + [wholly] * count + [partly] * count,
            out_specs=[whole((chips * 2 * high, width))] * 2,
        ),
        out_shape=[struct(chips * 2 * high, width)] * 2,
        compiler_params=LIMIT,
        cost_estimate=cost(10),
        name="wide",
    )(places(), *gates, *gates, *masked, *normed)


def inner_grads(normed, inners, thins, gain, live, seqs, used):
    count = len(inners)
    width = inners[0].shape[1]
    rows, features = normed[0].shape
    steps = max(1, width // WIDE_STEP)
    chips = seqs // 2
    entry = features // seqs + thins[0].shape[1] * 256 // width

    partly = pl.BlockSpec((rows, features // steps), lambda i, at: (0, i))
    shape = (chips * entry + sum_rows(used, gain.shape[0]), width)
    return pl.pallas_call(
        functools.partial(inner_kernel, seqs, used),
        grid_spec=pltpu.PrefetchScalarGridSpec(
            num_scalar_prefetch=1,
            grid=(steps,),
            in_specs=[partly] * count
            + [whole(inners[0].shape)] * count + [whole(thins[0].shape)] * count
            + [whole(gain.shape), pl.BlockSpec(memory_space=pltpu.SMEM)],
            out_specs=[whole(shape)] * 2,
        ),
        out_shape=[struct(*shape)] * 2,
        compiler_params=LIMIT,
        cost_estimate=cost(5),
        name="inner",
    )(places(), *normed, *inners, *thins, gain, live)


def assemble(wides, lasts, features, channels, seqs, taps, states, proj_width, rank):
    width = wides[0].shape[1]
    count = len(wides)
    rows = channels // seqs
    shapes = [
        (features // seqs, 2 * channels), (rows, features), (proj_width, rows), (rank, rows), (taps, channels),
        (1, channels), (1, channels), (1, channels), (1, channels), (1, channels),
        (states // count, channels), (1, features),
    ]
    return pl.pallas_call(
        assemble_kernel,
        in_specs=[pl.BlockSpec(memory_space=pltpu.SMEM)] + [pl.BlockSpec(memory_space=pltpu.VMEM)] * 2 * count,
        out_specs=[pl.BlockSpec(memory_space=pltpu.VMEM)] * len(shapes),
        out_shape=[struct(*shape) for shape in shapes],
        scratch_shapes=[pltpu.VMEM((rows, 256), F32)],
        compiler_params=LIMIT,
        cost_estimate=cost(4),
        name="assemble",
    )(places(), *wides, *lasts)


def dot(a, b, dims):
    return lax.dot_general(a, b, (dims, ((), ())), preferred_element_type=F32)


def body(
    tokens,
    lengths,
    grad_out,
    norm_gain,
    in_weight,
    conv_weight,
    conv_bias,
    xproj_weight,
    dtproj_weight,
    dt_bias,
    a_log,
    d_skip,
    out_weight,
):
    rows, features = tokens.shape
    channels = out_weight.shape[0]
    rank = dtproj_weight.shape[1]
    proj_width = xproj_weight.shape[1]
    states = (proj_width - rank) // 2
    taps = conv_weight.shape[0]
    group = lax.axis_size("state")
    seqs = lax.axis_size("seq")
    member = lax.axis_index("state")
    width = channels // group
    live_rows = jnp.clip(lengths - member * rows, 0, rows)
    alive = (jnp.arange(rows, dtype=jnp.int32) < live_rows[0]).astype(F32)[:, None]
    conv_row = conv_bias[None]
    xproj = jnp.pad(xproj_weight.T, ((0, 128 - proj_width), (0, 0)))

    a_full = placed(gathered(a_log), 0)
    rate2 = -jnp.exp(a_full) * LOG2E
    cotangent = grad_out.astype(F32)
    masked_low = (cotangent * alive).astype(BF16)
    inputs = tokens.astype(F32)
    inv_scale = lax.rsqrt(jnp.mean(inputs * inputs, axis=1, keepdims=True) + EPSILON)
    normed = inputs * inv_scale
    normed_low = (normed * norm_gain).astype(BF16)
    halo = shifted(normed_low[rows - 8 :], "state", 1)
    mixed, proj, inner, before = front(normed_low, halo, in_weight, conv_weight, conv_row, xproj, width)

    near = [d for d in range(1, group) if d & (d - 1) == 0]
    normed_late, mixed = lax.optimization_barrier((normed_low, mixed))
    normed_near = [swapped(normed_late, d) for d in near]
    step, gate_in, grad_gated, stats, state_end, grad_end, cols, *offers = local_ends(
        jnp.stack([live_rows[0], member]), proj, dtproj_weight.T, dt_bias[None], mixed, normed_low, in_weight,
        masked_low, out_weight, rate2, width,
    )
    *normed_near, offers = lax.optimization_barrier((*normed_near, offers))
    normed_pieces = {0: normed_low, **dict(zip(near, normed_near))}

    pieces = [jnp.concatenate([state_end, stats], axis=0)]
    pieces += [swapped(offer, d + 1) for d, offer in enumerate(offers)]
    pieces = jnp.stack(pieces)
    state_in = jnp.zeros((states, channels), F32)
    grad_in = jnp.zeros((states, channels), F32)
    for k in range(group - 1):
        one = lax.dynamic_index_in_dim(pieces, member ^ k, 0, keepdims=False)
        passed = one[:states] + jnp.exp2(rate2 * one[states : states + 1]) * state_in
        state_in = jnp.where(k < member, passed, state_in)
    for k in range(group - 1, 0, -1):
        one = lax.dynamic_index_in_dim(pieces, member ^ k, 0, keepdims=False)
        passed = one[:states] + jnp.exp2(rate2 * one[states : states + 1]) * grad_in
        grad_in = jnp.where(k > member, passed, grad_in)

    masked_late, state_in = lax.optimization_barrier((masked_low, state_in))
    masked_pieces = gathered(masked_late)

    first = list(range(1, group // 2 + 1))
    second = list(range(group // 2 + 1, group)) + [0]
    call = (cols, proj, rate2, step, mixed, gate_in, grad_gated, state_in, grad_in)
    call += (d_skip[None], dtproj_weight.T)
    one = list(full_scan(jnp.stack([member ^ d for d in first]), *call, []))
    *masked_pieces, normed_late, one[0] = lax.optimization_barrier((*masked_pieces, normed_low, one[0]))
    normed_pieces.update({d: swapped(normed_late, d) for d in range(1, group) if d not in near})
    normed_pieces = [normed_pieces[d] for d in range(group)]
    gates = {d: swapped(one[9 + q], d) for q, d in enumerate(first)}
    shared = [(k, one[k]) for k in range(8)]
    two = full_scan(jnp.stack([member ^ d for d in second]), *call, shared)
    gated_low, grad_gate_low, mix_grad, grad_a, scan_sums, grad_dtproj = two[:6]
    first_gates = [gates[d] for d in first]
    normed_pieces, *first_gates, grad_proj = lax.optimization_barrier((normed_pieces, *first_gates, two[8]))
    gates.update(dict(zip(first, first_gates)))

    window = jnp.concatenate([before, inner[:8]], axis=0).astype(F32)
    head_pre = conv_window(window, conv_weight, conv_row, 8)
    head_squash = jax.nn.sigmoid(head_pre)
    head_mixed = mix_grad[:8] + jnp.dot(grad_proj[:8], xproj, preferred_element_type=F32)
    head_grad = head_mixed * head_squash * (1.0 + head_pre * (1.0 - head_squash))
    ahead = shifted(head_grad, "state", -1)
    late_sends = [two[9 + q] for q in range(len(second))]
    ahead, *late_sends = lax.optimization_barrier((ahead, *late_sends))
    gates.update({d: swapped(v, d) if d else v for d, v in zip(second, late_sends)})
    call = (grad_proj, xproj, mix_grad, inner, before, ahead, conv_weight, conv_row, grad_a, scan_sums, stats)
    call += (grad_dtproj,)
    one = back(jnp.stack([member ^ d for d in first] + [member]), *call, [])
    inner_pieces = {d: swapped(one[2 + q], d) for q, d in enumerate(first)}
    two = back(jnp.stack([member ^ d for d in second] + [member]), *call, [(0, one[0]), (1, one[1])])
    grad_inner_low, thin_sends = two[:2]
    inner_pieces.update({d: swapped(two[2 + q], d) if d else two[2 + q] for q, d in enumerate(second)})
    thin_pieces = [thin_sends[0]] + [swapped(thin_sends[d], d) for d in range(1, group)]
    arrived = [inner_pieces[d] for d in first]
    gates, arrived, thin_sends = lax.optimization_barrier((gates, arrived, thin_sends))
    inner_pieces.update(dict(zip(first, arrived)))
    inner_pieces = [inner_pieces[d] for d in range(group)]
    fold = features // width
    high = features // seqs
    thin = width // seqs
    thin_rows = thin * 256 // width
    used = states + 5 + taps

    wide = wide_grads([gates[d] for d in range(group)], masked_pieces, normed_pieces, seqs)
    wide, _, (inner_pieces, thin_pieces), (gated_late, grad_gate_low) = seq_scatter(
        *wide, hold=(inner_pieces, thin_pieces), late=(gated_low, grad_gate_low)
    )
    branch = jnp.dot(gated_late, out_weight, preferred_element_type=F32)
    output = (inputs + alive * branch).astype(BF16)
    wide = wide.astype(BF16)
    owned = to_owner(wide[:high])

    grad_normed = dot(grad_inner_low, in_weight[:, :channels], ((1,), (1,))) + dot(
        grad_gate_low, in_weight[:, channels:], ((1,), (1,))
    )
    gain_part = jnp.sum(grad_normed * normed, axis=0).reshape(fold, width)
    scaled = grad_normed * norm_gain
    grad_tokens = cotangent + inv_scale * (
        scaled - normed * jnp.mean(scaled * normed, axis=1, keepdims=True)
    )

    last = inner_grads(normed_pieces, inner_pieces, thin_pieces, gain_part, live_rows.astype(F32), seqs, used)
    last, sums, _, owned = seq_scatter(*last, extra=sum_rows(used, fold), late=owned)
    wide_pieces = gathered(jnp.concatenate([owned, wide[high:]], axis=0))
    *wide_pieces, last, sums = lax.optimization_barrier((*wide_pieces, last, sums))
    words = two_words(jnp.concatenate([last[high:], sums], axis=0))
    last = gathered(jnp.concatenate([last[:high].astype(BF16), words], axis=0))

    (
        grad_in_w, grad_out_w, grad_xproj, grad_dtproj, grad_conv, grad_bias, grad_dtb, grad_skip, dt_mean,
        dt_spread, grad_a_log, grad_gain,
    ) = assemble(
        wide_pieces, last, features, channels, seqs, taps, states, proj_width, rank
    )
    return (
        output,
        grad_tokens,
        grad_gain[0],
        grad_in_w,
        grad_conv,
        grad_bias[0],
        grad_xproj.T,
        grad_dtproj.T,
        grad_dtb[0],
        grad_a_log,
        grad_skip[0],
        grad_out_w,
        dt_mean[0],
        dt_spread[0],
    )


def solution(mesh):
    rows = P(("seq", "state"), None)
    return jax.shard_map(
        body,
        mesh=mesh,
        in_specs=(rows, P("seq"), rows) + (P(),) * 7 + (P("state", None), P(), P()),
        out_specs=(rows, rows, P(), P("seq", None), P(), P(), P("seq", None), P("seq", None), P())
        + (P("state", None), P(), P("seq", None), P(), P()),
        check_vma=False,
    )
```

```python
import functools

import jax
import jax.numpy as jnp
from jax import lax
from jax.experimental import pallas as pl
from jax.experimental.pallas import tpu as pltpu
from jax.sharding import PartitionSpec as P

EPSILON = 1e-05
LOG2E = 1.4426950408889634
LN2 = 0.6931471805599453
F32 = jnp.float32
BF16 = jnp.bfloat16
ENDS_ROWS = 128
SCAN_ROWS = 64
BACK_ROWS = 128
WIDE_STEP = 256


def swapped(value, distance):
    count = lax.axis_size("state")
    return lax.ppermute(value, "state", [(i, i ^ distance) for i in range(count)])


def shifted(value, axis, steps):
    count = lax.axis_size(axis)
    leading, last = (max(0, -steps), min(count, count - steps))
    return lax.ppermute(value, axis, [(source, source + steps) for source in range(leading, last)])


def rotated(value, axis, steps):
    count = lax.axis_size(axis)
    return lax.ppermute(value, axis, [(i, (i + steps) % count) for i in range(count)])


def gathered(value):
    count = lax.axis_size("state")
    return [value] + [swapped(value, d) for d in range(1, count)]


def two_words(value):
    high = lax.reduce_precision(value, 8, 7)
    return jnp.concatenate([high.astype(BF16), (value - high).astype(BF16)], axis=0)


def one_word(value):
    count = value.shape[0] // 2
    return value[:count].astype(F32) + value[count:].astype(F32)


def seq_exchange(value, distance):
    count = lax.axis_size("seq")
    return lax.ppermute(value, "seq", [(i, i ^ distance) for i in range(count)])


def seq_scatter(mine, other, extra=0, hold=None, behind=None, late=None):
    seqs = lax.axis_size("seq")
    seq = lax.axis_index("seq")
    width = mine.shape[1]
    total = mine + seq_exchange(other, 1)
    if behind is not None:
        total, behind = lax.optimization_barrier((total, behind))
    chips = seqs // 2
    high = (total.shape[0] - extra) // chips
    total, sums = total[: chips * high], total[chips * high :]
    k = 1
    while chips > 1:
        chips //= 2
        total = total.reshape(chips, 2, high, width)
        bit = (seq >> k) & 1
        kept = lax.dynamic_index_in_dim(total, bit, 1, keepdims=False)
        away = lax.dynamic_index_in_dim(total, 1 - bit, 1, keepdims=False).astype(BF16)
        away = away.reshape(chips * high, width)
        if extra:
            away = jnp.concatenate([away, two_words(sums)], axis=0)
        got = seq_exchange(away, 1 << k)
        total = kept + got[: chips * high].astype(F32).reshape(kept.shape)
        if extra:
            sums = sums + one_word(got[chips * high :])
        if late is not None and k == 1:
            total, late = lax.optimization_barrier((total, late))
        k += 1
    total = total.reshape(high, width)
    if hold is not None:
        total, hold = lax.optimization_barrier((total, hold))
    return total, sums, hold, behind if late is None else late


def to_owner(value):
    seqs = lax.axis_size("seq")
    states = lax.axis_size("state")
    there = [(s * states + t, s * states + (t ^ (s % states))) for s in range(seqs) for t in range(states)]
    value = lax.ppermute(value, ("seq", "state"), there)
    pairs = [
        (s * states + (t ^ (s % states)), (t * seqs + s) // states * states + (t ^ (s % states)))
        for s in range(seqs)
        for t in range(states)
    ]
    return lax.ppermute(value, ("seq", "state"), pairs)


def placed(pieces, axis, out=None, start=0):
    me = lax.axis_index("state")
    size = pieces[0].shape[axis]
    if out is None:
        shape = list(pieces[0].shape)
        shape[axis] = size * len(pieces)
        out = jnp.zeros(shape, pieces[0].dtype)
    for d, piece in enumerate(pieces):
        out = lax.dynamic_update_slice_in_dim(out, piece, start + (me ^ d) * size, axis)
    return out


def fill_lanes(out_ref, cols_ref, rows):
    groups = min(16, rows // 8)
    states = cols_ref.shape[0]
    lanes = min(128, rows)

    def step(i, unused):
        tiles = []
        for u in range(groups):
            first = (i * groups + u) * 8
            base = pl.multiple_of((first // lanes) * lanes, lanes)
            tile = cols_ref[:, pl.ds(base, lanes)]
            tiles.append(pltpu.roll(tile, lax.rem(lanes - (first - base), lanes), axis=1))
        for u in range(groups):
            for r in range(8):
                out_ref[(i * groups + u) * 8 + r] = jnp.broadcast_to(
                    tiles[u][:, r : r + 1], (states, 128)
                )
        return 0

    lax.fori_loop(0, rows // (8 * groups), step, 0)


def sums_to_rows(values, sublane):
    step = 1
    while len(values) > 1:
        low = (sublane & step) == 0
        values = [
            jnp.where(low, a, b) + pltpu.roll(jnp.where(low, b, a), step, axis=0)
            for a, b in zip(values[::2], values[1::2])
        ]
        step *= 2
    return values[0]


def spread(ref, row, count):
    return jnp.broadcast_to(ref[pl.ds(row, 1), :], (count, ref.shape[1]))


def widened(value, times):
    return jnp.concatenate([value] * times, axis=1)


def conv_window(window, weight, bias, rows):
    taps = weight.shape[0]
    total = bias + weight[taps - 1 : taps] * window[8:]
    for s in range(1, taps):
        total = total + weight[taps - 1 - s : taps - s] * window[8 - s : 8 - s + rows]
    return total


def logistic(value):
    return 1.0 / (1.0 + jnp.exp(-value))


def rounded_grad(gate, grad_gated):
    return (grad_gated * (gate * logistic(gate))).astype(BF16).astype(F32)


def by_eight(value):
    total = value[0:8]
    for k in range(8, value.shape[0], 8):
        total = total + value[k : k + 8]
    return total


def widen_rows(ext, before, inner):
    rows = inner.shape[0]
    ext[0:8] = before[...].astype(F32)

    def move(i, unused):
        at = pl.multiple_of(i * 32, 32)
        ext[pl.ds(at + 8, 32), :] = inner[pl.ds(at, 32), :].astype(F32)
        return 0

    lax.fori_loop(0, rows // 32, move, 0)


def front_kernel(
    normed, halo, in_w, conv_w, conv_b, xproj, mixed_out, proj_out, inner, before, ext, low
):
    rows = inner.shape[0]

    @pl.when(pl.program_id(0) == 0)
    def _():
        proj_out[...] = jnp.zeros_like(proj_out)

    inner[...] = jnp.dot(normed[...], in_w[...], preferred_element_type=F32).astype(BF16)
    before[...] = jnp.dot(halo[...], in_w[...], preferred_element_type=F32).astype(BF16)
    widen_rows(ext, before, inner)
    weight = conv_w[...]
    bias = conv_b[...]

    def chunk(i, unused):
        at = pl.multiple_of(i * BACK_ROWS, BACK_ROWS)
        pre = conv_window(ext[pl.ds(at, BACK_ROWS + 8), :], weight, bias, BACK_ROWS)
        mixed = pre * logistic(pre)
        mixed_out[pl.ds(at, BACK_ROWS), :] = mixed
        low[pl.ds(at, BACK_ROWS), :] = mixed.astype(BF16)
        return 0

    lax.fori_loop(0, rows // BACK_ROWS, chunk, 0)
    proj_out[...] += dot(low[...], xproj[...], ((1,), (1,)))


def ends_kernel(
    live, proj, dtproj, dt_b, mixed, normed, gate_w, masked, out_w, rate,
    step_out, gate, grad_gated, stat_out, state_out, grad_out, cols_out, *rest,
):
    rows, width = mixed.shape
    states = rate.shape[0]
    rank = dtproj.shape[0]
    reps = width // 128
    messages, (lanes, drive, rank_low, raised_all, gy_out) = rest[:-5], rest[-5:]

    @pl.when(pl.program_id(0) == 0)
    def _():
        cols_out[...] = jnp.transpose(proj[...])[rank : rank + 2 * states]
        rank_low[...] = proj[:, :rank].astype(BF16)
        fill_lanes(lanes, cols_out, rows)

    gate[...] = jnp.dot(normed[...], gate_w[...], preferred_element_type=F32)
    grad_gated[...] = dot(masked[...], out_w[...], ((1,), (1,)))
    raised_all[...] = dt_b[...] + jnp.dot(rank_low[...], dtproj[...], preferred_element_type=F32)
    count = ENDS_ROWS
    zero8 = jnp.zeros((8, width), F32)

    def prepare(i, sums):
        at = pl.ds(pl.multiple_of(i * count, count), count)
        raised = raised_all[at, :]
        small = jnp.exp(-jnp.abs(raised))
        step = jnp.maximum(raised, 0.0) + jnp.log1p(small)
        step_out[at, :] = step
        drive[at, :] = step * mixed[at, :]
        gy_out[at, :] = rounded_grad(gate[at, :], grad_gated[at, :])
        row = i * count + lax.broadcasted_iota(jnp.int32, (count, width), 0)
        seen = jnp.where(row < live[0], step, 0.0)
        return sums[0] + by_eight(step), sums[1] + by_eight(seen), sums[2] + by_eight(seen * step)

    sums = lax.fori_loop(0, rows // count, prepare, (zero8, zero8, zero8))
    stat_out[...] = zero8
    for k in range(3):
        stat_out[k : k + 1, :] = jnp.sum(sums[k], axis=0, keepdims=True)

    rates = rate[...]
    groups = rows // 8

    def body(i, carry):
        state, grad = carry
        for r in range(8):
            p = i * 8 + r
            factor = jnp.exp2(rates * spread(step_out, p, states))
            b_wide = widened(lanes[p, 0:states], reps)
            state = factor * state + spread(drive, p, states) * b_wide
        for r in range(7, -1, -1):
            p = (groups - 1 - i) * 8 + r
            factor = jnp.exp2(rates * spread(step_out, p, states))
            c_wide = widened(lanes[p, states : 2 * states], reps)
            grad = factor * (grad + spread(gy_out, p, states) * c_wide)
        return state, grad

    zero = jnp.zeros((states, width), F32)
    state, grad = lax.fori_loop(0, groups, body, (zero, zero))
    state_out[...] = state
    grad_out[...] = grad
    for d, message in enumerate(messages):
        message[0:states, :] = jnp.where(live[1] < (live[1] ^ (d + 1)), state, grad)
        message[states : states + 8, :] = stat_out[...]


def scan_kernel(
    skipped, order, cols, proj, rate, step, mixed, gate, grad_gated, state_in, grad_in, skip, dtproj,
    *rest,
):
    rank_before, bc_before = rest[skipped - 2 : skipped] if skipped else (None, None)
    rest = rest[skipped:]
    gated_out, gate_out, mix_out, rate_out, vec_out, dtproj_out, rank_out, bc_out, proj_grad = rest[:9]
    sends = rest[9:-11]
    (
        lanes, held, b_sum, c_sum, drive, y_sum, decay_sum, source_sum, raised_low, rank_low, grad_y
    ) = rest[-11:]
    rows, width = step.shape
    states = rate.shape[0]
    rank = dtproj.shape[0]
    half = states // 2
    reps = width // 128
    block = pl.program_id(0)

    @pl.when(block == 0)
    def _():
        fill_lanes(lanes, cols, rows)
        rank_low[...] = proj[:, :rank].astype(BF16)
        b_sum[...] = jnp.zeros_like(b_sum)
        c_sum[...] = jnp.zeros_like(c_sum)
        rank_out[...] = rank_before[...] if skipped else jnp.zeros_like(rank_out)

    rates = rate[...]
    groups = rows // 8
    sublane = lax.broadcasted_iota(jnp.int32, (8, width), 0)
    held[0] = state_in[...]

    def forward(i, state):
        parts = []
        row = pl.ds(pl.multiple_of(i * 8, 8), 8)
        drive[row, :] = step[row, :] * mixed[row, :]
        grad_y[row, :] = rounded_grad(gate[row, :], grad_gated[row, :])
        for r in range(8):
            p = i * 8 + r
            factor = jnp.exp2(rates * spread(step, p, states))
            b_wide = widened(lanes[p, 0:states], reps)
            c_wide = widened(lanes[p, states : 2 * states], reps)
            state = factor * state + spread(drive, p, states) * b_wide
            held[p + 1] = state
            seen = state * c_wide
            parts.append(seen[:half] + seen[half:])
        y_sum[row, :] = sums_to_rows(parts, sublane)
        return state

    lax.fori_loop(0, groups, forward, state_in[...])

    def over_tiles(value):
        total = value[:, 0:128]
        for t in range(1, reps):
            total = total + value[:, 128 * t : 128 * t + 128]
        return total

    def backward(k, carry):
        grad_next, rate_sum = carry
        i = groups - 1 - k
        decay_parts = [None] * 8
        source_parts = [None] * 8
        here = held[i * 8 + 8]
        for r in range(7, -1, -1):
            p = i * 8 + r
            step_wide = spread(step, p, states)
            y_wide = spread(grad_y, p, states)
            factor = jnp.exp2(rates * step_wide)
            b_wide = widened(lanes[p, 0:states], reps)
            c_wide = widened(lanes[p, states : 2 * states], reps)
            grad = grad_next + y_wide * c_wide
            before = held[p]
            grad_next = factor * grad
            c_sum[p] += over_tiles(here * y_wide)
            b_sum[p] += over_tiles(grad * spread(drive, p, states))
            through = grad_next * before
            decay = through * rates
            rate_sum = rate_sum + through * step_wide
            source = grad * b_wide
            decay_parts[r] = decay[:half] + decay[half:]
            source_parts[r] = source[:half] + source[half:]
            here = before
        row = pl.ds(pl.multiple_of(i * 8, 8), 8)
        decay_sum[row, :] = sums_to_rows(decay_parts, sublane)
        source_sum[row, :] = sums_to_rows(source_parts, sublane)
        return grad_next, rate_sum

    zero = jnp.zeros((states, width), F32)
    unused, rate_sum = lax.fori_loop(0, groups, backward, (grad_in[...], zero))
    rate_out[...] = rate_sum * (rates * LN2)

    gain = skip[...]
    count = SCAN_ROWS
    zero8 = jnp.zeros((8, width), F32)

    def finish(i, sums):
        at = pl.ds(pl.multiple_of(i * count, count), count)
        value = gate[at, :]
        mix = mixed[at, :]
        upstream = grad_gated[at, :]
        full_y = y_sum[at, :] + gain * mix
        squash = logistic(value)
        act = value * squash
        gated = (full_y * act).astype(BF16)
        grad_gate = (upstream * full_y * squash * (1.0 + value * (1.0 - squash))).astype(BF16)
        gated_out[at, :] = gated
        gate_out[at, :] = grad_gate
        grad_full = upstream * act
        source = source_sum[at, :]
        width_step = step[at, :]
        grad_raised = (LN2 * decay_sum[at, :] + mix * source) * (1.0 - jnp.exp(-width_step))
        raised_low[at, :] = grad_raised.astype(BF16)
        mix_out[at, :] = width_step * source + grad_full * gain
        return sums[0] + by_eight(grad_raised), sums[1] + by_eight(grad_full * mix)

    sums = lax.fori_loop(0, rows // count, finish, (zero8, zero8))
    for d, send in enumerate(sends):

        @pl.when(block == d)
        def _(send=send):
            send[:, 0:width] = gated_out[...]
            send[:, width : 2 * width] = gate_out[...]

    vec_out[...] = zero8
    for k in range(2):
        vec_out[k : k + 1, :] = jnp.sum(sums[k], axis=0, keepdims=True)
    dtproj_out[...] = dot(raised_low[...], rank_low[...], ((0,), (0,)))
    rank_out[...] += dot(raised_low[...], dtproj[...], ((1,), (1,)))

    @pl.when(block == pl.num_programs(0) - 1)
    def _():
        lane = lax.broadcasted_iota(jnp.int32, (states, 128), 1)

        def tile(j, unused):
            def gather(i, carry):
                b_tile, c_tile = carry
                for r in range(64):
                    p = j * 128 + i * 64 + r
                    here = lane == i * 64 + r
                    b_tile = jnp.where(here, jnp.sum(b_sum[p], axis=1, keepdims=True), b_tile)
                    c_tile = jnp.where(here, jnp.sum(c_sum[p], axis=1, keepdims=True), c_tile)
                return b_tile, c_tile

            zero_tile = jnp.zeros((states, 128), F32)
            b_tile, c_tile = lax.fori_loop(0, 2, gather, (zero_tile, zero_tile))
            at = pl.ds(pl.multiple_of(j * 128, 128), 128)
            bc_out[0:states, at] = b_tile
            bc_out[states : 2 * states, at] = c_tile
            return 0

        lax.fori_loop(0, rows // 128, tile, 0)
        if skipped:
            bc_out[...] += bc_before[...]
        turned = jnp.transpose(bc_out[...])
        proj_grad[...] = jnp.concatenate(
            [rank_out[...], turned, jnp.zeros((rows, 128 - rank - 2 * states), F32)], axis=1
        ).astype(BF16)


def back_kernel(
    skipped, order, proj_grad, xproj, mix_grad, inner, before, ahead, conv_w, conv_b, rate_sums, scan_sums, step_sums,
    dtproj_grad, *rest,
):
    thin_before = rest[1] if skipped else None
    inner_out, thin_out, *rest = rest[skipped:]
    sends, (ext, pre_ext, low, mixed_grad) = rest[:-4], rest[-4:]
    rows, width = mix_grad.shape
    taps = conv_w.shape[0]
    states = rate_sums.shape[0]
    block = pl.program_id(0)
    if skipped:

        @pl.when(block == 0)
        def _():
            thin_out[...] = thin_before[...]

    widen_rows(ext, before, inner)
    weight = conv_w[...]
    bias = conv_b[...]
    pre_ext[rows : rows + 8, :] = ahead[...]
    mixed_grad[...] = mix_grad[...] + jnp.dot(proj_grad[...], xproj[...], preferred_element_type=F32)
    zero8 = jnp.zeros((8, width), F32)

    def chunk(i, sums):
        at = pl.multiple_of(i * BACK_ROWS, BACK_ROWS)
        window = ext[pl.ds(at, BACK_ROWS + 8), :]
        pre = conv_window(window, weight, bias, BACK_ROWS)
        squash = logistic(pre)
        low[pl.ds(at, BACK_ROWS), :] = (pre * squash).astype(BF16)
        grad_pre = mixed_grad[pl.ds(at, BACK_ROWS), :] * squash * (1.0 + pre * (1.0 - squash))
        pre_ext[pl.ds(at, BACK_ROWS), :] = grad_pre
        added = [sums[taps] + by_eight(grad_pre)]
        for k in range(taps - 1, -1, -1):
            shift = taps - 1 - k
            added.insert(0, sums[k] + by_eight(grad_pre * window[8 - shift : 8 + BACK_ROWS - shift]))
        return tuple(added)

    sums = lax.fori_loop(0, rows // BACK_ROWS, chunk, (zero8,) * (taps + 1))

    summed = jnp.concatenate(
        [rate_sums[...], scan_sums[0:2, :], step_sums[1:3, :]]
        + [jnp.sum(v, axis=0, keepdims=True) for v in sums]
        + [jnp.zeros((32 - states - 5 - taps, width), F32)],
        axis=0,
    )
    high = summed.astype(BF16)
    words = jnp.concatenate([high, (summed - high.astype(F32)).astype(BF16)], axis=0)

    xproj_grad = dot(low[...], proj_grad[...], ((0,), (0,)))
    xproj_grad = xproj_grad.astype(BF16)
    step_grad = dtproj_grad[...].astype(BF16)
    group, entries, thin, _ = thin_out.shape
    seqs = width // thin
    side = seqs // (entries - seqs)
    me = order[len(sends)]
    for c in range(seqs):
        chunk_index = order[block] * seqs + c
        place = lax.rem(chunk_index, group) ^ me
        thin_out[place, chunk_index // group] = xproj_grad[c * thin : (c + 1) * thin]
    for c in range(0, seqs, side * group):
        for t in range(group):
            parts = [
                step_grad[(c + k * group + t) * thin : (c + k * group + t + 1) * thin] for k in range(side)
            ]
            parts += [jnp.zeros_like(parts[0])] * (2 - side)
            at = (order[block] * seqs + c) // (group * side)
            thin_out[t ^ me, seqs + at] = jnp.concatenate(parts, axis=1)

    def spread_back(i, unused):
        at = pl.multiple_of(i * BACK_ROWS, BACK_ROWS)
        window = pre_ext[pl.ds(at, BACK_ROWS + 8), :]
        total = weight[taps - 1 : taps] * window[0:BACK_ROWS]
        for s in range(1, taps):
            total = total + weight[taps - 1 - s : taps - s] * window[s : s + BACK_ROWS]
        inner_out[pl.ds(at, BACK_ROWS), :] = total.astype(BF16)
        return 0

    lax.fori_loop(0, rows // BACK_ROWS, spread_back, 0)
    for d, send in enumerate(sends):

        @pl.when(block == d)
        def _(send=send):
            send[0:rows, :] = inner_out[...]
            send[rows : rows + 64, :] = words


def put_chunks(targets, total, core, step, entry, high, first_row, fold):
    width = targets[0].shape[1]
    rows = high // fold
    each = total.shape[0] // rows
    for c in range(each):
        first = pl.multiple_of((step * each + c) // 2 * entry, 8) + first_row
        for parity in range(2):

            @pl.when(lax.rem(core + c, 2) == parity)
            def _(parity=parity, first=first, c=c):
                for f in range(fold):
                    targets[parity][pl.ds(first + f * rows, rows), :] = total[
                        c * rows : (c + 1) * rows, f * width : (f + 1) * width
                    ]


def summed_products(lefts, rights):
    total = None
    for left, right in zip(lefts, rights):
        part = dot(left, right, ((0,), (0,)))
        total = part if total is None else total + part
    return total


def wide_kernel(high, at, *refs):
    count = (len(refs) - 2) // 4
    outs, gates, masked, normed = (refs[k * count : (k + 1) * count] for k in range(4))
    targets = refs[-2:]
    width = targets[0].shape[1]
    total = summed_products([r[...] for r in outs], [r[...] for r in masked])
    fold = masked[0].shape[1] // width
    step = pl.program_id(0)
    put_chunks(targets, total, at[0], step, 2 * high, high, 0, fold)
    total = summed_products([r[...] for r in normed], [r[...] for r in gates])
    put_chunks(targets, total, at[0], step, 2 * high, high, high, 1)


def sum_rows(used, gains):
    return -(-(used + gains + 1) // 16) * 16


def inner_kernel(total_chunks, used, at, *refs):
    count = (len(refs) - 4) // 3
    normed, inners, thins = (refs[k * count : (k + 1) * count] for k in range(3))
    gain, live = refs[3 * count : 3 * count + 2]
    targets = refs[-2:]
    core = at[0]
    rows = normed[0].shape[0]
    width = inners[0].shape[1]
    entries, thin, _ = thins[0].shape
    columns = 256
    seqs = total_chunks
    side = seqs // (entries - seqs)
    chips = seqs // 2
    extra = sum_rows(used, gain.shape[0])
    entry = (targets[0].shape[0] - extra) // chips
    packed = thin * columns // width
    high = entry - packed
    step = pl.program_id(0)
    total = summed_products([r[...] for r in normed], [r[0:rows, :] for r in inners])
    each = total.shape[0] // high
    for c in range(each):
        first = pl.multiple_of((step * each + c) // 2 * entry, 8)
        for parity in range(2):

            @pl.when(lax.rem(core + c, 2) == parity)
            def _(parity=parity, first=first, c=c):
                targets[parity][pl.ds(first, high), :] = total[c * high : (c + 1) * high]

    @pl.when(step == 0)
    def _():
        for i in range(seqs):
            value = thins[0][i].astype(F32)
            near = thins[0][seqs + i // side].astype(F32)
            for r in thins[1:]:
                value = value + r[i].astype(F32)
                near = near + r[seqs + i // side].astype(F32)
            at_lane = (i % side) * 64
            near = near[:, at_lane : at_lane + 64]
            value = jnp.concatenate([value, near, jnp.zeros_like(near)], axis=1)
            first = i // 2 * entry + high
            for parity in range(2):

                @pl.when(lax.rem(core + i, 2) == parity)
                def _(parity=parity, first=first, value=value):
                    if columns >= width:
                        for f in range(columns // width):
                            targets[parity][first + f * thin : first + (f + 1) * thin, :] = value[
                                :, f * width : (f + 1) * width
                            ]
                    else:
                        for f in range(width // columns):
                            targets[parity][
                                first : first + packed, f * columns : (f + 1) * columns
                            ] = value[f * packed : (f + 1) * packed]

        sums = None
        for r in inners:
            words = r[rows : rows + 64, :]
            value = words[0:32].astype(F32) + words[32:64].astype(F32)
            sums = value if sums is None else sums + value
        tail = jnp.concatenate(
            [
                sums[0:used],
                gain[...],
                jnp.full((extra - used - gain.shape[0], width), live[0], F32),
            ],
            axis=0,
        )
        for target in targets:
            target[chips * entry : chips * entry + extra, :] = tail


def assemble_kernel(
    at, *refs
):
    in_out, out_out, xproj_out, dtproj_out, conv_out, bias_out, dtb_out, skip_out, mean_out, spread_out = refs[-13:-3]
    a_out, gain_out, narrow = refs[-3:]
    count = (len(refs) - 13) // 2
    wides, lasts = refs[:count], refs[count : 2 * count]
    high = in_out.shape[0]
    channels = in_out.shape[1] // 2
    width = wides[0].shape[1]
    fold = out_out.shape[1] // width
    strip = high // fold
    thin, columns = narrow.shape[0] // count, narrow.shape[1]
    packed = thin * columns // width
    taps = conv_out.shape[0]
    mine = a_out.shape[0]
    states = mine * count
    rest = None
    for d in range(count):
        them = at[d + 1]
        lanes = pl.ds(pl.multiple_of(them * width, 128), width)
        half = (lasts[d].shape[0] - high) // 2
        words = lasts[d][high : high + half, :].astype(F32) + lasts[d][high + half :, :].astype(F32)
        piece = words[packed:]
        in_out[:, lanes] = lasts[d][0:high, :].astype(F32)
        in_out[:, pl.ds(pl.multiple_of(channels + them * width, 128), width)] = wides[d][
            high : 2 * high, :
        ].astype(F32)
        for f in range(fold):
            rows = pl.ds(pl.multiple_of(at[1 + count + d] * strip, 8), strip)
            out_out[rows, f * width : (f + 1) * width] = wides[d][f * strip : (f + 1) * strip, :].astype(F32)
        if columns >= width:
            for f in range(columns // width):
                rows = pl.ds(pl.multiple_of(them * thin, 8), thin)
                narrow[rows, f * width : (f + 1) * width] = words[f * thin : (f + 1) * thin]
        else:
            for f in range(width // columns):
                rows = pl.ds(pl.multiple_of(them * thin + f * packed, 8), packed)
                narrow[rows, :] = words[0:packed, f * columns : (f + 1) * columns]
        for k in range(count):

            @pl.when(at[1] == k)
            def _(k=k, lanes=lanes, piece=piece):
                a_out[:, lanes] = piece[k * mine : (k + 1) * mine]

        dtb_out[:, lanes] = piece[states : states + 1]
        skip_out[:, lanes] = piece[states + 1 : states + 2]
        mean_out[:, lanes] = piece[states + 2 : states + 3]
        spread_out[:, lanes] = piece[states + 3 : states + 4]
        conv_out[:, lanes] = piece[states + 4 : states + 4 + taps]
        bias_out[:, lanes] = piece[states + 4 + taps : states + 5 + taps]
        tail = piece[states + 5 + taps : states + 6 + taps + fold]
        rest = tail if rest is None else rest + tail
    turned = jnp.transpose(narrow[...])
    xproj_out[...] = turned[0 : xproj_out.shape[0]]
    dtproj_out[...] = turned[128 : 128 + dtproj_out.shape[0]]
    for f in range(fold):
        gain_out[:, f * width : (f + 1) * width] = rest[f : f + 1]
    live = rest[fold : fold + 1, 0:1]
    mean = mean_out[...] / live
    spread = spread_out[...] / live - mean * mean + 1e-06
    mean_out[...] = mean
    spread_out[...] = jnp.sqrt(spread)


def struct(*shape, dtype=F32):
    return jax.ShapeDtypeStruct(shape, dtype)


def whole(shape):
    return pl.BlockSpec(shape, lambda *unused: (0,) * len(shape))


LIMIT = pltpu.CompilerParams(vmem_limit_bytes=63 << 20)


def front(normed, halo, in_weight, conv_weight, conv_bias, xproj, width):
    rows, features = normed.shape
    channels = in_weight.shape[1] // 2

    def part(height):
        return pl.BlockSpec((height, width), lambda q: (0, q))

    return pl.pallas_call(
        front_kernel,
        grid=(channels // width,),
        in_specs=[
            whole(normed.shape), whole(halo.shape), part(features), part(conv_weight.shape[0]), part(1),
            part(xproj.shape[0]),
        ],
        out_specs=[part(rows), whole((rows, xproj.shape[0])), part(rows), part(8)],
        out_shape=[
            struct(rows, channels), struct(rows, xproj.shape[0]), struct(rows, channels, dtype=BF16),
            struct(8, channels, dtype=BF16),
        ],
        scratch_shapes=[pltpu.VMEM((rows + 8, width), F32), pltpu.VMEM((rows, width), BF16)],
        compiler_params=LIMIT,
        cost_estimate=cost(8),
        name="front",
    )(normed, halo, in_weight, conv_weight, conv_bias, xproj)


def local_ends(live, proj, dtproj, dt_bias, mixed, normed, in_weight, masked, out_weight, rate, width):
    rows, channels = mixed.shape
    features = normed.shape[1]
    states = rate.shape[0]
    rank = dtproj.shape[0]
    group = channels // width

    def part(height):
        return pl.BlockSpec((height, width), lambda q: (0, q))

    return pl.pallas_call(
        ends_kernel,
        grid=(channels // width,),
        in_specs=[
            pl.BlockSpec(memory_space=pltpu.SMEM), whole(proj.shape),
            part(rank), part(1), part(rows), whole(normed.shape),
            pl.BlockSpec((features, width), lambda q: (0, q + group)), whole(masked.shape),
            pl.BlockSpec((width, features), lambda q: (q, 0)), part(states),
        ],
        out_specs=[part(rows)] * 3 + [part(8), part(states), part(states), whole((2 * states, rows))]
        + [part(states + 8)] * (group - 1),
        out_shape=[struct(rows, channels)] * 3
        + [struct(8, channels), struct(states, channels), struct(states, channels), struct(2 * states, rows)]
        + [struct(states + 8, channels)] * (group - 1),
        scratch_shapes=[
            pltpu.VMEM((rows, 2 * states, 128), F32),
            pltpu.VMEM((rows, width), F32),
            pltpu.VMEM((rows, rank), BF16),
            pltpu.VMEM((rows, width), F32),
            pltpu.VMEM((rows, width), F32),
        ],
        compiler_params=LIMIT,
        cost_estimate=cost(40),
        name="ends",
    )(live, proj, dtproj, dt_bias, mixed, normed, in_weight, masked, out_weight, rate)


def full_scan(
    order, cols, proj, rate, step, mixed, gate, grad_gated, state_in, grad_in, skip, dtproj, earlier,
):
    rows, channels = step.shape
    states = rate.shape[0]
    rank = dtproj.shape[0]
    width = channels // lax.axis_size("state")
    blocks = order.shape[0]

    def part(height):
        return pl.BlockSpec((height, width), lambda q, order: (0, order[q]))

    tall = pl.BlockSpec((width, rank), lambda q, order: (order[q], 0))
    rows_f32 = part(rows)
    in_specs = [
        whole(cols.shape), whole(proj.shape), part(states), rows_f32, rows_f32, rows_f32, rows_f32,
        part(states), part(states), part(1), part(rank),
    ]
    out_specs = [
        part(rows), part(rows), part(rows), part(states), part(8), tall, whole((rows, rank)),
        whole((2 * states, rows)), whole((rows, 128)),
    ] + [whole((rows, 2 * width))] * blocks
    out_shape = [
        struct(rows, channels, dtype=BF16), struct(rows, channels, dtype=BF16),
        struct(rows, channels), struct(states, channels),
        struct(8, channels), struct(channels, rank), struct(rows, rank), struct(2 * states, rows),
        struct(rows, 128, dtype=BF16),
    ] + [struct(rows, 2 * width, dtype=BF16)] * blocks
    args = [
        order, cols, proj, rate, step, mixed, gate, grad_gated, state_in, grad_in, skip, dtproj,
    ]
    aliases = {}
    for out, value in earlier:
        aliases[len(args)] = out
        args.append(value)
        in_specs.append(pl.BlockSpec(memory_space=pl.ANY) if out < 6 else whole(value.shape))
    block = pltpu.VMEM((rows, width), F32)
    return pl.pallas_call(
        functools.partial(scan_kernel, len(earlier)),
        grid_spec=pltpu.PrefetchScalarGridSpec(
            num_scalar_prefetch=1,
            grid=(blocks,),
            in_specs=in_specs,
            out_specs=out_specs,
            scratch_shapes=[
                pltpu.VMEM((rows, 2 * states, 128), F32),
                pltpu.VMEM((rows + 1, states, width), F32),
                pltpu.VMEM((rows, states, 128), F32),
                pltpu.VMEM((rows, states, 128), F32),
                block, block, block, block,
                pltpu.VMEM((rows, width), BF16),
                pltpu.VMEM((rows, rank), BF16),
                block,
            ],
        ),
        out_shape=out_shape,
        input_output_aliases=aliases,
        compiler_params=LIMIT,
        cost_estimate=cost(50),
        name="scan",
    )(*args)


def back(
    order, proj_grad, xproj, mix_grad, inner, before, ahead, conv_weight, conv_bias, rate_sums, scan_sums,
    step_sums, dtproj_grad, earlier,
):
    rows, channels = mix_grad.shape
    blocks = order.shape[0] - 1
    seqs = lax.axis_size("seq")
    group = lax.axis_size("state")
    width = channels // group
    thin = width // seqs
    side = min(2, seqs // group)
    rank = dtproj_grad.shape[1]

    def part(height):
        return pl.BlockSpec((height, width), lambda q, order: (0, order[q]))

    def tall(columns):
        return pl.BlockSpec((width, columns), lambda q, order: (order[q], 0))

    in_specs = [
        whole(proj_grad.shape), part(xproj.shape[0]), part(rows), part(rows), part(8), part(8),
        part(conv_weight.shape[0]), part(1), part(rate_sums.shape[0]), part(8), part(8), tall(rank),
    ]
    args = [
        order, proj_grad, xproj, mix_grad, inner, before, ahead, conv_weight, conv_bias, rate_sums,
        scan_sums, step_sums, dtproj_grad,
    ]
    aliases = {}
    for out, value in earlier:
        aliases[len(args)] = out
        args.append(value)
        in_specs.append(pl.BlockSpec(memory_space=pl.ANY) if out == 0 else whole(value.shape))
    return pl.pallas_call(
        functools.partial(back_kernel, len(earlier)),
        grid_spec=pltpu.PrefetchScalarGridSpec(
            num_scalar_prefetch=1,
            grid=(blocks,),
            in_specs=in_specs,
            out_specs=[part(rows), whole((group, seqs + seqs // side, thin, 128))]
            + [whole((rows + 64, width))] * blocks,
            scratch_shapes=[
                pltpu.VMEM((rows + 8, width), F32),
                pltpu.VMEM((rows + 8, width), F32),
                pltpu.VMEM((rows, width), BF16),
                pltpu.VMEM((rows, width), F32),
            ],
        ),
        out_shape=[
            struct(rows, channels, dtype=BF16), struct(group, seqs + seqs // side, thin, 128, dtype=BF16),
        ] + [struct(rows + 64, width, dtype=BF16)] * blocks,
        input_output_aliases=aliases,
        compiler_params=LIMIT,
        cost_estimate=cost(18),
        name="back",
    )(*args)


def cost(micros):
    return pl.CostEstimate(flops=int(micros), transcendentals=0, bytes_accessed=1024)


def places():
    me = lax.axis_index("state")
    core = lax.axis_index("seq") % 2
    group = lax.axis_size("state")
    base = lax.axis_index("seq") * group // lax.axis_size("seq")
    order = [me ^ d for d in range(group)]
    return jnp.stack([core] + order + [base ^ k for k in order]).astype(jnp.int32)


def wide_grads(gates, masked, normed, seqs):
    count = len(gates)
    rows = gates[0].shape[0]
    width = gates[0].shape[1] // 2
    features = masked[0].shape[1]
    steps = max(1, width // WIDE_STEP)
    high = features // seqs
    chips = seqs // 2
    fixed = pl.BlockSpec((rows, width), lambda i, at: (0, 1))
    part = pl.BlockSpec((rows, width // steps), lambda i, at: (0, i))

    wholly = pl.BlockSpec((rows, features), lambda i, at: (0, 0))
    partly = pl.BlockSpec((rows, features // steps), lambda i, at: (0, i))
    return pl.pallas_call(
        functools.partial(wide_kernel, high),
        grid_spec=pltpu.PrefetchScalarGridSpec(
            num_scalar_prefetch=1,
            grid=(steps,),
            in_specs=[part] * count + [fixed] * count
            + [wholly] * count + [partly] * count,
            out_specs=[whole((chips * 2 * high, width))] * 2,
        ),
        out_shape=[struct(chips * 2 * high, width)] * 2,
        compiler_params=LIMIT,
        cost_estimate=cost(10),
        name="wide",
    )(places(), *gates, *gates, *masked, *normed)


def inner_grads(normed, inners, thins, gain, live, seqs, used):
    count = len(inners)
    width = inners[0].shape[1]
    rows, features = normed[0].shape
    steps = max(1, width // WIDE_STEP)
    chips = seqs // 2
    entry = features // seqs + thins[0].shape[1] * 256 // width

    partly = pl.BlockSpec((rows, features // steps), lambda i, at: (0, i))
    shape = (chips * entry + sum_rows(used, gain.shape[0]), width)
    return pl.pallas_call(
        functools.partial(inner_kernel, seqs, used),
        grid_spec=pltpu.PrefetchScalarGridSpec(
            num_scalar_prefetch=1,
            grid=(steps,),
            in_specs=[partly] * count
            + [whole(inners[0].shape)] * count + [whole(thins[0].shape)] * count
            + [whole(gain.shape), pl.BlockSpec(memory_space=pltpu.SMEM)],
            out_specs=[whole(shape)] * 2,
        ),
        out_shape=[struct(*shape)] * 2,
        compiler_params=LIMIT,
        cost_estimate=cost(5),
        name="inner",
    )(places(), *normed, *inners, *thins, gain, live)


def assemble(wides, lasts, features, channels, seqs, taps, states, proj_width, rank):
    width = wides[0].shape[1]
    count = len(wides)
    rows = channels // seqs
    shapes = [
        (features // seqs, 2 * channels), (rows, features), (proj_width, rows), (rank, rows), (taps, channels),
        (1, channels), (1, channels), (1, channels), (1, channels), (1, channels),
        (states // count, channels), (1, features),
    ]
    return pl.pallas_call(
        assemble_kernel,
        in_specs=[pl.BlockSpec(memory_space=pltpu.SMEM)] + [pl.BlockSpec(memory_space=pltpu.VMEM)] * 2 * count,
        out_specs=[pl.BlockSpec(memory_space=pltpu.VMEM)] * len(shapes),
        out_shape=[struct(*shape) for shape in shapes],
        scratch_shapes=[pltpu.VMEM((rows, 256), F32)],
        compiler_params=LIMIT,
        cost_estimate=cost(4),
        name="assemble",
    )(places(), *wides, *lasts)


def dot(a, b, dims):
    return lax.dot_general(a, b, (dims, ((), ())), preferred_element_type=F32)


def body(
    tokens,
    lengths,
    grad_out,
    norm_gain,
    in_weight,
    conv_weight,
    conv_bias,
    xproj_weight,
    dtproj_weight,
    dt_bias,
    a_log,
    d_skip,
    out_weight,
):
    rows, features = tokens.shape
    channels = out_weight.shape[0]
    rank = dtproj_weight.shape[1]
    proj_width = xproj_weight.shape[1]
    states = (proj_width - rank) // 2
    taps = conv_weight.shape[0]
    group = lax.axis_size("state")
    seqs = lax.axis_size("seq")
    member = lax.axis_index("state")
    width = channels // group
    live_rows = jnp.clip(lengths - member * rows, 0, rows)
    alive = (jnp.arange(rows, dtype=jnp.int32) < live_rows[0]).astype(F32)[:, None]
    conv_row = conv_bias[None]
    xproj = jnp.pad(xproj_weight.T, ((0, 128 - proj_width), (0, 0)))

    a_full = placed(gathered(a_log), 0)
    rate2 = -jnp.exp(a_full) * LOG2E
    cotangent = grad_out.astype(F32)
    masked_low = (cotangent * alive).astype(BF16)
    inputs = tokens.astype(F32)
    inv_scale = lax.rsqrt(jnp.mean(inputs * inputs, axis=1, keepdims=True) + EPSILON)
    normed = inputs * inv_scale
    normed_low = (normed * norm_gain).astype(BF16)
    halo = shifted(normed_low[rows - 8 :], "state", 1)
    mixed, proj, inner, before = front(normed_low, halo, in_weight, conv_weight, conv_row, xproj, width)

    near = [d for d in range(1, group) if d & (d - 1) == 0]
    normed_late, mixed = lax.optimization_barrier((normed_low, mixed))
    normed_near = [swapped(normed_late, d) for d in near]
    step, gate_in, grad_gated, stats, state_end, grad_end, cols, *offers = local_ends(
        jnp.stack([live_rows[0], member]), proj, dtproj_weight.T, dt_bias[None], mixed, normed_low, in_weight,
        masked_low, out_weight, rate2, width,
    )
    *normed_near, offers = lax.optimization_barrier((*normed_near, offers))
    normed_pieces = {0: normed_low, **dict(zip(near, normed_near))}

    pieces = [jnp.concatenate([state_end, stats], axis=0)]
    pieces += [swapped(offer, d + 1) for d, offer in enumerate(offers)]
    pieces = jnp.stack(pieces)
    state_in = jnp.zeros((states, channels), F32)
    grad_in = jnp.zeros((states, channels), F32)
    for k in range(group - 1):
        one = lax.dynamic_index_in_dim(pieces, member ^ k, 0, keepdims=False)
        passed = one[:states] + jnp.exp2(rate2 * one[states : states + 1]) * state_in
        state_in = jnp.where(k < member, passed, state_in)
    for k in range(group - 1, 0, -1):
        one = lax.dynamic_index_in_dim(pieces, member ^ k, 0, keepdims=False)
        passed = one[:states] + jnp.exp2(rate2 * one[states : states + 1]) * grad_in
        grad_in = jnp.where(k > member, passed, grad_in)

    masked_late, state_in = lax.optimization_barrier((masked_low, state_in))
    masked_pieces = gathered(masked_late)

    first = list(range(1, group // 2 + 1))
    second = list(range(group // 2 + 1, group)) + [0]
    call = (cols, proj, rate2, step, mixed, gate_in, grad_gated, state_in, grad_in)
    call += (d_skip[None], dtproj_weight.T)
    one = list(full_scan(jnp.stack([member ^ d for d in first]), *call, []))
    *masked_pieces, normed_late, one[0] = lax.optimization_barrier((*masked_pieces, normed_low, one[0]))
    normed_pieces.update({d: swapped(normed_late, d) for d in range(1, group) if d not in near})
    normed_pieces = [normed_pieces[d] for d in range(group)]
    gates = {d: swapped(one[9 + q], d) for q, d in enumerate(first)}
    shared = [(k, one[k]) for k in range(8)]
    two = full_scan(jnp.stack([member ^ d for d in second]), *call, shared)
    gated_low, grad_gate_low, mix_grad, grad_a, scan_sums, grad_dtproj = two[:6]
    first_gates = [gates[d] for d in first]
    normed_pieces, *first_gates, grad_proj = lax.optimization_barrier((normed_pieces, *first_gates, two[8]))
    gates.update(dict(zip(first, first_gates)))

    window = jnp.concatenate([before, inner[:8]], axis=0).astype(F32)
    head_pre = conv_window(window, conv_weight, conv_row, 8)
    head_squash = jax.nn.sigmoid(head_pre)
    head_mixed = mix_grad[:8] + jnp.dot(grad_proj[:8], xproj, preferred_element_type=F32)
    head_grad = head_mixed * head_squash * (1.0 + head_pre * (1.0 - head_squash))
    ahead = shifted(head_grad, "state", -1)
    late_sends = [two[9 + q] for q in range(len(second))]
    ahead, *late_sends = lax.optimization_barrier((ahead, *late_sends))
    gates.update({d: swapped(v, d) if d else v for d, v in zip(second, late_sends)})
    call = (grad_proj, xproj, mix_grad, inner, before, ahead, conv_weight, conv_row, grad_a, scan_sums, stats)
    call += (grad_dtproj,)
    one = back(jnp.stack([member ^ d for d in first] + [member]), *call, [])
    inner_pieces = {d: swapped(one[2 + q], d) for q, d in enumerate(first)}
    two = back(jnp.stack([member ^ d for d in second] + [member]), *call, [(0, one[0]), (1, one[1])])
    grad_inner_low, thin_sends = two[:2]
    inner_pieces.update({d: swapped(two[2 + q], d) if d else two[2 + q] for q, d in enumerate(second)})
    thin_pieces = [thin_sends[0]] + [swapped(thin_sends[d], d) for d in range(1, group)]
    arrived = [inner_pieces[d] for d in first]
    gates, arrived, thin_sends = lax.optimization_barrier((gates, arrived, thin_sends))
    inner_pieces.update(dict(zip(first, arrived)))
    inner_pieces = [inner_pieces[d] for d in range(group)]
    fold = features // width
    high = features // seqs
    thin = width // seqs
    thin_rows = thin * 256 // width
    used = states + 5 + taps

    wide = wide_grads([gates[d] for d in range(group)], masked_pieces, normed_pieces, seqs)
    wide, _, (inner_pieces, thin_pieces), (gated_late, grad_gate_low) = seq_scatter(
        *wide, hold=(inner_pieces, thin_pieces), late=(gated_low, grad_gate_low)
    )
    branch = jnp.dot(gated_late, out_weight, preferred_element_type=F32)
    output = (inputs + alive * branch).astype(BF16)
    wide = wide.astype(BF16)
    owned = to_owner(wide[:high])

    grad_normed = dot(grad_inner_low, in_weight[:, :channels], ((1,), (1,))) + dot(
        grad_gate_low, in_weight[:, channels:], ((1,), (1,))
    )
    gain_part = jnp.sum(grad_normed * normed, axis=0).reshape(fold, width)
    scaled = grad_normed * norm_gain
    grad_tokens = cotangent + inv_scale * (
        scaled - normed * jnp.mean(scaled * normed, axis=1, keepdims=True)
    )

    last = inner_grads(normed_pieces, inner_pieces, thin_pieces, gain_part, live_rows.astype(F32), seqs, used)
    last, sums, _, owned = seq_scatter(*last, extra=sum_rows(used, fold), late=owned)
    wide_pieces = gathered(jnp.concatenate([owned, wide[high:]], axis=0))
    *wide_pieces, last, sums = lax.optimization_barrier((*wide_pieces, last, sums))
    words = two_words(jnp.concatenate([last[high:], sums], axis=0))
    last = gathered(jnp.concatenate([last[:high].astype(BF16), words], axis=0))

    (
        grad_in_w, grad_out_w, grad_xproj, grad_dtproj, grad_conv, grad_bias, grad_dtb, grad_skip, dt_mean,
        dt_spread, grad_a_log, grad_gain,
    ) = assemble(
        wide_pieces, last, features, channels, seqs, taps, states, proj_width, rank
    )
    return (
        output,
        grad_tokens,
        grad_gain[0],
        grad_in_w,
        grad_conv,
        grad_bias[0],
        grad_xproj.T,
        grad_dtproj.T,
        grad_dtb[0],
        grad_a_log,
        grad_skip[0],
        grad_out_w,
        dt_mean[0],
        dt_spread[0],
    )


def solution(mesh):
    rows = P(("seq", "state"), None)
    return jax.shard_map(
        body,
        mesh=mesh,
        in_specs=(rows, P("seq"), rows) + (P(),) * 7 + (P("state", None), P(), P()),
        out_specs=(rows, rows, P(), P("seq", None), P(), P(), P("seq", None), P("seq", None), P())
        + (P("state", None), P(), P("seq", None), P(), P()),
        check_vma=False,
    )
```

```python
import functools

import jax
import jax.numpy as jnp
from jax import lax
from jax.experimental import pallas as pl
from jax.experimental.pallas import tpu as pltpu
from jax.sharding import PartitionSpec as P

EPSILON = 1e-05
LOG2E = 1.4426950408889634
LN2 = 0.6931471805599453
F32 = jnp.float32
BF16 = jnp.bfloat16
ENDS_ROWS = 128
SCAN_ROWS = 64
BACK_ROWS = 128
WIDE_STEP = 256


def swapped(value, distance):
    count = lax.axis_size("state")
    return lax.ppermute(value, "state", [(i, i ^ distance) for i in range(count)])


def shifted(value, axis, steps):
    count = lax.axis_size(axis)
    leading, last = (max(0, -steps), min(count, count - steps))
    return lax.ppermute(value, axis, [(source, source + steps) for source in range(leading, last)])


def rotated(value, axis, steps):
    count = lax.axis_size(axis)
    return lax.ppermute(value, axis, [(i, (i + steps) % count) for i in range(count)])


def gathered(value):
    count = lax.axis_size("state")
    return [value] + [swapped(value, d) for d in range(1, count)]


def two_words(value):
    high = lax.reduce_precision(value, 8, 7)
    return jnp.concatenate([high.astype(BF16), (value - high).astype(BF16)], axis=0)


def one_word(value):
    count = value.shape[0] // 2
    return value[:count].astype(F32) + value[count:].astype(F32)


def seq_exchange(value, distance):
    count = lax.axis_size("seq")
    return lax.ppermute(value, "seq", [(i, i ^ distance) for i in range(count)])


def seq_scatter(mine, other, extra=0, hold=None, behind=None, late=None):
    seqs = lax.axis_size("seq")
    seq = lax.axis_index("seq")
    width = mine.shape[1]
    total = mine + seq_exchange(other, 1)
    if behind is not None:
        total, behind = lax.optimization_barrier((total, behind))
    chips = seqs // 2
    high = (total.shape[0] - extra) // chips
    total, sums = total[: chips * high], total[chips * high :]
    k = 1
    while chips > 1:
        chips //= 2
        total = total.reshape(chips, 2, high, width)
        bit = (seq >> k) & 1
        kept = lax.dynamic_index_in_dim(total, bit, 1, keepdims=False)
        away = lax.dynamic_index_in_dim(total, 1 - bit, 1, keepdims=False).astype(BF16)
        away = away.reshape(chips * high, width)
        if extra:
            away = jnp.concatenate([away, two_words(sums)], axis=0)
        got = seq_exchange(away, 1 << k)
        total = kept + got[: chips * high].astype(F32).reshape(kept.shape)
        if extra:
            sums = sums + one_word(got[chips * high :])
        if late is not None and k == 1:
            total, late = lax.optimization_barrier((total, late))
        k += 1
    total = total.reshape(high, width)
    if hold is not None:
        total, hold = lax.optimization_barrier((total, hold))
    return total, sums, hold, behind if late is None else late


def to_owner(value):
    seqs = lax.axis_size("seq")
    states = lax.axis_size("state")
    there = [(s * states + t, s * states + (t ^ (s % states))) for s in range(seqs) for t in range(states)]
    value = lax.ppermute(value, ("seq", "state"), there)
    pairs = [
        (s * states + (t ^ (s % states)), (t * seqs + s) // states * states + (t ^ (s % states)))
        for s in range(seqs)
        for t in range(states)
    ]
    return lax.ppermute(value, ("seq", "state"), pairs)


def placed(pieces, axis, out=None, start=0):
    me = lax.axis_index("state")
    size = pieces[0].shape[axis]
    if out is None:
        shape = list(pieces[0].shape)
        shape[axis] = size * len(pieces)
        out = jnp.zeros(shape, pieces[0].dtype)
    for d, piece in enumerate(pieces):
        out = lax.dynamic_update_slice_in_dim(out, piece, start + (me ^ d) * size, axis)
    return out


def fill_lanes(out_ref, cols_ref, rows):
    groups = min(32, rows // 8)
    states = cols_ref.shape[0]
    lanes = min(128, rows)

    def step(i, unused):
        tiles = []
        for u in range(groups):
            first = (i * groups + u) * 8
            base = pl.multiple_of((first // lanes) * lanes, lanes)
            tile = cols_ref[:, pl.ds(base, lanes)]
            tiles.append(pltpu.roll(tile, lax.rem(lanes - (first - base), lanes), axis=1))
        for u in range(groups):
            for r in range(8):
                out_ref[(i * groups + u) * 8 + r] = jnp.broadcast_to(
                    tiles[u][:, r : r + 1], (states, 128)
                )
        return 0

    lax.fori_loop(0, rows // (8 * groups), step, 0)


def sums_to_rows(values, sublane):
    step = 1
    while len(values) > 1:
        low = (sublane & step) == 0
        values = [
            jnp.where(low, a, b) + pltpu.roll(jnp.where(low, b, a), step, axis=0)
            for a, b in zip(values[::2], values[1::2])
        ]
        step *= 2
    return values[0]


def spread(ref, row, count):
    return jnp.broadcast_to(ref[pl.ds(row, 1), :], (count, ref.shape[1]))


def widened(value, times):
    return jnp.concatenate([value] * times, axis=1)


def conv_window(window, weight, bias, rows):
    taps = weight.shape[0]
    total = bias + weight[taps - 1 : taps] * window[8:]
    for s in range(1, taps):
        total = total + weight[taps - 1 - s : taps - s] * window[8 - s : 8 - s + rows]
    return total


def logistic(value):
    return 1.0 / (1.0 + jnp.exp(-value))


def rounded_grad(gate, grad_gated):
    return (grad_gated * (gate * logistic(gate))).astype(BF16).astype(F32)


def by_eight(value):
    total = value[0:8]
    for k in range(8, value.shape[0], 8):
        total = total + value[k : k + 8]
    return total


def widen_rows(ext, before, inner):
    rows = inner.shape[0]
    ext[0:8] = before[...].astype(F32)

    def move(i, unused):
        at = pl.multiple_of(i * 32, 32)
        ext[pl.ds(at + 8, 32), :] = inner[pl.ds(at, 32), :].astype(F32)
        return 0

    lax.fori_loop(0, rows // 32, move, 0)


def front_kernel(
    normed, halo, in_w, conv_w, conv_b, xproj, mixed_out, proj_out, inner, before, ext, low
):
    rows = inner.shape[0]

    @pl.when(pl.program_id(0) == 0)
    def _():
        proj_out[...] = jnp.zeros_like(proj_out)

    inner[...] = jnp.dot(normed[...], in_w[...], preferred_element_type=F32).astype(BF16)
    before[...] = jnp.dot(halo[...], in_w[...], preferred_element_type=F32).astype(BF16)
    widen_rows(ext, before, inner)
    weight = conv_w[...]
    bias = conv_b[...]

    def chunk(i, unused):
        at = pl.multiple_of(i * BACK_ROWS, BACK_ROWS)
        pre = conv_window(ext[pl.ds(at, BACK_ROWS + 8), :], weight, bias, BACK_ROWS)
        mixed = pre * logistic(pre)
        mixed_out[pl.ds(at, BACK_ROWS), :] = mixed
        low[pl.ds(at, BACK_ROWS), :] = mixed.astype(BF16)
        return 0

    lax.fori_loop(0, rows // BACK_ROWS, chunk, 0)
    proj_out[...] += dot(low[...], xproj[...], ((1,), (1,)))


def ends_kernel(
    live, proj, dtproj, dt_b, mixed, normed, gate_w, masked, out_w, rate,
    step_out, gate, grad_gated, stat_out, state_out, grad_out, cols_out, *rest,
):
    rows, width = mixed.shape
    states = rate.shape[0]
    rank = dtproj.shape[0]
    reps = width // 128
    messages, (lanes, drive, rank_low, raised_all, gy_out) = rest[:-5], rest[-5:]

    @pl.when(pl.program_id(0) == 0)
    def _():
        cols_out[...] = jnp.transpose(proj[...])[rank : rank + 2 * states]
        rank_low[...] = proj[:, :rank].astype(BF16)
        fill_lanes(lanes, cols_out, rows)

    gate[...] = jnp.dot(normed[...], gate_w[...], preferred_element_type=F32)
    grad_gated[...] = dot(masked[...], out_w[...], ((1,), (1,)))
    raised_all[...] = dt_b[...] + jnp.dot(rank_low[...], dtproj[...], preferred_element_type=F32)
    count = ENDS_ROWS
    zero8 = jnp.zeros((8, width), F32)

    def prepare(i, sums):
        at = pl.ds(pl.multiple_of(i * count, count), count)
        raised = raised_all[at, :]
        small = jnp.exp(-jnp.abs(raised))
        step = jnp.maximum(raised, 0.0) + jnp.log1p(small)
        step_out[at, :] = step
        drive[at, :] = step * mixed[at, :]
        gy_out[at, :] = rounded_grad(gate[at, :], grad_gated[at, :])
        row = i * count + lax.broadcasted_iota(jnp.int32, (count, width), 0)
        seen = jnp.where(row < live[0], step, 0.0)
        return sums[0] + by_eight(step), sums[1] + by_eight(seen), sums[2] + by_eight(seen * step)

    sums = lax.fori_loop(0, rows // count, prepare, (zero8, zero8, zero8))
    stat_out[...] = zero8
    for k in range(3):
        stat_out[k : k + 1, :] = jnp.sum(sums[k], axis=0, keepdims=True)

    rates = rate[...]
    groups = rows // 8

    def body(i, carry):
        state, grad = carry
        for r in range(8):
            p = i * 8 + r
            factor = jnp.exp2(rates * spread(step_out, p, states))
            b_wide = widened(lanes[p, 0:states], reps)
            state = factor * state + spread(drive, p, states) * b_wide
        for r in range(7, -1, -1):
            p = (groups - 1 - i) * 8 + r
            factor = jnp.exp2(rates * spread(step_out, p, states))
            c_wide = widened(lanes[p, states : 2 * states], reps)
            grad = factor * (grad + spread(gy_out, p, states) * c_wide)
        return state, grad

    zero = jnp.zeros((states, width), F32)
    state, grad = lax.fori_loop(0, groups, body, (zero, zero))
    state_out[...] = state
    grad_out[...] = grad
    for d, message in enumerate(messages):
        message[0:states, :] = jnp.where(live[1] < (live[1] ^ (d + 1)), state, grad)
        message[states : states + 8, :] = stat_out[...]


def scan_kernel(
    skipped, order, cols, proj, rate, step, mixed, gate, grad_gated, state_in, grad_in, skip, dtproj,
    *rest,
):
    rank_before, bc_before = rest[skipped - 2 : skipped] if skipped else (None, None)
    rest = rest[skipped:]
    gated_out, gate_out, mix_out, rate_out, vec_out, dtproj_out, rank_out, bc_out, proj_grad = rest[:9]
    sends = rest[9:-11]
    (
        lanes, held, b_sum, c_sum, drive, y_sum, decay_sum, source_sum, raised_low, rank_low, grad_y
    ) = rest[-11:]
    rows, width = step.shape
    states = rate.shape[0]
    rank = dtproj.shape[0]
    half = states // 2
    reps = width // 128
    block = pl.program_id(0)

    @pl.when(block == 0)
    def _():
        fill_lanes(lanes, cols, rows)
        rank_low[...] = proj[:, :rank].astype(BF16)
        b_sum[...] = jnp.zeros_like(b_sum)
        c_sum[...] = jnp.zeros_like(c_sum)
        rank_out[...] = rank_before[...] if skipped else jnp.zeros_like(rank_out)

    rates = rate[...]
    groups = rows // 8
    sublane = lax.broadcasted_iota(jnp.int32, (8, width), 0)
    held[0] = state_in[...]

    def forward(i, state):
        parts = []
        row = pl.ds(pl.multiple_of(i * 8, 8), 8)
        drive[row, :] = step[row, :] * mixed[row, :]
        grad_y[row, :] = rounded_grad(gate[row, :], grad_gated[row, :])
        for r in range(8):
            p = i * 8 + r
            factor = jnp.exp2(rates * spread(step, p, states))
            b_wide = widened(lanes[p, 0:states], reps)
            c_wide = widened(lanes[p, states : 2 * states], reps)
            state = factor * state + spread(drive, p, states) * b_wide
            held[p + 1] = state
            seen = state * c_wide
            parts.append(seen[:half] + seen[half:])
        y_sum[row, :] = sums_to_rows(parts, sublane)
        return state

    lax.fori_loop(0, groups, forward, state_in[...], unroll=2)

    def over_tiles(value):
        total = value[:, 0:128]
        for t in range(1, reps):
            total = total + value[:, 128 * t : 128 * t + 128]
        return total

    def backward(k, carry):
        grad_next, rate_sum = carry
        i = groups - 1 - k
        decay_parts = [None] * 8
        source_parts = [None] * 8
        here = held[i * 8 + 8]
        for r in range(7, -1, -1):
            p = i * 8 + r
            step_wide = spread(step, p, states)
            y_wide = spread(grad_y, p, states)
            factor = jnp.exp2(rates * step_wide)
            b_wide = widened(lanes[p, 0:states], reps)
            c_wide = widened(lanes[p, states : 2 * states], reps)
            grad = grad_next + y_wide * c_wide
            before = held[p]
            grad_next = factor * grad
            c_sum[p] += over_tiles(here * y_wide)
            b_sum[p] += over_tiles(grad * spread(drive, p, states))
            through = grad_next * before
            decay = through * rates
            rate_sum = rate_sum + through * step_wide
            source = grad * b_wide
            decay_parts[r] = decay[:half] + decay[half:]
            source_parts[r] = source[:half] + source[half:]
            here = before
        row = pl.ds(pl.multiple_of(i * 8, 8), 8)
        decay_sum[row, :] = sums_to_rows(decay_parts, sublane)
        source_sum[row, :] = sums_to_rows(source_parts, sublane)
        return grad_next, rate_sum

    zero = jnp.zeros((states, width), F32)
    unused, rate_sum = lax.fori_loop(0, groups, backward, (grad_in[...], zero))
    rate_out[...] = rate_sum * (rates * LN2)

    gain = skip[...]
    count = SCAN_ROWS
    zero8 = jnp.zeros((8, width), F32)

    def finish(i, sums):
        at = pl.ds(pl.multiple_of(i * count, count), count)
        value = gate[at, :]
        mix = mixed[at, :]
        upstream = grad_gated[at, :]
        full_y = y_sum[at, :] + gain * mix
        squash = logistic(value)
        act = value * squash
        gated = (full_y * act).astype(BF16)
        grad_gate = (upstream * full_y * squash * (1.0 + value * (1.0 - squash))).astype(BF16)
        gated_out[at, :] = gated
        gate_out[at, :] = grad_gate
        grad_full = upstream * act
        source = source_sum[at, :]
        width_step = step[at, :]
        grad_raised = (LN2 * decay_sum[at, :] + mix * source) * (1.0 - jnp.exp(-width_step))
        raised_low[at, :] = grad_raised.astype(BF16)
        mix_out[at, :] = width_step * source + grad_full * gain
        return sums[0] + by_eight(grad_raised), sums[1] + by_eight(grad_full * mix)

    sums = lax.fori_loop(0, rows // count, finish, (zero8, zero8))
    for d, send in enumerate(sends):

        @pl.when(block == d)
        def _(send=send):
            send[:, 0:width] = gated_out[...]
            send[:, width : 2 * width] = gate_out[...]

    vec_out[...] = zero8
    for k in range(2):
        vec_out[k : k + 1, :] = jnp.sum(sums[k], axis=0, keepdims=True)
    dtproj_out[...] = dot(raised_low[...], rank_low[...], ((0,), (0,)))
    rank_out[...] += dot(raised_low[...], dtproj[...], ((1,), (1,)))

    @pl.when(block == pl.num_programs(0) - 1)
    def _():
        lane = lax.broadcasted_iota(jnp.int32, (states, 128), 1)

        def tile(j, unused):
            def gather(i, carry):
                b_tile, c_tile = carry
                for r in range(64):
                    p = j * 128 + i * 64 + r
                    here = lane == i * 64 + r
                    b_tile = jnp.where(here, jnp.sum(b_sum[p], axis=1, keepdims=True), b_tile)
                    c_tile = jnp.where(here, jnp.sum(c_sum[p], axis=1, keepdims=True), c_tile)
                return b_tile, c_tile

            zero_tile = jnp.zeros((states, 128), F32)
            b_tile, c_tile = lax.fori_loop(0, 2, gather, (zero_tile, zero_tile))
            at = pl.ds(pl.multiple_of(j * 128, 128), 128)
            bc_out[0:states, at] = b_tile
            bc_out[states : 2 * states, at] = c_tile
            return 0

        lax.fori_loop(0, rows // 128, tile, 0)
        if skipped:
            bc_out[...] += bc_before[...]
        turned = jnp.transpose(bc_out[...])
        proj_grad[...] = jnp.concatenate(
            [rank_out[...], turned, jnp.zeros((rows, 128 - rank - 2 * states), F32)], axis=1
        ).astype(BF16)


def back_kernel(
    skipped, order, proj_grad, xproj, mix_grad, inner, before, ahead, conv_w, conv_b, rate_sums, scan_sums, step_sums,
    dtproj_grad, *rest,
):
    thin_before = rest[1] if skipped else None
    inner_out, thin_out, *rest = rest[skipped:]
    sends, (ext, pre_ext, low, mixed_grad) = rest[:-4], rest[-4:]
    rows, width = mix_grad.shape
    taps = conv_w.shape[0]
    states = rate_sums.shape[0]
    block = pl.program_id(0)
    if skipped:

        @pl.when(block == 0)
        def _():
            thin_out[...] = thin_before[...]

    widen_rows(ext, before, inner)
    weight = conv_w[...]
    bias = conv_b[...]
    pre_ext[rows : rows + 8, :] = ahead[...]
    mixed_grad[...] = mix_grad[...] + jnp.dot(proj_grad[...], xproj[...], preferred_element_type=F32)
    zero8 = jnp.zeros((8, width), F32)

    def chunk(i, sums):
        at = pl.multiple_of(i * BACK_ROWS, BACK_ROWS)
        window = ext[pl.ds(at, BACK_ROWS + 8), :]
        pre = conv_window(window, weight, bias, BACK_ROWS)
        squash = logistic(pre)
        low[pl.ds(at, BACK_ROWS), :] = (pre * squash).astype(BF16)
        grad_pre = mixed_grad[pl.ds(at, BACK_ROWS), :] * squash * (1.0 + pre * (1.0 - squash))
        pre_ext[pl.ds(at, BACK_ROWS), :] = grad_pre
        added = [sums[taps] + by_eight(grad_pre)]
        for k in range(taps - 1, -1, -1):
            shift = taps - 1 - k
            added.insert(0, sums[k] + by_eight(grad_pre * window[8 - shift : 8 + BACK_ROWS - shift]))
        return tuple(added)

    sums = lax.fori_loop(0, rows // BACK_ROWS, chunk, (zero8,) * (taps + 1))

    summed = jnp.concatenate(
        [rate_sums[...], scan_sums[0:2, :], step_sums[1:3, :]]
        + [jnp.sum(v, axis=0, keepdims=True) for v in sums]
        + [jnp.zeros((32 - states - 5 - taps, width), F32)],
        axis=0,
    )
    high = summed.astype(BF16)
    words = jnp.concatenate([high, (summed - high.astype(F32)).astype(BF16)], axis=0)

    xproj_grad = dot(low[...], proj_grad[...], ((0,), (0,)))
    xproj_grad = xproj_grad.astype(BF16)
    step_grad = dtproj_grad[...].astype(BF16)
    group, entries, thin, _ = thin_out.shape
    seqs = width // thin
    side = seqs // (entries - seqs)
    me = order[len(sends)]
    for c in range(seqs):
        chunk_index = order[block] * seqs + c
        place = lax.rem(chunk_index, group) ^ me
        thin_out[place, chunk_index // group] = xproj_grad[c * thin : (c + 1) * thin]
    for c in range(0, seqs, side * group):
        for t in range(group):
            parts = [
                step_grad[(c + k * group + t) * thin : (c + k * group + t + 1) * thin] for k in range(side)
            ]
            parts += [jnp.zeros_like(parts[0])] * (2 - side)
            at = (order[block] * seqs + c) // (group * side)
            thin_out[t ^ me, seqs + at] = jnp.concatenate(parts, axis=1)

    def spread_back(i, unused):
        at = pl.multiple_of(i * BACK_ROWS, BACK_ROWS)
        window = pre_ext[pl.ds(at, BACK_ROWS + 8), :]
        total = weight[taps - 1 : taps] * window[0:BACK_ROWS]
        for s in range(1, taps):
            total = total + weight[taps - 1 - s : taps - s] * window[s : s + BACK_ROWS]
        inner_out[pl.ds(at, BACK_ROWS), :] = total.astype(BF16)
        return 0

    lax.fori_loop(0, rows // BACK_ROWS, spread_back, 0)
    for d, send in enumerate(sends):

        @pl.when(block == d)
        def _(send=send):
            send[0:rows, :] = inner_out[...]
            send[rows : rows + 64, :] = words


def put_chunks(targets, total, core, step, entry, high, first_row, fold):
    width = targets[0].shape[1]
    rows = high // fold
    each = total.shape[0] // rows
    for c in range(each):
        first = pl.multiple_of((step * each + c) // 2 * entry, 8) + first_row
        for parity in range(2):

            @pl.when(lax.rem(core + c, 2) == parity)
            def _(parity=parity, first=first, c=c):
                for f in range(fold):
                    targets[parity][pl.ds(first + f * rows, rows), :] = total[
                        c * rows : (c + 1) * rows, f * width : (f + 1) * width
                    ]


def summed_products(lefts, rights):
    total = None
    for left, right in zip(lefts, rights):
        part = dot(left, right, ((0,), (0,)))
        total = part if total is None else total + part
    return total


def wide_kernel(high, at, *refs):
    count = (len(refs) - 2) // 4
    outs, gates, masked, normed = (refs[k * count : (k + 1) * count] for k in range(4))
    targets = refs[-2:]
    width = targets[0].shape[1]
    total = summed_products([r[...] for r in outs], [r[...] for r in masked])
    fold = masked[0].shape[1] // width
    step = pl.program_id(0)
    put_chunks(targets, total, at[0], step, 2 * high, high, 0, fold)
    total = summed_products([r[...] for r in normed], [r[...] for r in gates])
    put_chunks(targets, total, at[0], step, 2 * high, high, high, 1)


def sum_rows(used, gains):
    return -(-(used + gains + 1) // 16) * 16


def inner_kernel(total_chunks, used, at, *refs):
    count = (len(refs) - 4) // 3
    normed, inners, thins = (refs[k * count : (k + 1) * count] for k in range(3))
    gain, live = refs[3 * count : 3 * count + 2]
    targets = refs[-2:]
    core = at[0]
    rows = normed[0].shape[0]
    width = inners[0].shape[1]
    entries, thin, _ = thins[0].shape
    columns = 256
    seqs = total_chunks
    side = seqs // (entries - seqs)
    chips = seqs // 2
    extra = sum_rows(used, gain.shape[0])
    entry = (targets[0].shape[0] - extra) // chips
    packed = thin * columns // width
    high = entry - packed
    step = pl.program_id(0)
    total = summed_products([r[...] for r in normed], [r[0:rows, :] for r in inners])
    each = total.shape[0] // high
    for c in range(each):
        first = pl.multiple_of((step * each + c) // 2 * entry, 8)
        for parity in range(2):

            @pl.when(lax.rem(core + c, 2) == parity)
            def _(parity=parity, first=first, c=c):
                targets[parity][pl.ds(first, high), :] = total[c * high : (c + 1) * high]

    @pl.when(step == 0)
    def _():
        for i in range(seqs):
            value = thins[0][i].astype(F32)
            near = thins[0][seqs + i // side].astype(F32)
            for r in thins[1:]:
                value = value + r[i].astype(F32)
                near = near + r[seqs + i // side].astype(F32)
            at_lane = (i % side) * 64
            near = near[:, at_lane : at_lane + 64]
            value = jnp.concatenate([value, near, jnp.zeros_like(near)], axis=1)
            first = i // 2 * entry + high
            for parity in range(2):

                @pl.when(lax.rem(core + i, 2) == parity)
                def _(parity=parity, first=first, value=value):
                    if columns >= width:
                        for f in range(columns // width):
                            targets[parity][first + f * thin : first + (f + 1) * thin, :] = value[
                                :, f * width : (f + 1) * width
                            ]
                    else:
                        for f in range(width // columns):
                            targets[parity][
                                first : first + packed, f * columns : (f + 1) * columns
                            ] = value[f * packed : (f + 1) * packed]

        sums = None
        for r in inners:
            words = r[rows : rows + 64, :]
            value = words[0:32].astype(F32) + words[32:64].astype(F32)
            sums = value if sums is None else sums + value
        tail = jnp.concatenate(
            [
                sums[0:used],
                gain[...],
                jnp.full((extra - used - gain.shape[0], width), live[0], F32),
            ],
            axis=0,
        )
        for target in targets:
            target[chips * entry : chips * entry + extra, :] = tail


def assemble_kernel(
    at, *refs
):
    in_out, out_out, xproj_out, dtproj_out, conv_out, bias_out, dtb_out, skip_out, mean_out, spread_out = refs[-13:-3]
    a_out, gain_out, narrow = refs[-3:]
    count = (len(refs) - 13) // 2
    wides, lasts = refs[:count], refs[count : 2 * count]
    high = in_out.shape[0]
    channels = in_out.shape[1] // 2
    width = wides[0].shape[1]
    fold = out_out.shape[1] // width
    strip = high // fold
    thin, columns = narrow.shape[0] // count, narrow.shape[1]
    packed = thin * columns // width
    taps = conv_out.shape[0]
    mine = a_out.shape[0]
    states = mine * count
    rest = None
    for d in range(count):
        them = at[d + 1]
        lanes = pl.ds(pl.multiple_of(them * width, 128), width)
        half = (lasts[d].shape[0] - high) // 2
        words = lasts[d][high : high + half, :].astype(F32) + lasts[d][high + half :, :].astype(F32)
        piece = words[packed:]
        in_out[:, lanes] = lasts[d][0:high, :].astype(F32)
        in_out[:, pl.ds(pl.multiple_of(channels + them * width, 128), width)] = wides[d][
            high : 2 * high, :
        ].astype(F32)
        for f in range(fold):
            rows = pl.ds(pl.multiple_of(at[1 + count + d] * strip, 8), strip)
            out_out[rows, f * width : (f + 1) * width] = wides[d][f * strip : (f + 1) * strip, :].astype(F32)
        if columns >= width:
            for f in range(columns // width):
                rows = pl.ds(pl.multiple_of(them * thin, 8), thin)
                narrow[rows, f * width : (f + 1) * width] = words[f * thin : (f + 1) * thin]
        else:
            for f in range(width // columns):
                rows = pl.ds(pl.multiple_of(them * thin + f * packed, 8), packed)
                narrow[rows, :] = words[0:packed, f * columns : (f + 1) * columns]
        for k in range(count):

            @pl.when(at[1] == k)
            def _(k=k, lanes=lanes, piece=piece):
                a_out[:, lanes] = piece[k * mine : (k + 1) * mine]

        dtb_out[:, lanes] = piece[states : states + 1]
        skip_out[:, lanes] = piece[states + 1 : states + 2]
        mean_out[:, lanes] = piece[states + 2 : states + 3]
        spread_out[:, lanes] = piece[states + 3 : states + 4]
        conv_out[:, lanes] = piece[states + 4 : states + 4 + taps]
        bias_out[:, lanes] = piece[states + 4 + taps : states + 5 + taps]
        tail = piece[states + 5 + taps : states + 6 + taps + fold]
        rest = tail if rest is None else rest + tail
    turned = jnp.transpose(narrow[...])
    xproj_out[...] = turned[0 : xproj_out.shape[0]]
    dtproj_out[...] = turned[128 : 128 + dtproj_out.shape[0]]
    for f in range(fold):
        gain_out[:, f * width : (f + 1) * width] = rest[f : f + 1]
    live = rest[fold : fold + 1, 0:1]
    mean = mean_out[...] / live
    spread = spread_out[...] / live - mean * mean + 1e-06
    mean_out[...] = mean
    spread_out[...] = jnp.sqrt(spread)


def struct(*shape, dtype=F32):
    return jax.ShapeDtypeStruct(shape, dtype)


def whole(shape):
    return pl.BlockSpec(shape, lambda *unused: (0,) * len(shape))


LIMIT = pltpu.CompilerParams(vmem_limit_bytes=63 << 20)


def front(normed, halo, in_weight, conv_weight, conv_bias, xproj, width):
    rows, features = normed.shape
    channels = in_weight.shape[1] // 2

    def part(height):
        return pl.BlockSpec((height, width), lambda q: (0, q))

    return pl.pallas_call(
        front_kernel,
        grid=(channels // width,),
        in_specs=[
            whole(normed.shape), whole(halo.shape), part(features), part(conv_weight.shape[0]), part(1),
            part(xproj.shape[0]),
        ],
        out_specs=[part(rows), whole((rows, xproj.shape[0])), part(rows), part(8)],
        out_shape=[
            struct(rows, channels), struct(rows, xproj.shape[0]), struct(rows, channels, dtype=BF16),
            struct(8, channels, dtype=BF16),
        ],
        scratch_shapes=[pltpu.VMEM((rows + 8, width), F32), pltpu.VMEM((rows, width), BF16)],
        compiler_params=LIMIT,
        cost_estimate=cost(8),
        name="front",
    )(normed, halo, in_weight, conv_weight, conv_bias, xproj)


def local_ends(live, proj, dtproj, dt_bias, mixed, normed, in_weight, masked, out_weight, rate, width):
    rows, channels = mixed.shape
    features = normed.shape[1]
    states = rate.shape[0]
    rank = dtproj.shape[0]
    group = channels // width

    def part(height):
        return pl.BlockSpec((height, width), lambda q: (0, q))

    return pl.pallas_call(
        ends_kernel,
        grid=(channels // width,),
        in_specs=[
            pl.BlockSpec(memory_space=pltpu.SMEM), whole(proj.shape),
            part(rank), part(1), part(rows), whole(normed.shape),
            pl.BlockSpec((features, width), lambda q: (0, q + group)), whole(masked.shape),
            pl.BlockSpec((width, features), lambda q: (q, 0)), part(states),
        ],
        out_specs=[part(rows)] * 3 + [part(8), part(states), part(states), whole((2 * states, rows))]
        + [part(states + 8)] * (group - 1),
        out_shape=[struct(rows, channels)] * 3
        + [struct(8, channels), struct(states, channels), struct(states, channels), struct(2 * states, rows)]
        + [struct(states + 8, channels)] * (group - 1),
        scratch_shapes=[
            pltpu.VMEM((rows, 2 * states, 128), F32),
            pltpu.VMEM((rows, width), F32),
            pltpu.VMEM((rows, rank), BF16),
            pltpu.VMEM((rows, width), F32),
            pltpu.VMEM((rows, width), F32),
        ],
        compiler_params=LIMIT,
        cost_estimate=cost(40),
        name="ends",
    )(live, proj, dtproj, dt_bias, mixed, normed, in_weight, masked, out_weight, rate)


def full_scan(
    order, cols, proj, rate, step, mixed, gate, grad_gated, state_in, grad_in, skip, dtproj, earlier,
):
    rows, channels = step.shape
    states = rate.shape[0]
    rank = dtproj.shape[0]
    width = channels // lax.axis_size("state")
    blocks = order.shape[0]

    def part(height):
        return pl.BlockSpec((height, width), lambda q, order: (0, order[q]))

    tall = pl.BlockSpec((width, rank), lambda q, order: (order[q], 0))
    rows_f32 = part(rows)
    in_specs = [
        whole(cols.shape), whole(proj.shape), part(states), rows_f32, rows_f32, rows_f32, rows_f32,
        part(states), part(states), part(1), part(rank),
    ]
    out_specs = [
        part(rows), part(rows), part(rows), part(states), part(8), tall, whole((rows, rank)),
        whole((2 * states, rows)), whole((rows, 128)),
    ] + [whole((rows, 2 * width))] * blocks
    out_shape = [
        struct(rows, channels, dtype=BF16), struct(rows, channels, dtype=BF16),
        struct(rows, channels), struct(states, channels),
        struct(8, channels), struct(channels, rank), struct(rows, rank), struct(2 * states, rows),
        struct(rows, 128, dtype=BF16),
    ] + [struct(rows, 2 * width, dtype=BF16)] * blocks
    args = [
        order, cols, proj, rate, step, mixed, gate, grad_gated, state_in, grad_in, skip, dtproj,
    ]
    aliases = {}
    for out, value in earlier:
        aliases[len(args)] = out
        args.append(value)
        in_specs.append(pl.BlockSpec(memory_space=pl.ANY) if out < 6 else whole(value.shape))
    block = pltpu.VMEM((rows, width), F32)
    return pl.pallas_call(
        functools.partial(scan_kernel, len(earlier)),
        grid_spec=pltpu.PrefetchScalarGridSpec(
            num_scalar_prefetch=1,
            grid=(blocks,),
            in_specs=in_specs,
            out_specs=out_specs,
            scratch_shapes=[
                pltpu.VMEM((rows, 2 * states, 128), F32),
                pltpu.VMEM((rows + 1, states, width), F32),
                pltpu.VMEM((rows, states, 128), F32),
                pltpu.VMEM((rows, states, 128), F32),
                block, block, block, block,
                pltpu.VMEM((rows, width), BF16),
                pltpu.VMEM((rows, rank), BF16),
                block,
            ],
        ),
        out_shape=out_shape,
        input_output_aliases=aliases,
        compiler_params=LIMIT,
        cost_estimate=cost(50),
        name="scan",
    )(*args)


def back(
    order, proj_grad, xproj, mix_grad, inner, before, ahead, conv_weight, conv_bias, rate_sums, scan_sums,
    step_sums, dtproj_grad, earlier,
):
    rows, channels = mix_grad.shape
    blocks = order.shape[0] - 1
    seqs = lax.axis_size("seq")
    group = lax.axis_size("state")
    width = channels // group
    thin = width // seqs
    side = min(2, seqs // group)
    rank = dtproj_grad.shape[1]

    def part(height):
        return pl.BlockSpec((height, width), lambda q, order: (0, order[q]))

    def tall(columns):
        return pl.BlockSpec((width, columns), lambda q, order: (order[q], 0))

    in_specs = [
        whole(proj_grad.shape), part(xproj.shape[0]), part(rows), part(rows), part(8), part(8),
        part(conv_weight.shape[0]), part(1), part(rate_sums.shape[0]), part(8), part(8), tall(rank),
    ]
    args = [
        order, proj_grad, xproj, mix_grad, inner, before, ahead, conv_weight, conv_bias, rate_sums,
        scan_sums, step_sums, dtproj_grad,
    ]
    aliases = {}
    for out, value in earlier:
        aliases[len(args)] = out
        args.append(value)
        in_specs.append(pl.BlockSpec(memory_space=pl.ANY) if out == 0 else whole(value.shape))
    return pl.pallas_call(
        functools.partial(back_kernel, len(earlier)),
        grid_spec=pltpu.PrefetchScalarGridSpec(
            num_scalar_prefetch=1,
            grid=(blocks,),
            in_specs=in_specs,
            out_specs=[part(rows), whole((group, seqs + seqs // side, thin, 128))]
            + [whole((rows + 64, width))] * blocks,
            scratch_shapes=[
                pltpu.VMEM((rows + 8, width), F32),
                pltpu.VMEM((rows + 8, width), F32),
                pltpu.VMEM((rows, width), BF16),
                pltpu.VMEM((rows, width), F32),
            ],
        ),
        out_shape=[
            struct(rows, channels, dtype=BF16), struct(group, seqs + seqs // side, thin, 128, dtype=BF16),
        ] + [struct(rows + 64, width, dtype=BF16)] * blocks,
        input_output_aliases=aliases,
        compiler_params=LIMIT,
        cost_estimate=cost(18),
        name="back",
    )(*args)


def cost(micros):
    return pl.CostEstimate(flops=int(micros), transcendentals=0, bytes_accessed=1024)


def places():
    me = lax.axis_index("state")
    core = lax.axis_index("seq") % 2
    group = lax.axis_size("state")
    base = lax.axis_index("seq") * group // lax.axis_size("seq")
    order = [me ^ d for d in range(group)]
    return jnp.stack([core] + order + [base ^ k for k in order]).astype(jnp.int32)


def wide_grads(gates, masked, normed, seqs):
    count = len(gates)
    rows = gates[0].shape[0]
    width = gates[0].shape[1] // 2
    features = masked[0].shape[1]
    steps = max(1, width // WIDE_STEP)
    high = features // seqs
    chips = seqs // 2
    fixed = pl.BlockSpec((rows, width), lambda i, at: (0, 1))
    part = pl.BlockSpec((rows, width // steps), lambda i, at: (0, i))

    wholly = pl.BlockSpec((rows, features), lambda i, at: (0, 0))
    partly = pl.BlockSpec((rows, features // steps), lambda i, at: (0, i))
    return pl.pallas_call(
        functools.partial(wide_kernel, high),
        grid_spec=pltpu.PrefetchScalarGridSpec(
            num_scalar_prefetch=1,
            grid=(steps,),
            in_specs=[part] * count + [fixed] * count
            + [wholly] * count + [partly] * count,
            out_specs=[whole((chips * 2 * high, width))] * 2,
        ),
        out_shape=[struct(chips * 2 * high, width)] * 2,
        compiler_params=LIMIT,
        cost_estimate=cost(10),
        name="wide",
    )(places(), *gates, *gates, *masked, *normed)


def inner_grads(normed, inners, thins, gain, live, seqs, used):
    count = len(inners)
    width = inners[0].shape[1]
    rows, features = normed[0].shape
    steps = max(1, width // WIDE_STEP)
    chips = seqs // 2
    entry = features // seqs + thins[0].shape[1] * 256 // width

    partly = pl.BlockSpec((rows, features // steps), lambda i, at: (0, i))
    shape = (chips * entry + sum_rows(used, gain.shape[0]), width)
    return pl.pallas_call(
        functools.partial(inner_kernel, seqs, used),
        grid_spec=pltpu.PrefetchScalarGridSpec(
            num_scalar_prefetch=1,
            grid=(steps,),
            in_specs=[partly] * count
            + [whole(inners[0].shape)] * count + [whole(thins[0].shape)] * count
            + [whole(gain.shape), pl.BlockSpec(memory_space=pltpu.SMEM)],
            out_specs=[whole(shape)] * 2,
        ),
        out_shape=[struct(*shape)] * 2,
        compiler_params=LIMIT,
        cost_estimate=cost(5),
        name="inner",
    )(places(), *normed, *inners, *thins, gain, live)


def assemble(wides, lasts, features, channels, seqs, taps, states, proj_width, rank):
    width = wides[0].shape[1]
    count = len(wides)
    rows = channels // seqs
    shapes = [
        (features // seqs, 2 * channels), (rows, features), (proj_width, rows), (rank, rows), (taps, channels),
        (1, channels), (1, channels), (1, channels), (1, channels), (1, channels),
        (states // count, channels), (1, features),
    ]
    return pl.pallas_call(
        assemble_kernel,
        in_specs=[pl.BlockSpec(memory_space=pltpu.SMEM)] + [pl.BlockSpec(memory_space=pltpu.VMEM)] * 2 * count,
        out_specs=[pl.BlockSpec(memory_space=pltpu.VMEM)] * len(shapes),
        out_shape=[struct(*shape) for shape in shapes],
        scratch_shapes=[pltpu.VMEM((rows, 256), F32)],
        compiler_params=LIMIT,
        cost_estimate=cost(4),
        name="assemble",
    )(places(), *wides, *lasts)


def dot(a, b, dims):
    return lax.dot_general(a, b, (dims, ((), ())), preferred_element_type=F32)


def body(
    tokens,
    lengths,
    grad_out,
    norm_gain,
    in_weight,
    conv_weight,
    conv_bias,
    xproj_weight,
    dtproj_weight,
    dt_bias,
    a_log,
    d_skip,
    out_weight,
):
    rows, features = tokens.shape
    channels = out_weight.shape[0]
    rank = dtproj_weight.shape[1]
    proj_width = xproj_weight.shape[1]
    states = (proj_width - rank) // 2
    taps = conv_weight.shape[0]
    group = lax.axis_size("state")
    seqs = lax.axis_size("seq")
    member = lax.axis_index("state")
    width = channels // group
    live_rows = jnp.clip(lengths - member * rows, 0, rows)
    alive = (jnp.arange(rows, dtype=jnp.int32) < live_rows[0]).astype(F32)[:, None]
    conv_row = conv_bias[None]
    xproj = jnp.pad(xproj_weight.T, ((0, 128 - proj_width), (0, 0)))

    a_full = placed(gathered(a_log), 0)
    rate2 = -jnp.exp(a_full) * LOG2E
    cotangent = grad_out.astype(F32)
    masked_low = (cotangent * alive).astype(BF16)
    inputs = tokens.astype(F32)
    inv_scale = lax.rsqrt(jnp.mean(inputs * inputs, axis=1, keepdims=True) + EPSILON)
    normed = inputs * inv_scale
    normed_low = (normed * norm_gain).astype(BF16)
    halo = shifted(normed_low[rows - 8 :], "state", 1)
    mixed, proj, inner, before = front(normed_low, halo, in_weight, conv_weight, conv_row, xproj, width)

    near = [d for d in range(1, group) if d & (d - 1) == 0]
    normed_late, mixed = lax.optimization_barrier((normed_low, mixed))
    normed_near = [swapped(normed_late, d) for d in near]
    step, gate_in, grad_gated, stats, state_end, grad_end, cols, *offers = local_ends(
        jnp.stack([live_rows[0], member]), proj, dtproj_weight.T, dt_bias[None], mixed, normed_low, in_weight,
        masked_low, out_weight, rate2, width,
    )
    *normed_near, offers = lax.optimization_barrier((*normed_near, offers))
    normed_pieces = {0: normed_low, **dict(zip(near, normed_near))}

    pieces = [jnp.concatenate([state_end, stats], axis=0)]
    pieces += [swapped(offer, d + 1) for d, offer in enumerate(offers)]
    pieces = jnp.stack(pieces)
    state_in = jnp.zeros((states, channels), F32)
    grad_in = jnp.zeros((states, channels), F32)
    for k in range(group - 1):
        one = lax.dynamic_index_in_dim(pieces, member ^ k, 0, keepdims=False)
        passed = one[:states] + jnp.exp2(rate2 * one[states : states + 1]) * state_in
        state_in = jnp.where(k < member, passed, state_in)
    for k in range(group - 1, 0, -1):
        one = lax.dynamic_index_in_dim(pieces, member ^ k, 0, keepdims=False)
        passed = one[:states] + jnp.exp2(rate2 * one[states : states + 1]) * grad_in
        grad_in = jnp.where(k > member, passed, grad_in)

    masked_late, state_in = lax.optimization_barrier((masked_low, state_in))
    masked_pieces = gathered(masked_late)

    first = list(range(1, group // 2 + 1))
    second = list(range(group // 2 + 1, group)) + [0]
    call = (cols, proj, rate2, step, mixed, gate_in, grad_gated, state_in, grad_in)
    call += (d_skip[None], dtproj_weight.T)
    one = list(full_scan(jnp.stack([member ^ d for d in first]), *call, []))
    *masked_pieces, normed_late, one[0] = lax.optimization_barrier((*masked_pieces, normed_low, one[0]))
    normed_pieces.update({d: swapped(normed_late, d) for d in range(1, group) if d not in near})
    normed_pieces = [normed_pieces[d] for d in range(group)]
    gates = {d: swapped(one[9 + q], d) for q, d in enumerate(first)}
    shared = [(k, one[k]) for k in range(8)]
    two = full_scan(jnp.stack([member ^ d for d in second]), *call, shared)
    gated_low, grad_gate_low, mix_grad, grad_a, scan_sums, grad_dtproj = two[:6]
    first_gates = [gates[d] for d in first]
    normed_pieces, *first_gates, grad_proj = lax.optimization_barrier((normed_pieces, *first_gates, two[8]))
    gates.update(dict(zip(first, first_gates)))

    window = jnp.concatenate([before, inner[:8]], axis=0).astype(F32)
    head_pre = conv_window(window, conv_weight, conv_row, 8)
    head_squash = jax.nn.sigmoid(head_pre)
    head_mixed = mix_grad[:8] + jnp.dot(grad_proj[:8], xproj, preferred_element_type=F32)
    head_grad = head_mixed * head_squash * (1.0 + head_pre * (1.0 - head_squash))
    ahead = shifted(head_grad, "state", -1)
    late_sends = [two[9 + q] for q in range(len(second))]
    ahead, *late_sends = lax.optimization_barrier((ahead, *late_sends))
    gates.update({d: swapped(v, d) if d else v for d, v in zip(second, late_sends)})
    call = (grad_proj, xproj, mix_grad, inner, before, ahead, conv_weight, conv_row, grad_a, scan_sums, stats)
    call += (grad_dtproj,)
    one = back(jnp.stack([member ^ d for d in first] + [member]), *call, [])
    inner_pieces = {d: swapped(one[2 + q], d) for q, d in enumerate(first)}
    two = back(jnp.stack([member ^ d for d in second] + [member]), *call, [(0, one[0]), (1, one[1])])
    grad_inner_low, thin_sends = two[:2]
    inner_pieces.update({d: swapped(two[2 + q], d) if d else two[2 + q] for q, d in enumerate(second)})
    thin_pieces = [thin_sends[0]] + [swapped(thin_sends[d], d) for d in range(1, group)]
    arrived = [inner_pieces[d] for d in first]
    gates, arrived, thin_sends = lax.optimization_barrier((gates, arrived, thin_sends))
    inner_pieces.update(dict(zip(first, arrived)))
    inner_pieces = [inner_pieces[d] for d in range(group)]
    fold = features // width
    high = features // seqs
    thin = width // seqs
    thin_rows = thin * 256 // width
    used = states + 5 + taps

    wide = wide_grads([gates[d] for d in range(group)], masked_pieces, normed_pieces, seqs)
    wide, _, (inner_pieces, thin_pieces), (gated_late, grad_gate_low) = seq_scatter(
        *wide, hold=(inner_pieces, thin_pieces), late=(gated_low, grad_gate_low)
    )
    branch = jnp.dot(gated_late, out_weight, preferred_element_type=F32)
    output = (inputs + alive * branch).astype(BF16)
    wide = wide.astype(BF16)
    owned = to_owner(wide[:high])

    grad_normed = dot(grad_inner_low, in_weight[:, :channels], ((1,), (1,))) + dot(
        grad_gate_low, in_weight[:, channels:], ((1,), (1,))
    )
    gain_part = jnp.sum(grad_normed * normed, axis=0).reshape(fold, width)
    scaled = grad_normed * norm_gain
    grad_tokens = cotangent + inv_scale * (
        scaled - normed * jnp.mean(scaled * normed, axis=1, keepdims=True)
    )

    last = inner_grads(normed_pieces, inner_pieces, thin_pieces, gain_part, live_rows.astype(F32), seqs, used)
    last, sums, _, owned = seq_scatter(*last, extra=sum_rows(used, fold), late=owned)
    wide_pieces = gathered(jnp.concatenate([owned, wide[high:]], axis=0))
    *wide_pieces, last, sums = lax.optimization_barrier((*wide_pieces, last, sums))
    words = two_words(jnp.concatenate([last[high:], sums], axis=0))
    last = gathered(jnp.concatenate([last[:high].astype(BF16), words], axis=0))

    (
        grad_in_w, grad_out_w, grad_xproj, grad_dtproj, grad_conv, grad_bias, grad_dtb, grad_skip, dt_mean,
        dt_spread, grad_a_log, grad_gain,
    ) = assemble(
        wide_pieces, last, features, channels, seqs, taps, states, proj_width, rank
    )
    return (
        output,
        grad_tokens,
        grad_gain[0],
        grad_in_w,
        grad_conv,
        grad_bias[0],
        grad_xproj.T,
        grad_dtproj.T,
        grad_dtb[0],
        grad_a_log,
        grad_skip[0],
        grad_out_w,
        dt_mean[0],
        dt_spread[0],
    )


def solution(mesh):
    rows = P(("seq", "state"), None)
    return jax.shard_map(
        body,
        mesh=mesh,
        in_specs=(rows, P("seq"), rows) + (P(),) * 7 + (P("state", None), P(), P()),
        out_specs=(rows, rows, P(), P("seq", None), P(), P(), P("seq", None), P("seq", None), P())
        + (P("state", None), P(), P("seq", None), P(), P()),
        check_vma=False,
    )
```
